32 devices in a mesh: seq: 8 (over z, x), tp: 4 (over y, core).
Axes of the slice: x: 2, y: 2, z: 4, core: 2. Of those that a mesh axis runs over, the one named last changes fastest.
Arguments:
- hidden_in: bfloat16 [16, 2048], replicated, may hold values from -6 to 6
- lengths: int32 [16], replicated, may hold values from 1 to 511, 2431 in all
- positions: int32 [16], replicated, may hold values from 0 to 1023
- query_weight: bfloat16 [2, 2048, 2048], P(None, 'seq', 'tp'), may hold values from -0.125 to 0.125
- key_weight: bfloat16 [2, 2048, 512], P(None, 'seq', 'tp'), may hold values from -4 to 4
- value_weight: bfloat16 [2, 2048, 512], P(None, 'seq', 'tp'), may hold values from -0.125 to 0.125
- out_weight: bfloat16 [2, 2048, 2048], P(None, 'tp', 'seq'), may hold values from -0.125 to 0.125
- gate_weight: bfloat16 [2, 2048, 8192], P(None, 'seq', 'tp'), may hold values from -0.125 to 0.125
- up_weight: bfloat16 [2, 2048, 8192], P(None, 'seq', 'tp'), may hold values from -0.125 to 0.125
- down_weight: bfloat16 [2, 8192, 2048], P(None, 'tp', 'seq'), may hold values from -0.0625 to 0.0625
- key_cache: bfloat16 [2, 16, 512, 512], P(None, None, 'seq', 'tp'), may hold values from -80 to 80
- value_cache: bfloat16 [2, 16, 512, 512], P(None, None, 'seq', 'tp'), may hold values from -6 to 6
Outputs:
- hidden_out: bfloat16 [16, 2048], replicated
- key_out: bfloat16 [2, 16, 512, 512], P(None, None, 'seq', 'tp')
- value_out: bfloat16 [2, 16, 512, 512], P(None, None, 'seq', 'tp')
The draws below stay inside these ranges and needn't reach their ends.
Inputs may be any that keep to these rules, and one draw needn't show every extreme that they name: Request b has its cached rows at positions 0 .. lengths[b] - 1 and its new token goes to row lengths[b]; rows above are padding. The longest request has exactly 511 cached rows.
All inputs are finite; a program needn't handle non-finite values.
Results may differ from the reference program's by a relative error of at most 0.015.
Values may be sent and summed in bfloat16 or wider, within the bound.
No kernel may reach another device: no remote copies, remote signals or barrier semaphores. Data moves between devices by JAX's collectives and lax.ppermute only.
A program may use at most 64 MiB of HBM per device.

```python
import math
import jax
import jax.numpy as jnp
import numpy as np
from jax import lax

D = 2048
HEADS = 32
KV_HEADS = 8
HEAD_DIM = 64
FF = 8192
LAYERS = 2
REQS = 16
KV_WIDTH = 512
SEQ_LEN = 512


def draw_key_cache(key, part):
    shape_all = (LAYERS, REQS, SEQ_LEN, KV_HEADS * HEAD_DIM)
    base_key = jax.random.fold_in(key, 11)
    sign_key = jax.random.fold_in(key, 23)
    base_vals = 3.0 * jax.random.truncated_normal(base_key, -6.0, 6.0, shape_all, jnp.float32)
    signs = jax.random.rademacher(sign_key, (LAYERS, REQS, 1, KV_HEADS * HEAD_DIM), jnp.float32)
    offset = jnp.arange(SEQ_LEN) % (SEQ_LEN // 4)
    strength = jnp.where(offset == 0, 80.0, jnp.where(offset == 1, 77.5, 0.0)).astype(jnp.float32)
    marked = (strength > 0.0)[None, None, :, None]
    result = jnp.where(marked, signs * strength[None, None, :, None], base_vals)
    return result.astype(jnp.bfloat16)


def draw_hidden_in(key, part):
    gain_key = jax.random.fold_in(key, 31)
    value_key = jax.random.fold_in(key, 37)
    phase_one = jax.random.uniform(jax.random.fold_in(gain_key, 1), (), jnp.float32, 0.0, 2.0 * math.pi)
    phase_two = jax.random.uniform(jax.random.fold_in(gain_key, 2), (), jnp.float32, 0.0, 2.0 * math.pi)
    rough = jax.random.uniform(jax.random.fold_in(gain_key, 3), (D,), jnp.float32, -0.4, 0.4)
    place = jnp.arange(D, dtype=jnp.float32) / D
    log_gain = 1.2 * jnp.sin(2.0 * math.pi * place + phase_one) + 0.5 * jnp.sin(6.0 * math.pi * place + phase_two) + rough
    gains = jnp.exp(log_gain)
    base_vals = jax.random.truncated_normal(value_key, -6.0, 6.0, (REQS, D), jnp.float32)
    return jnp.clip(base_vals * gains[None, :], -6.0, 6.0).astype(jnp.bfloat16)


def draw_key_weight(key, part):
    shape_all = (LAYERS, D, KV_HEADS * HEAD_DIM)
    base_vals = jax.random.truncated_normal(jax.random.fold_in(key, 41), -6.0, 6.0, shape_all, jnp.float32) / math.sqrt(D)
    return base_vals.astype(jnp.bfloat16)


def touch_ends(array, key, least, high):
    shape = array.shape
    spot = [jax.random.randint(jax.random.fold_in(key, axis), (), 0, shape[axis]) for axis in range(len(shape))]
    array = array.at[tuple(spot)].set(least)
    longest = shape.index(max(shape))
    spot[longest] = (spot[longest] + 1) % shape[longest]
    return array.at[tuple(spot)].set(high)


def block_levels(rng, dims, cuts, smallest, largest):
    factor_of, own = 1.0, jax.random.fold_in(rng, 6)
    for dim, parts in cuts:
        draws = jnp.exp(jax.random.uniform(jax.random.fold_in(own, dim), (parts,), jnp.float32, smallest / len(cuts), largest / len(cuts)))
        factor_of = factor_of * jnp.repeat(draws, dims[dim] // parts).reshape([-1 if axis == dim else 1 for axis in range(len(dims))])
    return factor_of


def profile(count, total, reach, slope):
    loads = [(1 << 20) // math.isqrt(rank ** slope) + 1 for rank in range(2, count + 1)]
    surplus, holding = total - reach - (count - 1), [1] * (count - 1)
    while surplus > 0:
        movable = [i for i in range(count - 1) if holding[i] < reach]
        pool, remaining = sum([loads[i] for i in movable]), surplus
        for i in movable:
            extra = min(reach - holding[i], max(1, remaining * loads[i] // pool), surplus)
            holding[i] = holding[i] + extra
            surplus = surplus - extra
    return np.array([reach] + holding)


def uneven_parts(own_key, number_of, total, most, lean):
    if number_of == 2:
        one = jax.random.randint(own_key, (), max(1, total - most), min(most, total - 1) + 1)
        return jnp.stack([one, total - one])
    sizes = jnp.asarray(profile(number_of, total, most, lean), jnp.int32)
    pairs = (number_of - 1) // 2
    source_of, receiver = sizes[1:1 + 2 * pairs:2], sizes[2:2 + 2 * pairs:2]
    margin = jnp.minimum(source_of - 1, most - receiver)
    moved = jax.random.randint(jax.random.fold_in(own_key, 1), (pairs,), 0, 1 << 20) % (margin + 1)
    sizes = sizes.at[1:1 + 2 * pairs:2].set(source_of - moved).at[2:2 + 2 * pairs:2].set(receiver + moved)
    return sizes[jax.random.permutation(jax.random.fold_in(own_key, 2), number_of)]


def gaussian(rng, extent, deviation, limit, pieces=(), kind=jnp.bfloat16):
    factor_of = block_levels(rng, extent, pieces, -0.22, 0.18) if pieces else 1.0
    entries = jax.random.normal(rng, extent, jnp.float32) * deviation * factor_of
    return jnp.minimum(jnp.maximum(entries, -limit), limit).astype(kind)


def setup_inputs(seed: int = 0) -> dict:
    key_list = jax.random.split(jax.random.key(seed), 13)
    hidden_in = draw_hidden_in(jax.random.fold_in(key_list[12], 71), 0)
    lengths = uneven_parts(key_list[1], REQS, SEQ_LEN - 1 + (REQS - 1) * (SEQ_LEN // 4), SEQ_LEN - 1, 2).astype(jnp.int32)
    positions = touch_ends(jax.random.randint(key_list[2], (REQS,), 0, 2 * SEQ_LEN), jax.random.fold_in(key_list[2], 1), 0, (2 * SEQ_LEN) - 1).astype(jnp.int32)
    query_weight = gaussian(key_list[3], (LAYERS, D, D), D ** -0.5, 0.125, ((1, 8), (2, 4)))
    key_weight = draw_key_weight(jax.random.fold_in(key_list[12], 71), 0)
    value_weight = gaussian(key_list[5], (LAYERS, D, KV_WIDTH), D ** -0.5, 0.125, ((1, 8), (2, 4)))
    out_weight = gaussian(key_list[6], (LAYERS, D, D), D ** -0.5, 0.125, ((1, 4), (2, 8)))
    gate_weight = gaussian(key_list[7], (LAYERS, D, FF), D ** -0.5, 0.125, ((1, 8), (2, 4)))
    up_weight = gaussian(key_list[8], (LAYERS, D, FF), D ** -0.5, 0.125, ((1, 8), (2, 4)))
    down_weight = gaussian(key_list[9], (LAYERS, FF, D), FF ** -0.5, 0.0625, ((1, 4), (2, 8)))
    key_cache = draw_key_cache(jax.random.fold_in(key_list[12], 71), 0)
    value_cache = gaussian(key_list[11], (LAYERS, REQS, SEQ_LEN, KV_WIDTH), 1.0, 6.0, ((2, 8), (3, 4)))
    return dict(hidden_in=hidden_in, lengths=lengths, positions=positions, query_weight=query_weight, key_weight=key_weight, value_weight=value_weight, out_weight=out_weight, gate_weight=gate_weight, up_weight=up_weight, down_weight=down_weight, key_cache=key_cache, value_cache=value_cache)


eps_norm = 1e-05
neg_fill = -1e+30

def rms_norm(stream):
    as_float = stream.astype(jnp.float32)
    spread = lax.optimization_barrier(jnp.mean(as_float * as_float, axis=-1, keepdims=True))
    return (as_float * lax.rsqrt(spread + eps_norm)).astype(jnp.bfloat16)

def rotate(heads, positions):
    half_dim = heads.shape[-1] // 2
    inverse = 500000.0 ** (-(2.0 * jnp.arange(half_dim, dtype=jnp.float32)) / heads.shape[-1])
    angles = positions.astype(jnp.float32)[:, None] * inverse[None, :]
    cosine = jnp.cos(angles)[:, None, :]
    sine = jnp.sin(angles)[:, None, :]
    first_half = heads[..., :half_dim]
    second_half = heads[..., half_dim:]
    return jnp.concatenate([first_half * cosine - second_half * sine, second_half * cosine + first_half * sine], axis=-1)

def reference(hidden_in, lengths, positions, query_weight, key_weight, value_weight, out_weight, gate_weight, up_weight, down_weight, key_cache, value_cache):
    stream = hidden_in
    score_scale = 1.0 / math.sqrt(HEAD_DIM)
    repeat = HEADS // KV_HEADS
    slot_ids = jnp.arange(SEQ_LEN, dtype=jnp.int32)
    key_layers = []
    value_layers = []
    for layer_idx in range(LAYERS):
        normed = rms_norm(stream)
        query = jnp.dot(normed, query_weight[layer_idx], preferred_element_type=jnp.float32).reshape(REQS, HEADS, HEAD_DIM)
        key_new = jnp.dot(normed, key_weight[layer_idx], preferred_element_type=jnp.float32).reshape(REQS, KV_HEADS, HEAD_DIM)
        value_new = jnp.dot(normed, value_weight[layer_idx], preferred_element_type=jnp.float32).astype(jnp.bfloat16)
        query = rotate(query, positions).astype(jnp.bfloat16)
        key_new = rotate(key_new, positions).astype(jnp.bfloat16).reshape(REQS, KV_WIDTH)
        new_slot = (slot_ids[None, :] == lengths[:, None])[:, :, None]
        key_rows = jnp.where(new_slot, key_new[:, None, :], key_cache[layer_idx])
        value_rows = jnp.where(new_slot, value_new[:, None, :], value_cache[layer_idx])

        def attend(packed):
            query_one, key_one, value_one, length_one = packed
            query_grouped = query_one.reshape(KV_HEADS, repeat, HEAD_DIM).astype(jnp.float32)
            keys_grouped = key_one.reshape(SEQ_LEN, KV_HEADS, HEAD_DIM).astype(jnp.float32)
            scores = jnp.einsum('krd,skd->krs', query_grouped, keys_grouped) * score_scale
            live_mask = (slot_ids <= length_one)[None, None, :]
            scores = jnp.where(live_mask, scores, neg_fill)
            row_top = lax.optimization_barrier(jnp.max(scores, axis=2, keepdims=True))
            weights = jnp.where(live_mask, jnp.exp(scores - row_top), 0.0)
            totals = lax.optimization_barrier(jnp.sum(weights, axis=2))
            rounded = lax.optimization_barrier(weights.astype(jnp.bfloat16))
            weighted = jnp.einsum('krs,skd->krd', rounded.astype(jnp.float32), value_one.reshape(SEQ_LEN, KV_HEADS, HEAD_DIM).astype(jnp.float32))
            return (weighted / totals[:, :, None]).astype(jnp.bfloat16)
        attended = lax.map(attend, (query, key_rows, value_rows, lengths)).reshape(REQS, D)
        attn_proj = jnp.dot(attended, out_weight[layer_idx], preferred_element_type=jnp.float32)
        mid = (stream.astype(jnp.float32) + attn_proj).astype(jnp.bfloat16)
        normed_two = rms_norm(mid)
        gate_sum = jnp.dot(normed_two, gate_weight[layer_idx], preferred_element_type=jnp.float32)
        up_sum = jnp.dot(normed_two, up_weight[layer_idx], preferred_element_type=jnp.float32)
        hidden = (jax.nn.silu(gate_sum) * up_sum).astype(jnp.bfloat16)
        down_proj = jnp.dot(hidden, down_weight[layer_idx], preferred_element_type=jnp.float32)
        stream = (mid.astype(jnp.float32) + down_proj).astype(jnp.bfloat16)
        key_layers.append(key_rows)
        value_layers.append(value_rows)
    return (stream, jnp.stack(key_layers), jnp.stack(value_layers))
```

```python
import math

import jax
import jax.numpy as jnp
from jax import lax
from jax.sharding import PartitionSpec as P

HEAD_DIM = 64
LAYERS = 2
eps_norm = 1e-05
neg_fill = -1e30


def split_hi_lo(value, parts):
    out = []
    rest = value
    for _ in range(parts):
        head = lax.reduce_precision(rest, 8, 7)
        out.append(head.astype(jnp.bfloat16))
        rest = rest - head
    return out


def seq_swap(chunks):
    return lax.all_to_all(chunks, "seq", 0, 0)


def make_per_device(n_seq, n_tp):
    def tp_sum(part):
        total = part
        for k in range(1, n_tp):
            total = total + lax.ppermute(part, "tp", [(i, (i + k) % n_tp) for i in range(n_tp)])
        return total

    def per_device(
        hidden_in,
        lengths,
        positions,
        query_weight,
        key_weight,
        value_weight,
        out_weight,
        gate_weight,
        up_weight,
        down_weight,
        key_cache,
        value_cache,
    ):
        seq_index = lax.axis_index("seq")
        requests, width = hidden_in.shape
        col_count = out_weight.shape[2]
        col_start = seq_index * col_count
        block_len = key_cache.shape[2]
        kv_width = key_cache.shape[3]
        query_width = query_weight.shape[2]
        heads = query_width // HEAD_DIM
        kv_heads = kv_width // HEAD_DIM
        repeat = heads // kv_heads
        ff_here = gate_weight.shape[2]
        ff_own = ff_here // n_seq
        scale = 1.0 / math.sqrt(HEAD_DIM)
        slots = seq_index * block_len + jnp.arange(block_len, dtype=jnp.int32)
        new_slot = (slots[None, :] == lengths[:, None])[:, :, None]
        live = (slots[None, :] <= lengths[:, None])[:, None, None, :]

        half = HEAD_DIM // 2
        inverse = 500000.0 ** (-(2.0 * jnp.arange(half, dtype=jnp.float32)) / HEAD_DIM)
        angles = positions.astype(jnp.float32)[:, None] * inverse[None, :]
        cosine = jnp.cos(angles)[:, None, :]
        sine = jnp.sin(angles)[:, None, :]

        def rotate(x):
            a, b = x[..., :half], x[..., half:]
            return jnp.concatenate([a * cosine - b * sine, b * cosine + a * sine], axis=-1)

        def stats_of(x):
            f = x.astype(jnp.float32)
            return jnp.sum(f * f, axis=-1, keepdims=True)

        def pad_lanes(cols):
            joined = jnp.concatenate(cols, axis=-1)
            return jnp.pad(joined, ((0, 0), (0, -joined.shape[-1] % 128)))

        own = lax.dynamic_slice_in_dim(hidden_in, col_start, col_count, 1)
        key_layers = []
        value_layers = []
        for layer in range(LAYERS):
            part = jnp.concatenate(
                [
                    jnp.dot(own, w[layer], preferred_element_type=jnp.float32)
                    for w in (query_weight, key_weight, value_weight)
                ],
                axis=1,
            ).astype(jnp.bfloat16)
            packed = jnp.concatenate([part, pad_lanes(split_hi_lo(stats_of(own), 2))], axis=1)
            got = seq_swap(jnp.broadcast_to(packed[None], (n_seq,) + packed.shape))
            got = jnp.sum(got.astype(jnp.float32), axis=0)
            qkv = query_width + 2 * kv_width
            spread = (got[:, qkv : qkv + 1] + got[:, qkv + 1 : qkv + 2]) / width
            got = got[:, :qkv] * lax.rsqrt(spread + eps_norm)
            query = rotate(got[:, :query_width].reshape(requests, heads, HEAD_DIM))
            query = query.astype(jnp.bfloat16).reshape(requests, kv_heads, repeat, HEAD_DIM)
            key_new = rotate(
                got[:, query_width : query_width + kv_width].reshape(requests, kv_heads, HEAD_DIM)
            )
            key_new = key_new.astype(jnp.bfloat16).reshape(requests, kv_width)
            value_new = got[:, query_width + kv_width :].astype(jnp.bfloat16)
            key_rows = jnp.where(new_slot, key_new[:, None, :], key_cache[layer])
            value_rows = jnp.where(new_slot, value_new[:, None, :], value_cache[layer])
            key_layers.append(key_rows)
            value_layers.append(value_rows)
            key_heads = key_rows.reshape(requests, block_len, kv_heads, HEAD_DIM)
            value_heads = value_rows.reshape(requests, block_len, kv_heads, HEAD_DIM)
            scores = (
                jnp.einsum("bkrd,bskd->bkrs", query, key_heads, preferred_element_type=jnp.float32)
                * scale
            )
            scores = jnp.where(live, scores, neg_fill)
            top = jnp.max(scores, axis=3)
            weights = jnp.where(live, jnp.exp(scores - top[..., None]), 0.0)
            sums = jnp.sum(weights, axis=3)
            acc = jnp.einsum(
                "bkrs,bskd->bkrd",
                weights.astype(jnp.bfloat16),
                value_heads,
                preferred_element_type=jnp.float32,
            )
            packed = jnp.concatenate(
                [
                    acc.reshape(requests, query_width).astype(jnp.bfloat16),
                    pad_lanes(
                        split_hi_lo(top.reshape(requests, heads), 3)
                        + split_hi_lo(sums.reshape(requests, heads), 2)
                    ),
                ],
                axis=1,
            )
            got = seq_swap(jnp.broadcast_to(packed[None], (n_seq,) + packed.shape))
            got = got.astype(jnp.float32)
            acc = got[:, :, :query_width].reshape(n_seq, requests, heads, HEAD_DIM)
            side = got[:, :, query_width : query_width + 5 * heads].reshape(
                n_seq, requests, 5, heads
            )
            tops = side[:, :, 0] + side[:, :, 1] + side[:, :, 2]
            factor = jnp.exp(tops - jnp.max(tops, axis=0, keepdims=True))
            total = jnp.sum(factor * (side[:, :, 3] + side[:, :, 4]), axis=0)
            attended = jnp.sum(acc * factor[..., None], axis=0) / total[..., None]
            attended = attended.astype(jnp.bfloat16).reshape(requests, query_width)

            part = jnp.dot(attended, out_weight[layer], preferred_element_type=jnp.float32)
            mid = (own.astype(jnp.float32) + tp_sum(part)).astype(jnp.bfloat16)

            gate = jnp.dot(mid, gate_weight[layer], preferred_element_type=jnp.float32)
            up = jnp.dot(mid, up_weight[layer], preferred_element_type=jnp.float32)
            side = pad_lanes(split_hi_lo(stats_of(mid), 2))
            packed = jnp.concatenate(
                [
                    gate.astype(jnp.bfloat16).reshape(requests, n_seq, ff_own),
                    up.astype(jnp.bfloat16).reshape(requests, n_seq, ff_own),
                    jnp.broadcast_to(side[:, None], (requests, n_seq, side.shape[1])),
                ],
                axis=2,
            )
            got = seq_swap(packed.transpose(1, 0, 2))
            got = jnp.sum(got.astype(jnp.float32), axis=0)
            spread = (got[:, 2 * ff_own : 2 * ff_own + 1] + got[:, 2 * ff_own + 1 : 2 * ff_own + 2]) / width
            inv = lax.rsqrt(spread + eps_norm)
            hidden = jax.nn.silu(got[:, :ff_own] * inv) * (got[:, ff_own : 2 * ff_own] * inv)
            hidden = hidden.astype(jnp.bfloat16)
            hidden = seq_swap(jnp.broadcast_to(hidden[None], (n_seq,) + hidden.shape))
            hidden = hidden.transpose(1, 0, 2).reshape(requests, ff_here)
            part = jnp.dot(hidden, down_weight[layer], preferred_element_type=jnp.float32)
            own = (mid.astype(jnp.float32) + tp_sum(part)).astype(jnp.bfloat16)

        stream = seq_swap(jnp.broadcast_to(own[None], (n_seq,) + own.shape))
        stream = stream.transpose(1, 0, 2).reshape(requests, width)
        return (stream, jnp.stack(key_layers), jnp.stack(value_layers))

    return per_device


def solution(mesh):
    return jax.shard_map(
        make_per_device(mesh.shape["seq"], mesh.shape["tp"]),
        mesh=mesh,
        in_specs=(
            P(),
            P(),
            P(),
            P(None, "seq", "tp"),
            P(None, "seq", "tp"),
            P(None, "seq", "tp"),
            P(None, "tp", "seq"),
            P(None, "seq", "tp"),
            P(None, "seq", "tp"),
            P(None, "tp", "seq"),
            P(None, None, "seq", "tp"),
            P(None, None, "seq", "tp"),
        ),
        out_specs=(P(), P(None, None, "seq", "tp"), P(None, None, "seq", "tp")),
        check_vma=False,
    )
```

```python
import functools
import math

import jax
import jax.numpy as jnp
from jax import lax
from jax.experimental import pallas as pl
from jax.experimental.pallas import tpu as pltpu
from jax.sharding import PartitionSpec as P

HEAD_DIM = 64
LAYERS = 2
eps_norm = 1e-05
neg_fill = -1e30


def split_hi_lo(value, parts):
    out = []
    rest = value
    for _ in range(parts):
        head = lax.reduce_precision(rest, 8, 7)
        out.append(head.astype(jnp.bfloat16))
        rest = rest - head
    return out


def seq_swap(chunks):
    return lax.all_to_all(chunks, "seq", 0, 0)


def make_plain(n_seq, n_tp):
    def tp_sum(part):
        total = part
        for k in range(1, n_tp):
            total = total + lax.ppermute(part, "tp", [(i, (i + k) % n_tp) for i in range(n_tp)])
        return total

    def per_device(
        hidden_in,
        lengths,
        positions,
        query_weight,
        key_weight,
        value_weight,
        out_weight,
        gate_weight,
        up_weight,
        down_weight,
        key_cache,
        value_cache,
    ):
        seq_index = lax.axis_index("seq")
        requests, width = hidden_in.shape
        col_count = out_weight.shape[2]
        col_start = seq_index * col_count
        block_len = key_cache.shape[2]
        kv_width = key_cache.shape[3]
        query_width = query_weight.shape[2]
        heads = query_width // HEAD_DIM
        kv_heads = kv_width // HEAD_DIM
        repeat = heads // kv_heads
        ff_here = gate_weight.shape[2]
        ff_own = ff_here // n_seq
        scale = 1.0 / math.sqrt(HEAD_DIM)
        slots = seq_index * block_len + jnp.arange(block_len, dtype=jnp.int32)
        new_slot = (slots[None, :] == lengths[:, None])[:, :, None]
        live = (slots[None, :] <= lengths[:, None])[:, None, None, :]

        half = HEAD_DIM // 2
        inverse = 500000.0 ** (-(2.0 * jnp.arange(half, dtype=jnp.float32)) / HEAD_DIM)
        angles = positions.astype(jnp.float32)[:, None] * inverse[None, :]
        cosine = jnp.cos(angles)[:, None, :]
        sine = jnp.sin(angles)[:, None, :]

        def rotate(x):
            a, b = x[..., :half], x[..., half:]
            return jnp.concatenate([a * cosine - b * sine, b * cosine + a * sine], axis=-1)

        def stats_of(x):
            f = x.astype(jnp.float32)
            return jnp.sum(f * f, axis=-1, keepdims=True)

        def pad_lanes(cols):
            joined = jnp.concatenate(cols, axis=-1)
            return jnp.pad(joined, ((0, 0), (0, -joined.shape[-1] % 128)))

        own = lax.dynamic_slice_in_dim(hidden_in, col_start, col_count, 1)
        key_layers = []
        value_layers = []
        for layer in range(LAYERS):
            part = jnp.concatenate(
                [
                    jnp.dot(own, w[layer], preferred_element_type=jnp.float32)
                    for w in (query_weight, key_weight, value_weight)
                ],
                axis=1,
            ).astype(jnp.bfloat16)
            packed = jnp.concatenate([part, pad_lanes(split_hi_lo(stats_of(own), 2))], axis=1)
            got = seq_swap(jnp.broadcast_to(packed[None], (n_seq,) + packed.shape))
            got = jnp.sum(got.astype(jnp.float32), axis=0)
            qkv = query_width + 2 * kv_width
            spread = (got[:, qkv : qkv + 1] + got[:, qkv + 1 : qkv + 2]) / width
            got = got[:, :qkv] * lax.rsqrt(spread + eps_norm)
            query = rotate(got[:, :query_width].reshape(requests, heads, HEAD_DIM))
            query = query.astype(jnp.bfloat16).reshape(requests, kv_heads, repeat, HEAD_DIM)
            key_new = rotate(
                got[:, query_width : query_width + kv_width].reshape(requests, kv_heads, HEAD_DIM)
            )
            key_new = key_new.astype(jnp.bfloat16).reshape(requests, kv_width)
            value_new = got[:, query_width + kv_width :].astype(jnp.bfloat16)
            key_rows = jnp.where(new_slot, key_new[:, None, :], key_cache[layer])
            value_rows = jnp.where(new_slot, value_new[:, None, :], value_cache[layer])
            key_layers.append(key_rows)
            value_layers.append(value_rows)
            key_heads = key_rows.reshape(requests, block_len, kv_heads, HEAD_DIM)
            value_heads = value_rows.reshape(requests, block_len, kv_heads, HEAD_DIM)
            scores = (
                jnp.einsum("bkrd,bskd->bkrs", query, key_heads, preferred_element_type=jnp.float32)
                * scale
            )
            scores = jnp.where(live, scores, neg_fill)
            top = jnp.max(scores, axis=3)
            weights = jnp.where(live, jnp.exp(scores - top[..., None]), 0.0)
            sums = jnp.sum(weights, axis=3)
            acc = jnp.einsum(
                "bkrs,bskd->bkrd",
                weights.astype(jnp.bfloat16),
                value_heads,
                preferred_element_type=jnp.float32,
            )
            packed = jnp.concatenate(
                [
                    acc.reshape(requests, query_width).astype(jnp.bfloat16),
                    pad_lanes(
                        split_hi_lo(top.reshape(requests, heads), 3)
                        + split_hi_lo(sums.reshape(requests, heads), 2)
                    ),
                ],
                axis=1,
            )
            got = seq_swap(jnp.broadcast_to(packed[None], (n_seq,) + packed.shape))
            got = got.astype(jnp.float32)
            acc = got[:, :, :query_width].reshape(n_seq, requests, heads, HEAD_DIM)
            side = got[:, :, query_width : query_width + 5 * heads].reshape(
                n_seq, requests, 5, heads
            )
            tops = side[:, :, 0] + side[:, :, 1] + side[:, :, 2]
            factor = jnp.exp(tops - jnp.max(tops, axis=0, keepdims=True))
            total = jnp.sum(factor * (side[:, :, 3] + side[:, :, 4]), axis=0)
            attended = jnp.sum(acc * factor[..., None], axis=0) / total[..., None]
            attended = attended.astype(jnp.bfloat16).reshape(requests, query_width)

            part = jnp.dot(attended, out_weight[layer], preferred_element_type=jnp.float32)
            mid = (own.astype(jnp.float32) + tp_sum(part)).astype(jnp.bfloat16)

            gate = jnp.dot(mid, gate_weight[layer], preferred_element_type=jnp.float32)
            up = jnp.dot(mid, up_weight[layer], preferred_element_type=jnp.float32)
            side = pad_lanes(split_hi_lo(stats_of(mid), 2))
            packed = jnp.concatenate(
                [
                    gate.astype(jnp.bfloat16).reshape(requests, n_seq, ff_own),
                    up.astype(jnp.bfloat16).reshape(requests, n_seq, ff_own),
                    jnp.broadcast_to(side[:, None], (requests, n_seq, side.shape[1])),
                ],
                axis=2,
            )
            got = seq_swap(packed.transpose(1, 0, 2))
            got = jnp.sum(got.astype(jnp.float32), axis=0)
            spread = (got[:, 2 * ff_own : 2 * ff_own + 1] + got[:, 2 * ff_own + 1 : 2 * ff_own + 2]) / width
            inv = lax.rsqrt(spread + eps_norm)
            hidden = jax.nn.silu(got[:, :ff_own] * inv) * (got[:, ff_own : 2 * ff_own] * inv)
            hidden = hidden.astype(jnp.bfloat16)
            hidden = seq_swap(jnp.broadcast_to(hidden[None], (n_seq,) + hidden.shape))
            hidden = hidden.transpose(1, 0, 2).reshape(requests, ff_here)
            part = jnp.dot(hidden, down_weight[layer], preferred_element_type=jnp.float32)
            own = (mid.astype(jnp.float32) + tp_sum(part)).astype(jnp.bfloat16)

        stream = seq_swap(jnp.broadcast_to(own[None], (n_seq,) + own.shape))
        stream = stream.transpose(1, 0, 2).reshape(requests, width)
        return (stream, jnp.stack(key_layers), jnp.stack(value_layers))

    return per_device


LANES = 128
VMEM_ROOM = 8 << 20


def lane_ids(shape):
    return lax.broadcasted_iota(jnp.int32, shape, len(shape) - 1)


def as_hi_lo(value, lane):
    wide = jnp.broadcast_to(value, lane.shape)
    high = wide.astype(jnp.bfloat16).astype(jnp.float32)
    return jnp.where(lane == 0, high, jnp.where(lane == 1, wide - high, 0.0)).astype(jnp.bfloat16)


def square_sum(own):
    wide = own.astype(jnp.float32)
    return jnp.sum(wide * wide, axis=1, keepdims=True)


def dot32(a, b):
    return jnp.dot(a, b, preferred_element_type=jnp.float32)


def call(body, out_shape, *args, name):
    vmem = pl.BlockSpec(memory_space=pltpu.VMEM)
    single = not isinstance(out_shape, (tuple, list))
    return pl.pallas_call(
        body,
        out_shape=out_shape,
        in_specs=[vmem] * len(args),
        out_specs=vmem if single else [vmem] * len(out_shape),
        compiler_params=pltpu.CompilerParams(vmem_limit_bytes=VMEM_ROOM),
        name=name,
    )(*[pltpu.with_memory_space_constraint(a, pltpu.VMEM) for a in args])


def project_body(layer, own, wq_ref, wk_ref, wv_ref, out_ref):
    part = [dot32(own, w[layer]).astype(jnp.bfloat16) for w in (wq_ref, wk_ref, wv_ref)]
    lane = lane_ids((own.shape[0], LANES))
    part.append(as_hi_lo(square_sum(own), lane))
    for member in range(out_ref.shape[0]):
        at = 0
        for piece in part:
            out_ref[member, :, at : at + piece.shape[1]] = piece
            at += piece.shape[1]


def first_kernel(own_ref, wq_ref, wk_ref, wv_ref, out_ref):
    project_body(0, own_ref[...], wq_ref, wk_ref, wv_ref, out_ref)


def sum_parts(base_ref, part_refs):
    total = part_refs[0][...]
    for ref in part_refs[1:]:
        total = total + ref[...]
    return (base_ref[...].astype(jnp.float32) + total).astype(jnp.bfloat16)


def next_kernel(layer, n_parts, *refs):
    base_ref, parts = refs[0], refs[1 : 1 + n_parts]
    wq_ref, wk_ref, wv_ref, own_ref, out_ref = refs[1 + n_parts :]
    own = sum_parts(base_ref, parts)
    own_ref[...] = own
    project_body(layer, own, wq_ref, wk_ref, wv_ref, out_ref)


def last_kernel(n_parts, *refs):
    base_ref, parts, out_ref = refs[0], refs[1 : 1 + n_parts], refs[1 + n_parts]
    own = sum_parts(base_ref, parts)
    for member in range(out_ref.shape[0]):
        out_ref[member] = own


def attend_kernel(
    layer, width, heads, kv_heads, got_ref, cos_ref, sin_ref, first_ref, last_ref, fresh_ref,
    key_ref, value_ref, out_ref, key_new_ref, value_new_ref,
):
    members, requests, _ = got_ref.shape
    query_width = heads * HEAD_DIM
    repeat = heads // kv_heads
    block = key_ref.shape[2]

    def summed(at):
        total = got_ref[0, :, at : at + LANES].astype(jnp.float32)
        for member in range(1, members):
            total = total + got_ref[member, :, at : at + LANES].astype(jnp.float32)
        return total

    lane = lane_ids((requests, LANES))
    low = lane < HEAD_DIM
    side = summed(query_width + 2 * kv_heads * HEAD_DIM)
    spread = (side[:, 0:1] + side[:, 1:2]) * (1.0 / width)
    inv = lax.rsqrt(spread + eps_norm)
    cosine = cos_ref[...]
    sine = sin_ref[...]
    half = HEAD_DIM // 2

    def rotated(at):
        x = summed(at) * inv
        other = jnp.where(
            lane % HEAD_DIM < half, pltpu.roll(x, LANES - half, 1), pltpu.roll(x, half, 1)
        )
        return x * cosine + other * sine

    stacked = []
    for pair in range(heads // 2):
        x = rotated(pair * LANES)
        turned = pltpu.roll(x, HEAD_DIM, 1)
        if 2 * pair // repeat == 0:
            stacked += [jnp.where(low, x, 0.0), jnp.where(low, turned, 0.0)]
        else:
            stacked += [jnp.where(low, 0.0, turned), jnp.where(low, 0.0, x)]
    query = jnp.concatenate(stacked, axis=0).astype(jnp.bfloat16)
    key_new = rotated(query_width).astype(jnp.bfloat16)
    value_new = (summed(query_width + LANES) * inv).astype(jnp.bfloat16)
    key_new_ref[...] = key_new
    value_new_ref[...] = value_new

    fresh = fresh_ref[...] > 0
    keys = []
    values = []
    for b in range(requests):
        here = fresh[b * block : (b + 1) * block]
        k = key_ref[layer, b].astype(jnp.float32)
        v = value_ref[layer, b].astype(jnp.float32)
        keys.append(jnp.where(here, key_new[b : b + 1].astype(jnp.float32), k).astype(jnp.bfloat16))
        values.append(
            jnp.where(here, value_new[b : b + 1].astype(jnp.float32), v).astype(jnp.bfloat16)
        )
    keys = jnp.concatenate(keys, axis=0)
    values = jnp.concatenate(values, axis=0)
    scores = lax.dot_general(
        query, keys, (((1,), (1,)), ((), ())), preferred_element_type=jnp.float32
    ) * (1.0 / math.sqrt(HEAD_DIM))
    column = lane_ids(scores.shape)
    live = (column >= first_ref[...]) & (column < last_ref[...])
    scores = jnp.where(live, scores, neg_fill)
    top = jnp.max(scores, axis=1, keepdims=True)
    weights = jnp.where(live, jnp.exp(scores - top), 0.0)
    sums = jnp.sum(weights, axis=1, keepdims=True)
    acc = dot32(weights.astype(jnp.bfloat16), values)
    turned = pltpu.roll(acc, HEAD_DIM, 1)

    side = jnp.zeros((requests, LANES), jnp.float32)
    for h in range(heads):
        rows = slice(h * requests, (h + 1) * requests)
        for group in range(5):
            side = jnp.where(lane == group * heads + h, (top if group < 3 else sums)[rows], side)
    one = side.astype(jnp.bfloat16).astype(jnp.float32)
    two = (side - one).astype(jnp.bfloat16).astype(jnp.float32)
    three = side - one - two
    second = ((lane >= heads) & (lane < 2 * heads)) | (lane >= 4 * heads)
    third = (lane >= 2 * heads) & (lane < 3 * heads)
    side = jnp.where(third, three, jnp.where(second, two, one)).astype(jnp.bfloat16)
    pieces = []
    for pair in range(heads // 2):
        even = slice(2 * pair * requests, (2 * pair + 1) * requests)
        odd = slice((2 * pair + 1) * requests, (2 * pair + 2) * requests)
        if 2 * pair // repeat == 0:
            pieces.append(jnp.where(low, acc[even], turned[odd]).astype(jnp.bfloat16))
        else:
            pieces.append(jnp.where(low, turned[even], acc[odd]).astype(jnp.bfloat16))
    pieces.append(side)
    for member in range(members):
        for i, piece in enumerate(pieces):
            out_ref[member, :, i * LANES : (i + 1) * LANES] = piece


def combine_kernel(layer, heads, got_ref, w_ref, out_ref):
    members, requests, _ = got_ref.shape
    query_width = heads * HEAD_DIM
    low = lane_ids((requests, LANES)) < HEAD_DIM
    sides = [
        got_ref[m, :, query_width : query_width + LANES].astype(jnp.float32) for m in range(members)
    ]
    tops = [
        s[:, :heads] + s[:, heads : 2 * heads] + s[:, 2 * heads : 3 * heads] for s in sides
    ]
    sums = [s[:, 3 * heads : 4 * heads] + s[:, 4 * heads : 5 * heads] for s in sides]
    top = tops[0]
    for t in tops[1:]:
        top = jnp.maximum(top, t)
    factors = [jnp.exp(t - top) for t in tops]
    total = factors[0] * sums[0]
    for f, s in zip(factors[1:], sums[1:]):
        total = total + f * s

    def spread(column, pair):
        return jnp.where(low, column[:, 2 * pair : 2 * pair + 1], column[:, 2 * pair + 1 : 2 * pair + 2])

    attended = []
    for pair in range(heads // 2):
        acc = jnp.zeros((requests, LANES), jnp.float32)
        for m in range(members):
            piece = got_ref[m, :, pair * LANES : (pair + 1) * LANES].astype(jnp.float32)
            acc = acc + piece * spread(factors[m], pair)
        attended.append((acc / spread(total, pair)).astype(jnp.bfloat16))
    out_ref[...] = dot32(jnp.concatenate(attended, axis=1), w_ref[layer])


def widen_kernel(layer, n_parts, *refs):
    base_ref, parts = refs[0], refs[1 : 1 + n_parts]
    gate_ref, up_ref, mid_ref, out_ref = refs[1 + n_parts :]
    mid = sum_parts(base_ref, parts)
    mid_ref[...] = mid
    side = as_hi_lo(square_sum(mid), lane_ids((mid.shape[0], LANES)))
    members = out_ref.shape[0]
    own = gate_ref.shape[2] // members
    for member in range(members):
        cols = slice(member * own, (member + 1) * own)
        out_ref[member, :, :own] = dot32(mid, gate_ref[layer, :, cols]).astype(jnp.bfloat16)
        out_ref[member, :, own : 2 * own] = dot32(mid, up_ref[layer, :, cols]).astype(jnp.bfloat16)
        out_ref[member, :, 2 * own :] = side


def silu_kernel(width, got_ref, out_ref):
    members, _, span = got_ref.shape
    own = (span - LANES) // 2
    total = got_ref[0].astype(jnp.float32)
    for member in range(1, members):
        total = total + got_ref[member].astype(jnp.float32)
    spread = (total[:, 2 * own : 2 * own + 1] + total[:, 2 * own + 1 : 2 * own + 2]) * (1.0 / width)
    inv = lax.rsqrt(spread + eps_norm)
    gate = total[:, :own] * inv
    hidden = (gate / (1.0 + jnp.exp(-gate)) * (total[:, own : 2 * own] * inv)).astype(jnp.bfloat16)
    for member in range(members):
        out_ref[member] = hidden


def down_kernel(layer, got_ref, w_ref, out_ref):
    hidden = jnp.concatenate([got_ref[m] for m in range(got_ref.shape[0])], axis=1)
    out_ref[...] = dot32(hidden, w_ref[layer])


def make_with_kernels(n_seq, n_tp):
    def tp_parts(part):
        return [part] + [
            lax.ppermute(part, "tp", [(i, (i + k) % n_tp) for i in range(n_tp)])
            for k in range(1, n_tp)
        ]

    def per_device(
        hidden_in,
        lengths,
        positions,
        query_weight,
        key_weight,
        value_weight,
        out_weight,
        gate_weight,
        up_weight,
        down_weight,
        key_cache,
        value_cache,
    ):
        seq_index = lax.axis_index("seq")
        requests, width = hidden_in.shape
        col_count = out_weight.shape[2]
        block_len = key_cache.shape[2]
        kv_width = key_cache.shape[3]
        query_width = query_weight.shape[2]
        heads = query_width // HEAD_DIM
        kv_heads = kv_width // HEAD_DIM
        ff_own = gate_weight.shape[2] // n_seq
        bf16, f32 = jnp.bfloat16, jnp.float32

        def shape(dims, kind):
            return pltpu.VMEM(dims, kind)

        slots = seq_index * block_len + jnp.arange(block_len, dtype=jnp.int32)
        new_slot = slots[None, :] == lengths[:, None]
        fresh = new_slot.astype(jnp.int32).reshape(requests * block_len, 1)
        row_request = jnp.arange(heads * requests, dtype=jnp.int32) % requests
        first = row_request * block_len
        count = jnp.clip(lengths + 1 - seq_index * block_len, 0, block_len)
        last = first + jnp.tile(count, heads)
        half = HEAD_DIM // 2
        inverse = 500000.0 ** (-(2.0 * jnp.arange(half, dtype=jnp.float32)) / HEAD_DIM)
        angles = positions.astype(jnp.float32)[:, None] * inverse[None, :]
        cosine = jnp.cos(angles)
        sine = jnp.sin(angles)
        cosine = jnp.tile(cosine, (1, LANES // half))
        sine = jnp.tile(jnp.concatenate([-sine, sine], axis=1), (1, LANES // HEAD_DIM))

        own = lax.dynamic_slice_in_dim(hidden_in, seq_index * col_count, col_count, 1)
        packed_shape = shape((n_seq, requests, query_width + 2 * kv_width + LANES), bf16)
        part_shape = shape((requests, col_count), f32)
        own_shape = shape((requests, col_count), bf16)
        new_shape = shape((requests, kv_width), bf16)
        key_layers = []
        value_layers = []
        parts = None
        mid = None
        for layer in range(LAYERS):
            weights = (query_weight, key_weight, value_weight)
            if parts is None:
                packed = call(first_kernel, packed_shape, own, *weights, name="first")
            else:
                own, packed = call(
                    functools.partial(next_kernel, layer, n_tp),
                    (own_shape, packed_shape),
                    mid,
                    *parts,
                    *weights,
                    name="next",
                )
            packed, key_new, value_new = call(
                functools.partial(attend_kernel, layer, width, heads, kv_heads),
                (shape((n_seq, requests, query_width + LANES), bf16), new_shape, new_shape),
                seq_swap(packed),
                cosine,
                sine,
                first[:, None],
                last[:, None],
                fresh,
                key_cache,
                value_cache,
                name="attend",
            )
            key_layers.append(jnp.where(new_slot[:, :, None], key_new[:, None, :], key_cache[layer]))
            value_layers.append(
                jnp.where(new_slot[:, :, None], value_new[:, None, :], value_cache[layer])
            )
            part = call(
                functools.partial(combine_kernel, layer, heads),
                part_shape,
                seq_swap(packed),
                out_weight,
                name="combine",
            )
            mid, packed = call(
                functools.partial(widen_kernel, layer, n_tp),
                (own_shape, shape((n_seq, requests, 2 * ff_own + LANES), bf16)),
                own,
                *tp_parts(part),
                gate_weight,
                up_weight,
                name="widen",
            )
            hidden = call(
                functools.partial(silu_kernel, width),
                shape((n_seq, requests, ff_own), bf16),
                seq_swap(packed),
                name="silu",
            )
            part = call(
                functools.partial(down_kernel, layer),
                part_shape,
                seq_swap(hidden),
                down_weight,
                name="down",
            )
            parts = tp_parts(part)
        stream = call(
            functools.partial(last_kernel, n_tp),
            shape((n_seq, requests, col_count), bf16),
            mid,
            *parts,
            name="last",
        )
        stream = seq_swap(stream).transpose(1, 0, 2).reshape(requests, width)
        return (stream, jnp.stack(key_layers), jnp.stack(value_layers))

    return per_device


def solution(mesh):
    n_seq, n_tp = mesh.shape["seq"], mesh.shape["tp"]

    def per_device(*args):
        gate_weight, key_cache = args[7], args[10]
        aligned = (
            args[6].shape[2] % LANES == 0
            and gate_weight.shape[2] // n_seq % LANES == 0
            and key_cache.shape[3] == LANES
        )
        make = make_with_kernels if aligned else make_plain
        return make(n_seq, n_tp)(*args)

    return jax.shard_map(
        per_device,
        mesh=mesh,
        in_specs=(
            P(),
            P(),
            P(),
            P(None, "seq", "tp"),
            P(None, "seq", "tp"),
            P(None, "seq", "tp"),
            P(None, "tp", "seq"),
            P(None, "seq", "tp"),
            P(None, "seq", "tp"),
            P(None, "tp", "seq"),
            P(None, None, "seq", "tp"),
            P(None, None, "seq", "tp"),
        ),
        out_specs=(P(), P(None, None, "seq", "tp"), P(None, None, "seq", "tp")),
        check_vma=False,
    )
```

```python
import functools
import math

import jax
import jax.numpy as jnp
from jax import lax
from jax.experimental import pallas as pl
from jax.experimental.pallas import tpu as pltpu
from jax.sharding import PartitionSpec as P

HEAD_DIM = 64
LAYERS = 2
eps_norm = 1e-05
neg_fill = -1e30


def split_hi_lo(value, parts):
    out = []
    rest = value
    for _ in range(parts):
        head = lax.reduce_precision(rest, 8, 7)
        out.append(head.astype(jnp.bfloat16))
        rest = rest - head
    return out


def seq_swap(chunks):
    return lax.all_to_all(chunks, "seq", 0, 0)


def make_plain(n_seq, n_tp):
    def tp_sum(part):
        total = part
        for k in range(1, n_tp):
            total = total + lax.ppermute(part, "tp", [(i, (i + k) % n_tp) for i in range(n_tp)])
        return total

    def per_device(
        hidden_in,
        lengths,
        positions,
        query_weight,
        key_weight,
        value_weight,
        out_weight,
        gate_weight,
        up_weight,
        down_weight,
        key_cache,
        value_cache,
    ):
        seq_index = lax.axis_index("seq")
        requests, width = hidden_in.shape
        col_count = out_weight.shape[2]
        col_start = seq_index * col_count
        block_len = key_cache.shape[2]
        kv_width = key_cache.shape[3]
        query_width = query_weight.shape[2]
        heads = query_width // HEAD_DIM
        kv_heads = kv_width // HEAD_DIM
        repeat = heads // kv_heads
        ff_here = gate_weight.shape[2]
        ff_own = ff_here // n_seq
        scale = 1.0 / math.sqrt(HEAD_DIM)
        slots = seq_index * block_len + jnp.arange(block_len, dtype=jnp.int32)
        new_slot = (slots[None, :] == lengths[:, None])[:, :, None]
        live = (slots[None, :] <= lengths[:, None])[:, None, None, :]

        half = HEAD_DIM // 2
        inverse = 500000.0 ** (-(2.0 * jnp.arange(half, dtype=jnp.float32)) / HEAD_DIM)
        angles = positions.astype(jnp.float32)[:, None] * inverse[None, :]
        cosine = jnp.cos(angles)[:, None, :]
        sine = jnp.sin(angles)[:, None, :]

        def rotate(x):
            a, b = x[..., :half], x[..., half:]
            return jnp.concatenate([a * cosine - b * sine, b * cosine + a * sine], axis=-1)

        def stats_of(x):
            f = x.astype(jnp.float32)
            return jnp.sum(f * f, axis=-1, keepdims=True)

        def pad_lanes(cols):
            joined = jnp.concatenate(cols, axis=-1)
            return jnp.pad(joined, ((0, 0), (0, -joined.shape[-1] % 128)))

        own = lax.dynamic_slice_in_dim(hidden_in, col_start, col_count, 1)
        key_layers = []
        value_layers = []
        for layer in range(LAYERS):
            part = jnp.concatenate(
                [
                    jnp.dot(own, w[layer], preferred_element_type=jnp.float32)
                    for w in (query_weight, key_weight, value_weight)
                ],
                axis=1,
            ).astype(jnp.bfloat16)
            packed = jnp.concatenate([part, pad_lanes(split_hi_lo(stats_of(own), 2))], axis=1)
            got = seq_swap(jnp.broadcast_to(packed[None], (n_seq,) + packed.shape))
            got = jnp.sum(got.astype(jnp.float32), axis=0)
            qkv = query_width + 2 * kv_width
            spread = (got[:, qkv : qkv + 1] + got[:, qkv + 1 : qkv + 2]) / width
            got = got[:, :qkv] * lax.rsqrt(spread + eps_norm)
            query = rotate(got[:, :query_width].reshape(requests, heads, HEAD_DIM))
            query = query.astype(jnp.bfloat16).reshape(requests, kv_heads, repeat, HEAD_DIM)
            key_new = rotate(
                got[:, query_width : query_width + kv_width].reshape(requests, kv_heads, HEAD_DIM)
            )
            key_new = key_new.astype(jnp.bfloat16).reshape(requests, kv_width)
            value_new = got[:, query_width + kv_width :].astype(jnp.bfloat16)
            key_rows = jnp.where(new_slot, key_new[:, None, :], key_cache[layer])
            value_rows = jnp.where(new_slot, value_new[:, None, :], value_cache[layer])
            key_layers.append(key_rows)
            value_layers.append(value_rows)
            key_heads = key_rows.reshape(requests, block_len, kv_heads, HEAD_DIM)
            value_heads = value_rows.reshape(requests, block_len, kv_heads, HEAD_DIM)
            scores = (
                jnp.einsum("bkrd,bskd->bkrs", query, key_heads, preferred_element_type=jnp.float32)
                * scale
            )
            scores = jnp.where(live, scores, neg_fill)
            top = jnp.max(scores, axis=3)
            weights = jnp.where(live, jnp.exp(scores - top[..., None]), 0.0)
            sums = jnp.sum(weights, axis=3)
            acc = jnp.einsum(
                "bkrs,bskd->bkrd",
                weights.astype(jnp.bfloat16),
                value_heads,
                preferred_element_type=jnp.float32,
            )
            packed = jnp.concatenate(
                [
                    acc.reshape(requests, query_width).astype(jnp.bfloat16),
                    pad_lanes(
                        split_hi_lo(top.reshape(requests, heads), 3)
                        + split_hi_lo(sums.reshape(requests, heads), 2)
                    ),
                ],
                axis=1,
            )
            got = seq_swap(jnp.broadcast_to(packed[None], (n_seq,) + packed.shape))
            got = got.astype(jnp.float32)
            acc = got[:, :, :query_width].reshape(n_seq, requests, heads, HEAD_DIM)
            side = got[:, :, query_width : query_width + 5 * heads].reshape(
                n_seq, requests, 5, heads
            )
            tops = side[:, :, 0] + side[:, :, 1] + side[:, :, 2]
            factor = jnp.exp(tops - jnp.max(tops, axis=0, keepdims=True))
            total = jnp.sum(factor * (side[:, :, 3] + side[:, :, 4]), axis=0)
            attended = jnp.sum(acc * factor[..., None], axis=0) / total[..., None]
            attended = attended.astype(jnp.bfloat16).reshape(requests, query_width)

            part = jnp.dot(attended, out_weight[layer], preferred_element_type=jnp.float32)
            mid = (own.astype(jnp.float32) + tp_sum(part)).astype(jnp.bfloat16)

            gate = jnp.dot(mid, gate_weight[layer], preferred_element_type=jnp.float32)
            up = jnp.dot(mid, up_weight[layer], preferred_element_type=jnp.float32)
            side = pad_lanes(split_hi_lo(stats_of(mid), 2))
            packed = jnp.concatenate(
                [
                    gate.astype(jnp.bfloat16).reshape(requests, n_seq, ff_own),
                    up.astype(jnp.bfloat16).reshape(requests, n_seq, ff_own),
                    jnp.broadcast_to(side[:, None], (requests, n_seq, side.shape[1])),
                ],
                axis=2,
            )
            got = seq_swap(packed.transpose(1, 0, 2))
            got = jnp.sum(got.astype(jnp.float32), axis=0)
            spread = (got[:, 2 * ff_own : 2 * ff_own + 1] + got[:, 2 * ff_own + 1 : 2 * ff_own + 2]) / width
            inv = lax.rsqrt(spread + eps_norm)
            hidden = jax.nn.silu(got[:, :ff_own] * inv) * (got[:, ff_own : 2 * ff_own] * inv)
            hidden = hidden.astype(jnp.bfloat16)
            hidden = seq_swap(jnp.broadcast_to(hidden[None], (n_seq,) + hidden.shape))
            hidden = hidden.transpose(1, 0, 2).reshape(requests, ff_here)
            part = jnp.dot(hidden, down_weight[layer], preferred_element_type=jnp.float32)
            own = (mid.astype(jnp.float32) + tp_sum(part)).astype(jnp.bfloat16)

        stream = seq_swap(jnp.broadcast_to(own[None], (n_seq,) + own.shape))
        stream = stream.transpose(1, 0, 2).reshape(requests, width)
        return (stream, jnp.stack(key_layers), jnp.stack(value_layers))

    return per_device


LANES = 128
VMEM_ROOM = 8 << 20


def lane_ids(shape):
    return lax.broadcasted_iota(jnp.int32, shape, len(shape) - 1)


def as_hi_lo(value, lane):
    wide = jnp.broadcast_to(value, lane.shape)
    high = wide.astype(jnp.bfloat16).astype(jnp.float32)
    return jnp.where(lane == 0, high, jnp.where(lane == 1, wide - high, 0.0)).astype(jnp.bfloat16)


def square_sum(own):
    wide = own.astype(jnp.float32)
    return jnp.sum(wide * wide, axis=1, keepdims=True)


def dot32(a, b):
    return jnp.dot(a, b, preferred_element_type=jnp.float32)


def call(body, out_shape, *args, name, held=True, scratch=(), out_specs=None):
    vmem = pl.BlockSpec(memory_space=pltpu.VMEM)
    where = vmem if held else pl.BlockSpec(memory_space=pltpu.HBM)
    single = not isinstance(out_shape, (tuple, list))
    args = [pltpu.with_memory_space_constraint(a, pltpu.VMEM if held else pltpu.HBM) for a in args]
    return pl.pallas_call(
        body,
        out_shape=out_shape,
        in_specs=[where] * len(args),
        out_specs=out_specs or (vmem if single else [vmem] * len(out_shape)),
        scratch_shapes=list(scratch),
        compiler_params=pltpu.CompilerParams(vmem_limit_bytes=VMEM_ROOM),
        name=name,
    )(*args)


def project_body(own, weights, out_ref):
    part = [dot32(own, w).astype(jnp.bfloat16) for w in weights]
    lane = lane_ids((own.shape[0], LANES))
    part.append(as_hi_lo(square_sum(own), lane))
    for member in range(out_ref.shape[0]):
        at = 0
        for piece in part:
            out_ref[member, :, at : at + piece.shape[1]] = piece
            at += piece.shape[1]


def first_kernel(n_more, *refs):
    hidden_ref, length_ref, position_ref, wq_ref, wk_ref, wv_ref = refs[:6]
    more = refs[6 : 6 + n_more]
    own_ref, cos_ref, sin_ref, table_ref, out_ref = refs[6 + n_more : 11 + n_more]
    more_here = refs[11 + n_more : 11 + 2 * n_more]
    wq_here, wk_here, wv_here, lengths, positions, sems = refs[11 + 2 * n_more :]
    span = own_ref.shape[1]
    start = pl.multiple_of(lax.axis_index("seq") * span, LANES)
    copies = [
        pltpu.make_async_copy(position_ref, positions, sems.at[0]),
        pltpu.make_async_copy(length_ref, lengths, sems.at[1]),
        pltpu.make_async_copy(hidden_ref.at[:, pl.ds(start, span)], own_ref, sems.at[2]),
        pltpu.make_async_copy(wq_ref.at[0], wq_here, sems.at[3]),
        pltpu.make_async_copy(wk_ref.at[0], wk_here, sems.at[4]),
        pltpu.make_async_copy(wv_ref.at[0], wv_here, sems.at[5]),
    ]
    copies += [
        pltpu.make_async_copy(ref.at[0], here.at[0], sems.at[6 + i])
        for i, (ref, here) in enumerate(zip(more, more_here))
    ]
    for copy in copies:
        copy.start()
    copies[0].wait()
    copies[1].wait()
    half = HEAD_DIM // 2
    lane = lane_ids(table_ref.shape)
    row = lax.broadcasted_iota(jnp.int32, table_ref.shape, 0)
    place = jnp.zeros(table_ref.shape, jnp.int32)
    length = jnp.zeros(table_ref.shape, jnp.int32)
    for b in range(table_ref.shape[0]):
        place = jnp.where(row == b, positions[b], place)
        length = jnp.where(row == b, lengths[b], length)
    inverse = jnp.zeros(table_ref.shape, jnp.float32)
    for i in range(half):
        inverse = jnp.where(lane % half == i, 500000.0 ** (-2.0 * i / HEAD_DIM), inverse)
    angles = place.astype(jnp.float32) * inverse
    sine = jnp.sin(angles)
    table_ref[...] = length
    cos_ref[...] = jnp.cos(angles)
    sin_ref[...] = jnp.where(lane % HEAD_DIM < half, -sine, sine)
    for copy in copies[2:6]:
        copy.wait()
    project_body(own_ref[...], [wq_here[...], wk_here[...], wv_here[...]], out_ref)
    for copy in copies[6:]:
        copy.wait()


def store_kernel(keep_ref, length_ref, key_ref, value_ref, *refs):
    layers, requests, block, _ = key_ref.shape
    fresh_rows = refs[: 2 * layers]
    key_out, value_out, token_ref, key_here, value_here, sems = refs[2 * layers :]
    token_ref[...] = jnp.zeros_like(token_ref)
    fresh = length_ref[...] - lax.axis_index("seq") * block
    slot = lax.broadcasted_iota(jnp.int32, (block, LANES), 0)
    copies = []
    for layer in range(layers):
        for i, (old, here, out) in enumerate(
            [(key_ref, key_here, key_out), (value_ref, value_here, value_out)]
        ):
            new = fresh_rows[2 * layer + i][...].astype(jnp.float32)
            for b in range(requests):
                row = jnp.where(
                    slot == fresh[b : b + 1], new[b : b + 1], old[layer, b].astype(jnp.float32)
                )
                here[layer, b] = row.astype(jnp.bfloat16)
            copies.append(
                pltpu.make_async_copy(here.at[layer], out.at[layer], sems.at[2 * layer + i])
            )
            copies[-1].start()
    for copy in copies:
        copy.wait()


def sum_parts(base_ref, part_refs):
    total = part_refs[0][...]
    for ref in part_refs[1:]:
        total = total + ref[...]
    return (base_ref[...].astype(jnp.float32) + total).astype(jnp.bfloat16)


def next_kernel(layer, n_parts, *refs):
    base_ref, parts = refs[0], refs[1 : 1 + n_parts]
    wq_ref, wk_ref, wv_ref, own_ref, out_ref = refs[1 + n_parts :]
    own = sum_parts(base_ref, parts)
    own_ref[...] = own
    project_body(own, [w[layer] for w in (wq_ref, wk_ref, wv_ref)], out_ref)


def half_of(value, core):
    middle = value.shape[1] // 2
    return jnp.where(core == 0, value[:, :middle], value[:, middle:])


def meet_kernel(n_tp, mid_ref, keep_ref, got_ref, token_ref, out_ref):
    place = lax.axis_index("tp")
    total = keep_ref[...] + got_ref[...]
    base = half_of(mid_ref[...].astype(jnp.float32), place % 2)
    total = (total + jnp.where(place < 2, base, 0.0)).astype(jnp.bfloat16)
    for member in range(out_ref.shape[0]):
        out_ref[member] = total


def last_kernel(n_tp, got_ref, out_ref):
    span = got_ref.shape[2]
    for block in range(got_ref.shape[0] // n_tp):
        for core in range(2):
            total = got_ref[block * n_tp + core].astype(jnp.float32)
            for pair in range(1, n_tp // 2):
                total = total + got_ref[block * n_tp + 2 * pair + core].astype(jnp.float32)
            at = (2 * block + core) * span
            out_ref[:, at : at + span] = total.astype(jnp.bfloat16)


def attend_kernel(
    layer, width, heads, kv_heads, got_ref, cos_ref, sin_ref, length_ref,
    key_ref, value_ref, out_ref, key_new_ref, value_new_ref,
):
    members, requests, _ = got_ref.shape
    query_width = heads * HEAD_DIM
    repeat = heads // kv_heads
    block = key_ref.shape[2]

    def summed(at):
        total = got_ref[0, :, at : at + LANES].astype(jnp.float32)
        for member in range(1, members):
            total = total + got_ref[member, :, at : at + LANES].astype(jnp.float32)
        return total

    lane = lane_ids((requests, LANES))
    low = lane < HEAD_DIM
    side = summed(query_width + 2 * kv_heads * HEAD_DIM)
    spread = (side[:, 0:1] + side[:, 1:2]) * (1.0 / width)
    inv = lax.rsqrt(spread + eps_norm)
    cosine = cos_ref[...]
    sine = sin_ref[...]
    half = HEAD_DIM // 2

    def rotated(at):
        x = summed(at) * inv
        other = jnp.where(
            lane % HEAD_DIM < half, pltpu.roll(x, LANES - half, 1), pltpu.roll(x, half, 1)
        )
        return x * cosine + other * sine

    stacked = []
    for pair in range(heads // 2):
        x = rotated(pair * LANES)
        turned = pltpu.roll(x, HEAD_DIM, 1)
        if 2 * pair // repeat == 0:
            stacked += [jnp.where(low, x, 0.0), jnp.where(low, turned, 0.0)]
        else:
            stacked += [jnp.where(low, 0.0, turned), jnp.where(low, 0.0, x)]
    query = jnp.concatenate(stacked, axis=0).astype(jnp.bfloat16)
    key_new = rotated(query_width).astype(jnp.bfloat16)
    value_new = (summed(query_width + LANES) * inv).astype(jnp.bfloat16)
    key_new_ref[...] = key_new
    value_new_ref[...] = value_new

    fresh = length_ref[...] - lax.axis_index("seq") * block
    slot = lax.broadcasted_iota(jnp.int32, (block, LANES), 0)
    keys = []
    values = []
    for b in range(requests):
        here = slot == fresh[b : b + 1]
        k = key_ref[layer, b].astype(jnp.float32)
        v = value_ref[layer, b].astype(jnp.float32)
        keys.append(jnp.where(here, key_new[b : b + 1].astype(jnp.float32), k).astype(jnp.bfloat16))
        values.append(
            jnp.where(here, value_new[b : b + 1].astype(jnp.float32), v).astype(jnp.bfloat16)
        )
    keys = jnp.concatenate(keys, axis=0)
    values = jnp.concatenate(values, axis=0)
    scores = lax.dot_general(
        query, keys, (((1,), (1,)), ((), ())), preferred_element_type=jnp.float32
    ) * (1.0 / math.sqrt(HEAD_DIM))
    begin = lax.broadcasted_iota(jnp.int32, (requests, LANES), 0) * block
    end = begin + jnp.clip(fresh + 1, 0, block)
    copies = scores.shape[1] // LANES
    begin = jnp.concatenate([jnp.concatenate([begin] * heads, axis=0)] * copies, axis=1)
    end = jnp.concatenate([jnp.concatenate([end] * heads, axis=0)] * copies, axis=1)
    column = lane_ids(scores.shape)
    live = (column >= begin) & (column < end)
    scores = jnp.where(live, scores, neg_fill)
    top = jnp.max(scores, axis=1, keepdims=True)
    weights = jnp.where(live, jnp.exp(scores - top), 0.0)
    sums = jnp.sum(weights, axis=1, keepdims=True)
    acc = dot32(weights.astype(jnp.bfloat16), values)
    turned = pltpu.roll(acc, HEAD_DIM, 1)

    side = jnp.zeros((requests, LANES), jnp.float32)
    for h in range(heads):
        rows = slice(h * requests, (h + 1) * requests)
        for group in range(5):
            side = jnp.where(lane == group * heads + h, (top if group < 3 else sums)[rows], side)
    one = side.astype(jnp.bfloat16).astype(jnp.float32)
    two = (side - one).astype(jnp.bfloat16).astype(jnp.float32)
    three = side - one - two
    second = ((lane >= heads) & (lane < 2 * heads)) | (lane >= 4 * heads)
    third = (lane >= 2 * heads) & (lane < 3 * heads)
    side = jnp.where(third, three, jnp.where(second, two, one)).astype(jnp.bfloat16)
    pieces = []
    for pair in range(heads // 2):
        even = slice(2 * pair * requests, (2 * pair + 1) * requests)
        odd = slice((2 * pair + 1) * requests, (2 * pair + 2) * requests)
        if 2 * pair // repeat == 0:
            pieces.append(jnp.where(low, acc[even], turned[odd]).astype(jnp.bfloat16))
        else:
            pieces.append(jnp.where(low, turned[even], acc[odd]).astype(jnp.bfloat16))
    pieces.append(side)
    for member in range(members):
        for i, piece in enumerate(pieces):
            out_ref[member, :, i * LANES : (i + 1) * LANES] = piece


def combine_kernel(layer, heads, got_ref, w_ref, out_ref):
    members, requests, _ = got_ref.shape
    query_width = heads * HEAD_DIM
    low = lane_ids((requests, LANES)) < HEAD_DIM
    sides = [
        got_ref[m, :, query_width : query_width + LANES].astype(jnp.float32) for m in range(members)
    ]
    tops = [
        s[:, :heads] + s[:, heads : 2 * heads] + s[:, 2 * heads : 3 * heads] for s in sides
    ]
    sums = [s[:, 3 * heads : 4 * heads] + s[:, 4 * heads : 5 * heads] for s in sides]
    top = tops[0]
    for t in tops[1:]:
        top = jnp.maximum(top, t)
    factors = [jnp.exp(t - top) for t in tops]
    total = factors[0] * sums[0]
    for f, s in zip(factors[1:], sums[1:]):
        total = total + f * s

    def spread(column, pair):
        return jnp.where(low, column[:, 2 * pair : 2 * pair + 1], column[:, 2 * pair + 1 : 2 * pair + 2])

    attended = []
    for pair in range(heads // 2):
        acc = jnp.zeros((requests, LANES), jnp.float32)
        for m in range(members):
            piece = got_ref[m, :, pair * LANES : (pair + 1) * LANES].astype(jnp.float32)
            acc = acc + piece * spread(factors[m], pair)
        attended.append((acc / spread(total, pair)).astype(jnp.bfloat16))
    out_ref[...] = dot32(jnp.concatenate(attended, axis=1), w_ref[layer])


def widen_kernel(layer, n_parts, *refs):
    base_ref, parts = refs[0], refs[1 : 1 + n_parts]
    gate_ref, up_ref, mid_ref, out_ref = refs[1 + n_parts :]
    mid = sum_parts(base_ref, parts)
    mid_ref[...] = mid
    side = as_hi_lo(square_sum(mid), lane_ids((mid.shape[0], LANES)))
    members = out_ref.shape[0]
    own = gate_ref.shape[2] // members
    for member, owner in enumerate(member_order(members)):
        cols = slice(owner * own, (owner + 1) * own)
        out_ref[member, :, :own] = dot32(mid, gate_ref[layer, :, cols]).astype(jnp.bfloat16)
        out_ref[member, :, own : 2 * own] = dot32(mid, up_ref[layer, :, cols]).astype(jnp.bfloat16)
        out_ref[member, :, 2 * own :] = side


def silu_kernel(width, got_ref, out_ref):
    members, _, span = got_ref.shape
    own = (span - LANES) // 2
    total = got_ref[0].astype(jnp.float32)
    for member in range(1, members):
        total = total + got_ref[member].astype(jnp.float32)
    spread = (total[:, 2 * own : 2 * own + 1] + total[:, 2 * own + 1 : 2 * own + 2]) * (1.0 / width)
    inv = lax.rsqrt(spread + eps_norm)
    gate = total[:, :own] * inv
    hidden = (gate / (1.0 + jnp.exp(-gate)) * (total[:, own : 2 * own] * inv)).astype(jnp.bfloat16)
    for member in range(members):
        out_ref[member] = hidden


def in_order(got_ref):
    order = member_order(got_ref.shape[0])
    return jnp.concatenate([got_ref[order.index(m)] for m in range(len(order))], axis=1)


def down_kernel(layer, got_ref, w_ref, out_ref):
    hidden = in_order(got_ref)
    out_ref[...] = dot32(hidden, w_ref[layer])


def down_last_kernel(layer, got_ref, w_ref, keep_ref, give_ref):
    hidden = in_order(got_ref)
    part = dot32(hidden, w_ref[layer])
    core = lax.axis_index("tp") % 2
    keep_ref[...] = half_of(part, core)
    give_ref[...] = half_of(part, 1 - core)


def member_order(n_seq):
    return [0, 7, 2, 5, 1, 6, 3, 4] if n_seq == 8 else list(range(n_seq))


def make_with_kernels(n_seq, n_tp):
    order = member_order(n_seq)
    groups = [[s * n_tp + t for s in order] for t in range(n_tp)]

    def swap(chunks):
        return lax.all_to_all(chunks, ("seq", "tp"), 0, 0, axis_index_groups=groups)

    def tp_parts(part):
        got = [
            lax.ppermute(part, "tp", [(i, (i + k) % n_tp) for i in range(n_tp)])
            for k in range(1, n_tp)
        ]
        return [part] + got

    def per_device(
        hidden_in,
        lengths,
        positions,
        query_weight,
        key_weight,
        value_weight,
        out_weight,
        gate_weight,
        up_weight,
        down_weight,
        key_cache,
        value_cache,
    ):
        requests, width = hidden_in.shape
        col_count = out_weight.shape[2]
        kv_width = key_cache.shape[3]
        query_width = query_weight.shape[2]
        heads = query_width // HEAD_DIM
        kv_heads = kv_width // HEAD_DIM
        ff_own = gate_weight.shape[2] // n_seq
        bf16, f32 = jnp.bfloat16, jnp.float32

        def shape(dims, kind):
            return pltpu.VMEM(dims, kind)

        packed_shape = shape((n_seq, requests, query_width + 2 * kv_width + LANES), bf16)
        part_shape = shape((requests, col_count), f32)
        own_shape = shape((requests, col_count), bf16)
        new_shape = shape((requests, kv_width), bf16)
        fresh_rows = []
        packed_weights = (query_weight, key_weight, value_weight)
        table_shape = (requests, LANES)
        stored = (key_cache, value_cache, out_weight, gate_weight, up_weight)
        own, cosine, sine, length_table, packed, *early = call(
            functools.partial(first_kernel, len(stored)),
            (
                own_shape,
                shape(table_shape, f32),
                shape(table_shape, f32),
                shape(table_shape, jnp.int32),
                packed_shape,
            )
            + tuple(shape((1,) + a.shape[1:], bf16) for a in stored),
            hidden_in,
            lengths,
            positions,
            *packed_weights,
            *stored,
            name="first",
            held=False,
            scratch=[pltpu.VMEM(w.shape[1:], bf16) for w in packed_weights]
            + [pltpu.SMEM((requests,), jnp.int32)] * 2
            + [pltpu.SemaphoreType.DMA((6 + len(stored),))],
        )
        parts = None
        mid = None
        for layer in range(LAYERS):
            keys, values, out_here, gate_here, up_here = early if layer == 0 else stored
            if layer > 0:
                own, packed = call(
                    functools.partial(next_kernel, layer, n_tp),
                    (own_shape, packed_shape),
                    mid,
                    *parts,
                    *packed_weights,
                    name="next",
                )
            packed, key_new, value_new = call(
                functools.partial(attend_kernel, layer, width, heads, kv_heads),
                (shape((n_seq, requests, query_width + LANES), bf16), new_shape, new_shape),
                swap(packed),
                cosine,
                sine,
                length_table,
                keys,
                values,
                name="attend",
                )
            fresh_rows += [key_new, value_new]
            part = call(
                functools.partial(combine_kernel, layer, heads),
                part_shape,
                swap(packed),
                out_here,
                name="combine",
            )
            mid, packed = call(
                functools.partial(widen_kernel, layer, n_tp),
                (own_shape, shape((n_seq, requests, 2 * ff_own + LANES), bf16)),
                own,
                *tp_parts(part),
                gate_here,
                up_here,
                name="widen",
            )
            hidden = call(
                functools.partial(silu_kernel, width),
                shape((n_seq, requests, ff_own), bf16),
                swap(packed),
                name="silu",
            )
            hidden = swap(hidden)
            if layer + 1 < LAYERS:
                part = call(
                    functools.partial(down_kernel, layer), part_shape, hidden, down_weight, name="down"
                )
                parts = tp_parts(part)
        half_shape = shape((requests, col_count // 2), f32)
        keep, give = call(
            functools.partial(down_last_kernel, LAYERS - 1),
            (half_shape, half_shape),
            hidden,
            down_weight,
            name="down_last",
        )
        give = lax.ppermute(give, "tp", [(i, i ^ 1) for i in range(n_tp)])
        cache_shape = jax.ShapeDtypeStruct(key_cache.shape, bf16)
        hbm = pl.BlockSpec(memory_space=pltpu.HBM)
        key_out, value_out, token = call(
            store_kernel,
            (cache_shape, cache_shape, shape((8, LANES), f32)),
            keep,
            length_table,
            key_cache,
            value_cache,
            *fresh_rows,
            name="store",
            out_specs=[hbm, hbm, pl.BlockSpec(memory_space=pltpu.VMEM)],
            scratch=[pltpu.VMEM(key_cache.shape, bf16)] * 2
            + [pltpu.SemaphoreType.DMA((2 * LAYERS,))],
        )
        stream = call(
            functools.partial(meet_kernel, n_tp),
            shape((n_seq * n_tp, requests, col_count // 2), bf16),
            mid,
            keep,
            give,
            token,
            name="meet",
        )
        stream = lax.all_to_all(stream, ("seq", "tp"), 0, 0)
        stream = call(
            functools.partial(last_kernel, n_tp),
            jax.ShapeDtypeStruct((requests, width), bf16),
            stream,
            name="last",
        )
        return (stream, key_out, value_out)

    return per_device


def solution(mesh):
    n_seq, n_tp = mesh.shape["seq"], mesh.shape["tp"]

    def per_device(*args):
        gate_weight, key_cache = args[7], args[10]
        aligned = (
            args[6].shape[2] % (2 * LANES) == 0
            and n_tp % 2 == 0
            and gate_weight.shape[2] // n_seq % LANES == 0
            and key_cache.shape[3] == LANES
        )
        make = make_with_kernels if aligned else make_plain
        return make(n_seq, n_tp)(*args)

    return jax.shard_map(
        per_device,
        mesh=mesh,
        in_specs=(
            P(),
            P(),
            P(),
            P(None, "seq", "tp"),
            P(None, "seq", "tp"),
            P(None, "seq", "tp"),
            P(None, "tp", "seq"),
            P(None, "seq", "tp"),
            P(None, "seq", "tp"),
            P(None, "tp", "seq"),
            P(None, None, "seq", "tp"),
            P(None, None, "seq", "tp"),
        ),
        out_specs=(P(), P(None, None, "seq", "tp"), P(None, None, "seq", "tp")),
        check_vma=False,
    )
```

```python
import functools
import math

import jax
import jax.numpy as jnp
from jax import lax
from jax.experimental import pallas as pl
from jax.experimental.pallas import tpu as pltpu
from jax.sharding import PartitionSpec as P

HEAD_DIM = 64
LAYERS = 2
eps_norm = 1e-05
neg_fill = -1e30


def split_hi_lo(value, parts):
    out = []
    rest = value
    for _ in range(parts):
        head = lax.reduce_precision(rest, 8, 7)
        out.append(head.astype(jnp.bfloat16))
        rest = rest - head
    return out


def seq_swap(chunks):
    return lax.all_to_all(chunks, "seq", 0, 0)


def make_plain(n_seq, n_tp):
    def tp_sum(part):
        total = part
        for k in range(1, n_tp):
            total = total + lax.ppermute(part, "tp", [(i, (i + k) % n_tp) for i in range(n_tp)])
        return total

    def per_device(
        hidden_in,
        lengths,
        positions,
        query_weight,
        key_weight,
        value_weight,
        out_weight,
        gate_weight,
        up_weight,
        down_weight,
        key_cache,
        value_cache,
    ):
        seq_index = lax.axis_index("seq")
        requests, width = hidden_in.shape
        col_count = out_weight.shape[2]
        col_start = seq_index * col_count
        block_len = key_cache.shape[2]
        kv_width = key_cache.shape[3]
        query_width = query_weight.shape[2]
        heads = query_width // HEAD_DIM
        kv_heads = kv_width // HEAD_DIM
        repeat = heads // kv_heads
        ff_here = gate_weight.shape[2]
        ff_own = ff_here // n_seq
        scale = 1.0 / math.sqrt(HEAD_DIM)
        slots = seq_index * block_len + jnp.arange(block_len, dtype=jnp.int32)
        new_slot = (slots[None, :] == lengths[:, None])[:, :, None]
        live = (slots[None, :] <= lengths[:, None])[:, None, None, :]

        half = HEAD_DIM // 2
        inverse = 500000.0 ** (-(2.0 * jnp.arange(half, dtype=jnp.float32)) / HEAD_DIM)
        angles = positions.astype(jnp.float32)[:, None] * inverse[None, :]
        cosine = jnp.cos(angles)[:, None, :]
        sine = jnp.sin(angles)[:, None, :]

        def rotate(x):
            a, b = x[..., :half], x[..., half:]
            return jnp.concatenate([a * cosine - b * sine, b * cosine + a * sine], axis=-1)

        def stats_of(x):
            f = x.astype(jnp.float32)
            return jnp.sum(f * f, axis=-1, keepdims=True)

        def pad_lanes(cols):
            joined = jnp.concatenate(cols, axis=-1)
            return jnp.pad(joined, ((0, 0), (0, -joined.shape[-1] % 128)))

        own = lax.dynamic_slice_in_dim(hidden_in, col_start, col_count, 1)
        key_layers = []
        value_layers = []
        for layer in range(LAYERS):
            part = jnp.concatenate(
                [
                    jnp.dot(own, w[layer], preferred_element_type=jnp.float32)
                    for w in (query_weight, key_weight, value_weight)
                ],
                axis=1,
            ).astype(jnp.bfloat16)
            packed = jnp.concatenate([part, pad_lanes(split_hi_lo(stats_of(own), 2))], axis=1)
            got = seq_swap(jnp.broadcast_to(packed[None], (n_seq,) + packed.shape))
            got = jnp.sum(got.astype(jnp.float32), axis=0)
            qkv = query_width + 2 * kv_width
            spread = (got[:, qkv : qkv + 1] + got[:, qkv + 1 : qkv + 2]) / width
            got = got[:, :qkv] * lax.rsqrt(spread + eps_norm)
            query = rotate(got[:, :query_width].reshape(requests, heads, HEAD_DIM))
            query = query.astype(jnp.bfloat16).reshape(requests, kv_heads, repeat, HEAD_DIM)
            key_new = rotate(
                got[:, query_width : query_width + kv_width].reshape(requests, kv_heads, HEAD_DIM)
            )
            key_new = key_new.astype(jnp.bfloat16).reshape(requests, kv_width)
            value_new = got[:, query_width + kv_width :].astype(jnp.bfloat16)
            key_rows = jnp.where(new_slot, key_new[:, None, :], key_cache[layer])
            value_rows = jnp.where(new_slot, value_new[:, None, :], value_cache[layer])
            key_layers.append(key_rows)
            value_layers.append(value_rows)
            key_heads = key_rows.reshape(requests, block_len, kv_heads, HEAD_DIM)
            value_heads = value_rows.reshape(requests, block_len, kv_heads, HEAD_DIM)
            scores = (
                jnp.einsum("bkrd,bskd->bkrs", query, key_heads, preferred_element_type=jnp.float32)
                * scale
            )
            scores = jnp.where(live, scores, neg_fill)
            top = jnp.max(scores, axis=3)
            weights = jnp.where(live, jnp.exp(scores - top[..., None]), 0.0)
            sums = jnp.sum(weights, axis=3)
            acc = jnp.einsum(
                "bkrs,bskd->bkrd",
                weights.astype(jnp.bfloat16),
                value_heads,
                preferred_element_type=jnp.float32,
            )
            packed = jnp.concatenate(
                [
                    acc.reshape(requests, query_width).astype(jnp.bfloat16),
                    pad_lanes(
                        split_hi_lo(top.reshape(requests, heads), 3)
                        + split_hi_lo(sums.reshape(requests, heads), 2)
                    ),
                ],
                axis=1,
            )
            got = seq_swap(jnp.broadcast_to(packed[None], (n_seq,) + packed.shape))
            got = got.astype(jnp.float32)
            acc = got[:, :, :query_width].reshape(n_seq, requests, heads, HEAD_DIM)
            side = got[:, :, query_width : query_width + 5 * heads].reshape(
                n_seq, requests, 5, heads
            )
            tops = side[:, :, 0] + side[:, :, 1] + side[:, :, 2]
            factor = jnp.exp(tops - jnp.max(tops, axis=0, keepdims=True))
            total = jnp.sum(factor * (side[:, :, 3] + side[:, :, 4]), axis=0)
            attended = jnp.sum(acc * factor[..., None], axis=0) / total[..., None]
            attended = attended.astype(jnp.bfloat16).reshape(requests, query_width)

            part = jnp.dot(attended, out_weight[layer], preferred_element_type=jnp.float32)
            mid = (own.astype(jnp.float32) + tp_sum(part)).astype(jnp.bfloat16)

            gate = jnp.dot(mid, gate_weight[layer], preferred_element_type=jnp.float32)
            up = jnp.dot(mid, up_weight[layer], preferred_element_type=jnp.float32)
            side = pad_lanes(split_hi_lo(stats_of(mid), 2))
            packed = jnp.concatenate(
                [
                    gate.astype(jnp.bfloat16).reshape(requests, n_seq, ff_own),
                    up.astype(jnp.bfloat16).reshape(requests, n_seq, ff_own),
                    jnp.broadcast_to(side[:, None], (requests, n_seq, side.shape[1])),
                ],
                axis=2,
            )
            got = seq_swap(packed.transpose(1, 0, 2))
            got = jnp.sum(got.astype(jnp.float32), axis=0)
            spread = (got[:, 2 * ff_own : 2 * ff_own + 1] + got[:, 2 * ff_own + 1 : 2 * ff_own + 2]) / width
            inv = lax.rsqrt(spread + eps_norm)
            hidden = jax.nn.silu(got[:, :ff_own] * inv) * (got[:, ff_own : 2 * ff_own] * inv)
            hidden = hidden.astype(jnp.bfloat16)
            hidden = seq_swap(jnp.broadcast_to(hidden[None], (n_seq,) + hidden.shape))
            hidden = hidden.transpose(1, 0, 2).reshape(requests, ff_here)
            part = jnp.dot(hidden, down_weight[layer], preferred_element_type=jnp.float32)
            own = (mid.astype(jnp.float32) + tp_sum(part)).astype(jnp.bfloat16)

        stream = seq_swap(jnp.broadcast_to(own[None], (n_seq,) + own.shape))
        stream = stream.transpose(1, 0, 2).reshape(requests, width)
        return (stream, jnp.stack(key_layers), jnp.stack(value_layers))

    return per_device


LANES = 128
VMEM_ROOM = 8 << 20
QUARTER = LANES // 4
NEW_AT = 2 * QUARTER


def lane_ids(shape):
    return lax.broadcasted_iota(jnp.int32, shape, len(shape) - 1)


def as_hi_lo(value, lane):
    wide = jnp.broadcast_to(value, lane.shape)
    high = wide.astype(jnp.bfloat16).astype(jnp.float32)
    return jnp.where(lane == 0, high, jnp.where(lane == 1, wide - high, 0.0)).astype(jnp.bfloat16)


def member_order(n_seq, odd):
    if n_seq != 8:
        return list(range(n_seq))
    return [3, 2, 6, 7, 5, 4, 0, 1] if odd else [0, 1, 3, 2, 6, 7, 5, 4]


def position_of(member, n_seq):
    even, odd = (member_order(n_seq, side).index(member) for side in (False, True))
    return jnp.where(lax.axis_index("tp") % 2 == 0, even, odd)


def square_sum(own):
    wide = own.astype(jnp.float32)
    return jnp.sum(wide * wide, axis=1, keepdims=True)


def dot32(a, b):
    return jnp.dot(a, b, preferred_element_type=jnp.float32)


def call(body, out_shape, *args, name, held=True, scratch=(), out_specs=None):
    vmem = pl.BlockSpec(memory_space=pltpu.VMEM)
    where = vmem if held else pl.BlockSpec(memory_space=pltpu.HBM)
    single = not isinstance(out_shape, (tuple, list))
    args = [pltpu.with_memory_space_constraint(a, pltpu.VMEM if held else pltpu.HBM) for a in args]
    return pl.pallas_call(
        body,
        out_shape=out_shape,
        in_specs=[where] * len(args),
        out_specs=out_specs or (vmem if single else [vmem] * len(out_shape)),
        scratch_shapes=list(scratch),
        compiler_params=pltpu.CompilerParams(vmem_limit_bytes=VMEM_ROOM),
        name=name,
    )(*args)


def to_row(column):
    shape = (column.shape[0], LANES)
    row = lax.broadcasted_iota(jnp.int32, shape, 0)
    return jnp.sum(jnp.where(lane_ids(shape) == row, column, 0.0), axis=0, keepdims=True)


def to_column(line, requests):
    shape = (requests, LANES)
    row = lax.broadcasted_iota(jnp.int32, shape, 0)
    return jnp.sum(jnp.where(lane_ids(shape) == row, line, 0.0), axis=1, keepdims=True)


def project_body(own, weights, out_ref):
    requests = own.shape[0]
    members = out_ref.shape[0]
    per = requests // members
    query, key, value = [dot32(own, w) for w in weights]
    width = query.shape[1]
    query = query.astype(jnp.bfloat16)
    line = to_row(square_sum(own))
    high = line.astype(jnp.bfloat16).astype(jnp.float32)
    row = lax.broadcasted_iota(jnp.int32, (requests, LANES), 0)
    base = jnp.where(row == 2 * per, high, jnp.where(row == 2 * per + 1, line - high, 0.0))
    for member in range(members):
        block = base
        for r in range(per):
            at = member * per + r
            block = jnp.where(row == 2 * r, key[at : at + 1], block)
            block = jnp.where(row == 2 * r + 1, value[at : at + 1], block)
        place = position_of(member, members)
        out_ref[place, :, :width] = query
        out_ref[place, :, width:] = block.astype(jnp.bfloat16)


def first_kernel(n_more, *refs):
    hidden_ref, length_ref, position_ref, wq_ref, wk_ref, wv_ref = refs[:6]
    more = refs[6 : 6 + n_more]
    own_ref, cos_ref, sin_ref, table_ref, out_ref = refs[6 + n_more : 11 + n_more]
    more_here = refs[11 + n_more : 11 + 2 * n_more]
    wq_here, wk_here, wv_here, lengths, positions, sems = refs[11 + 2 * n_more :]
    span = own_ref.shape[1]
    start = pl.multiple_of(lax.axis_index("seq") * span, LANES)
    copies = [
        pltpu.make_async_copy(position_ref, positions, sems.at[0]),
        pltpu.make_async_copy(length_ref, lengths, sems.at[1]),
        pltpu.make_async_copy(hidden_ref.at[:, pl.ds(start, span)], own_ref, sems.at[2]),
        pltpu.make_async_copy(wq_ref.at[0], wq_here, sems.at[3]),
        pltpu.make_async_copy(wk_ref.at[0], wk_here, sems.at[4]),
        pltpu.make_async_copy(wv_ref.at[0], wv_here, sems.at[5]),
    ]
    copies += [
        pltpu.make_async_copy(ref.at[0], here.at[0], sems.at[6 + i])
        for i, (ref, here) in enumerate(zip(more, more_here))
    ]
    for copy in copies:
        copy.start()
    copies[0].wait()
    copies[1].wait()
    half = HEAD_DIM // 2
    lane = lane_ids(table_ref.shape)
    row = lax.broadcasted_iota(jnp.int32, table_ref.shape, 0)
    place = jnp.zeros(table_ref.shape, jnp.int32)
    length = jnp.zeros(table_ref.shape, jnp.int32)
    for b in range(table_ref.shape[0]):
        place = jnp.where(row == b, positions[b], place)
        length = jnp.where(row == b, lengths[b], length)
    inverse = jnp.zeros(table_ref.shape, jnp.float32)
    for i in range(half):
        inverse = jnp.where(lane % half == i, 500000.0 ** (-2.0 * i / HEAD_DIM), inverse)
    angles = place.astype(jnp.float32) * inverse
    sine = jnp.sin(angles)
    table_ref[...] = length
    cos_ref[...] = jnp.cos(angles)
    sin_ref[...] = jnp.where(lane % HEAD_DIM < half, -sine, sine)
    for copy in copies[2:6]:
        copy.wait()
    project_body(own_ref[...], [wq_here[...], wk_here[...], wv_here[...]], out_ref)
    for copy in copies[6:]:
        copy.wait()


def store_kernel(keep_ref, length_ref, key_ref, value_ref, *refs):
    layers, requests, block, _ = key_ref.shape
    sent_refs = refs[:layers]
    key_out, value_out, token_ref, key_here, value_here, sems = refs[layers:]
    token_ref[...] = jnp.zeros_like(token_ref)
    fresh = length_ref[...] - lax.axis_index("seq") * block
    slot = lax.broadcasted_iota(jnp.int32, (block, LANES), 0)
    row = lax.broadcasted_iota(jnp.int32, (requests, LANES), 0)
    quarter_here = lane_ids((requests, LANES)) // QUARTER
    copies = []
    for layer in range(layers):
        members, _, span = sent_refs[layer].shape
        per = requests // members
        for member in range(members):
            sent = sent_refs[layer][position_of(member, members), :, span - LANES :]
            sent = sent.astype(jnp.float32)
            wide = jnp.zeros((requests, LANES), jnp.float32)
            for quarter in range(4):
                shifted = pltpu.roll(sent, (QUARTER * quarter - NEW_AT) % LANES, 1)
                wide = jnp.where((quarter_here == quarter) & (row % 4 == quarter), shifted, wide)
            for r in range(per):
                b = member * per + r
                here = slot == fresh[b : b + 1]
                for i, (old, new_here) in enumerate([(key_ref, key_here), (value_ref, value_here)]):
                    j = 4 * (2 * r + i)
                    new = jnp.sum(wide[j : j + 4], axis=0, keepdims=True)
                    kept = jnp.where(here, new, old[layer, b].astype(jnp.float32))
                    new_here[layer, b] = kept.astype(jnp.bfloat16)
        for i, (here, out) in enumerate([(key_here, key_out), (value_here, value_out)]):
            copies.append(
                pltpu.make_async_copy(here.at[layer], out.at[layer], sems.at[2 * layer + i])
            )
            copies[-1].start()
    for copy in copies:
        copy.wait()


def sum_parts(base_ref, part_refs):
    total = part_refs[0][...]
    for ref in part_refs[1:]:
        total = total + ref[...]
    return (base_ref[...].astype(jnp.float32) + total).astype(jnp.bfloat16)


def next_kernel(layer, n_parts, *refs):
    base_ref, parts = refs[0], refs[1 : 1 + n_parts]
    wq_ref, wk_ref, wv_ref, own_ref, out_ref = refs[1 + n_parts :]
    own = sum_parts(base_ref, parts)
    own_ref[...] = own
    project_body(own, [w[layer] for w in (wq_ref, wk_ref, wv_ref)], out_ref)


def half_of(value, core):
    middle = value.shape[1] // 2
    return jnp.where(core == 0, value[:, :middle], value[:, middle:])


def meet_kernel(n_tp, mid_ref, keep_ref, got_ref, token_ref, out_ref):
    place = lax.axis_index("tp")
    total = keep_ref[...] + got_ref[...]
    base = half_of(mid_ref[...].astype(jnp.float32), place % 2)
    total = (total + jnp.where(place < 2, base, 0.0)).astype(jnp.bfloat16)
    for member in range(out_ref.shape[0]):
        out_ref[member] = total


def last_kernel(n_tp, got_ref, out_ref):
    span = got_ref.shape[2]
    for block in range(got_ref.shape[0] // n_tp):
        for core in range(2):
            total = got_ref[block * n_tp + core].astype(jnp.float32)
            for pair in range(1, n_tp // 2):
                total = total + got_ref[block * n_tp + 2 * pair + core].astype(jnp.float32)
            at = (2 * block + core) * span
            out_ref[:, at : at + span] = total.astype(jnp.bfloat16)


def attend_kernel(
    layer, width, heads, kv_heads, got_ref, cos_ref, sin_ref, length_ref,
    key_ref, value_ref, out_ref,
):
    members, requests, _ = got_ref.shape
    query_width = heads * HEAD_DIM
    repeat = heads // kv_heads
    block = key_ref.shape[2]
    per = requests // members
    place = lax.axis_index("seq")

    def summed(at):
        total = got_ref[0, :, at : at + LANES].astype(jnp.float32)
        for member in range(1, members):
            total = total + got_ref[member, :, at : at + LANES].astype(jnp.float32)
        return total

    lane = lane_ids((requests, LANES))
    low = lane < HEAD_DIM
    fresh_sums = summed(query_width)
    spread = (fresh_sums[2 * per : 2 * per + 1] + fresh_sums[2 * per + 1 : 2 * per + 2]) * (
        1.0 / width
    )
    inv_line = lax.rsqrt(spread + eps_norm)
    inv = to_column(inv_line, requests)
    half = HEAD_DIM // 2

    def rotated(x, cosine, sine):
        first = lane_ids(x.shape) % HEAD_DIM < half
        other = jnp.where(first, pltpu.roll(x, LANES - half, 1), pltpu.roll(x, half, 1))
        return x * cosine + other * sine

    stacked = []
    for pair in range(heads // 2):
        x = rotated(summed(pair * LANES) * inv, cos_ref[...], sin_ref[...])
        turned = pltpu.roll(x, HEAD_DIM, 1)
        if 2 * pair // repeat == 0:
            stacked += [jnp.where(low, x, 0.0), jnp.where(low, turned, 0.0)]
        else:
            stacked += [jnp.where(low, 0.0, turned), jnp.where(low, 0.0, x)]
    query = jnp.concatenate(stacked, axis=0).astype(jnp.bfloat16)

    request = lax.broadcasted_iota(jnp.int32, (requests, LANES), 0)
    key_new = jnp.zeros((requests, LANES), jnp.float32)
    value_new = jnp.zeros((requests, LANES), jnp.float32)
    rows = []
    for r in range(per):
        at = place * per + r
        scale = jnp.sum(
            jnp.where(lane_ids((1, LANES)) == at, inv_line, 0.0), axis=1, keepdims=True
        )
        key = rotated(
            fresh_sums[2 * r : 2 * r + 1] * scale, cos_ref[pl.ds(at, 1)], sin_ref[pl.ds(at, 1)]
        )
        key = key.astype(jnp.bfloat16).astype(jnp.float32)
        value = (fresh_sums[2 * r + 1 : 2 * r + 2] * scale).astype(jnp.bfloat16).astype(jnp.float32)
        key_new = jnp.where(request == at, key, key_new)
        value_new = jnp.where(request == at, value, value_new)
        rows += [key, value]
    owned = jnp.concatenate([request // per == place] * heads, axis=0)

    def per_head(x):
        return jnp.concatenate([x] * heads, axis=0)

    to_scores = 1.0 / math.sqrt(HEAD_DIM)
    fresh_scores = (
        jnp.sum(query.astype(jnp.float32) * per_head(key_new), axis=1, keepdims=True) * to_scores
    )
    owned_row = owned[:, 0:1]
    fresh_scores = jnp.where(owned_row, fresh_scores, neg_fill)

    keys = key_ref[layer].reshape(requests * block, LANES)
    values = value_ref[layer].reshape(requests * block, LANES)
    scores = lax.dot_general(
        query, keys, (((1,), (1,)), ((), ())), preferred_element_type=jnp.float32
    ) * to_scores
    begin = request * block
    end = begin + jnp.clip(length_ref[...] - place * block, 0, block)
    copies = scores.shape[1] // LANES
    begin = jnp.concatenate([per_head(begin)] * copies, axis=1)
    end = jnp.concatenate([per_head(end)] * copies, axis=1)
    column = lane_ids(scores.shape)
    live = (column >= begin) & (column < end)
    scores = jnp.where(live, scores, neg_fill)
    top = jnp.maximum(jnp.max(scores, axis=1, keepdims=True), fresh_scores)
    weights = jnp.where(live, jnp.exp(scores - top), 0.0)
    fresh_weights = jnp.where(owned_row, jnp.exp(fresh_scores - top), 0.0)
    sums = jnp.sum(weights, axis=1, keepdims=True) + fresh_weights
    acc = dot32(weights.astype(jnp.bfloat16), values)
    acc = acc + fresh_weights.astype(jnp.bfloat16).astype(jnp.float32) * per_head(value_new)
    turned = pltpu.roll(acc, HEAD_DIM, 1)

    side = jnp.zeros((requests, LANES), jnp.float32)
    for h in range(heads):
        part = slice(h * requests, (h + 1) * requests)
        for group in range(5):
            side = jnp.where(lane == group * heads + h, (top if group < 3 else sums)[part], side)
    spare = jnp.zeros((requests, LANES), jnp.float32)
    for j, line in enumerate(rows):
        spare = jnp.where(request // 4 == j, line, spare)
    for quarter in range(4):
        shifted = pltpu.roll(spare, (NEW_AT - QUARTER * quarter) % LANES, 1)
        side = jnp.where(
            (lane >= NEW_AT) & (lane < NEW_AT + QUARTER) & (request % 4 == quarter), shifted, side
        )
    one = side.astype(jnp.bfloat16).astype(jnp.float32)
    two = (side - one).astype(jnp.bfloat16).astype(jnp.float32)
    three = side - one - two
    second = ((lane >= heads) & (lane < 2 * heads)) | ((lane >= 4 * heads) & (lane < 5 * heads))
    third = (lane >= 2 * heads) & (lane < 3 * heads)
    side = jnp.where(third, three, jnp.where(second, two, one)).astype(jnp.bfloat16)
    pieces = []
    for pair in range(heads // 2):
        even = slice(2 * pair * requests, (2 * pair + 1) * requests)
        odd = slice((2 * pair + 1) * requests, (2 * pair + 2) * requests)
        if 2 * pair // repeat == 0:
            pieces.append(jnp.where(low, acc[even], turned[odd]).astype(jnp.bfloat16))
        else:
            pieces.append(jnp.where(low, turned[even], acc[odd]).astype(jnp.bfloat16))
    pieces.append(side)
    for member in range(members):
        for i, piece in enumerate(pieces):
            out_ref[member, :, i * LANES : (i + 1) * LANES] = piece


def combine_kernel(layer, heads, got_ref, w_ref, out_ref):
    members, requests, _ = got_ref.shape
    query_width = heads * HEAD_DIM
    low = lane_ids((requests, LANES)) < HEAD_DIM
    sides = [
        got_ref[m, :, query_width : query_width + LANES].astype(jnp.float32) for m in range(members)
    ]
    tops = [
        s[:, :heads] + s[:, heads : 2 * heads] + s[:, 2 * heads : 3 * heads] for s in sides
    ]
    sums = [s[:, 3 * heads : 4 * heads] + s[:, 4 * heads : 5 * heads] for s in sides]
    top = tops[0]
    for t in tops[1:]:
        top = jnp.maximum(top, t)
    factors = [jnp.exp(t - top) for t in tops]
    total = factors[0] * sums[0]
    for f, s in zip(factors[1:], sums[1:]):
        total = total + f * s

    def spread(column, pair):
        return jnp.where(low, column[:, 2 * pair : 2 * pair + 1], column[:, 2 * pair + 1 : 2 * pair + 2])

    attended = []
    for pair in range(heads // 2):
        acc = jnp.zeros((requests, LANES), jnp.float32)
        for m in range(members):
            piece = got_ref[m, :, pair * LANES : (pair + 1) * LANES].astype(jnp.float32)
            acc = acc + piece * spread(factors[m], pair)
        attended.append((acc / spread(total, pair)).astype(jnp.bfloat16))
    out_ref[...] = dot32(jnp.concatenate(attended, axis=1), w_ref[layer])


def widen_kernel(layer, n_parts, *refs):
    base_ref, parts = refs[0], refs[1 : 1 + n_parts]
    gate_ref, up_ref, mid_ref, out_ref = refs[1 + n_parts :]
    mid = sum_parts(base_ref, parts)
    mid_ref[...] = mid
    side = as_hi_lo(square_sum(mid), lane_ids((mid.shape[0], LANES)))
    members = out_ref.shape[0]
    own = gate_ref.shape[2] // members
    for member in range(members):
        cols = slice(member * own, (member + 1) * own)
        place = position_of(member, members)
        out_ref[place, :, :own] = dot32(mid, gate_ref[layer, :, cols]).astype(jnp.bfloat16)
        out_ref[place, :, own : 2 * own] = dot32(mid, up_ref[layer, :, cols]).astype(jnp.bfloat16)
        out_ref[place, :, 2 * own :] = side


def silu_kernel(width, got_ref, out_ref):
    members, _, span = got_ref.shape
    own = (span - LANES) // 2
    total = got_ref[0].astype(jnp.float32)
    for member in range(1, members):
        total = total + got_ref[member].astype(jnp.float32)
    spread = (total[:, 2 * own : 2 * own + 1] + total[:, 2 * own + 1 : 2 * own + 2]) * (1.0 / width)
    inv = lax.rsqrt(spread + eps_norm)
    gate = total[:, :own] * inv
    hidden = (gate / (1.0 + jnp.exp(-gate)) * (total[:, own : 2 * own] * inv)).astype(jnp.bfloat16)
    for member in range(members):
        out_ref[member] = hidden


def in_order(got_ref):
    members = got_ref.shape[0]
    return jnp.concatenate([got_ref[position_of(m, members)] for m in range(members)], axis=1)


def down_kernel(layer, got_ref, w_ref, out_ref):
    hidden = in_order(got_ref)
    out_ref[...] = dot32(hidden, w_ref[layer])


def down_last_kernel(layer, got_ref, w_ref, keep_ref, give_ref):
    hidden = in_order(got_ref)
    part = dot32(hidden, w_ref[layer])
    core = lax.axis_index("tp") % 2
    keep_ref[...] = half_of(part, core)
    give_ref[...] = half_of(part, 1 - core)


def make_with_kernels(n_seq, n_tp):
    groups = [[s * n_tp + t for s in member_order(n_seq, t % 2 == 1)] for t in range(n_tp)]

    def swap(chunks):
        return lax.all_to_all(chunks, ("seq", "tp"), 0, 0, axis_index_groups=groups)

    def tp_parts(part):
        got = [
            lax.ppermute(part, "tp", [(i, (i + k) % n_tp) for i in range(n_tp)])
            for k in range(1, n_tp)
        ]
        return [part] + got

    def per_device(
        hidden_in,
        lengths,
        positions,
        query_weight,
        key_weight,
        value_weight,
        out_weight,
        gate_weight,
        up_weight,
        down_weight,
        key_cache,
        value_cache,
    ):
        requests, width = hidden_in.shape
        col_count = out_weight.shape[2]
        kv_width = key_cache.shape[3]
        query_width = query_weight.shape[2]
        heads = query_width // HEAD_DIM
        kv_heads = kv_width // HEAD_DIM
        ff_own = gate_weight.shape[2] // n_seq
        bf16, f32 = jnp.bfloat16, jnp.float32

        def shape(dims, kind):
            return pltpu.VMEM(dims, kind)

        packed_shape = shape((n_seq, requests, query_width + LANES), bf16)
        part_shape = shape((requests, col_count), f32)
        own_shape = shape((requests, col_count), bf16)
        sent = []
        packed_weights = (query_weight, key_weight, value_weight)
        table_shape = (requests, LANES)
        stored = (key_cache, value_cache, out_weight, gate_weight, up_weight)
        own, cosine, sine, length_table, packed, *early = call(
            functools.partial(first_kernel, len(stored)),
            (
                own_shape,
                shape(table_shape, f32),
                shape(table_shape, f32),
                shape(table_shape, jnp.int32),
                packed_shape,
            )
            + tuple(shape((1,) + a.shape[1:], bf16) for a in stored),
            hidden_in,
            lengths,
            positions,
            *packed_weights,
            *stored,
            name="first",
            held=False,
            scratch=[pltpu.VMEM(w.shape[1:], bf16) for w in packed_weights]
            + [pltpu.SMEM((requests,), jnp.int32)] * 2
            + [pltpu.SemaphoreType.DMA((6 + len(stored),))],
        )
        parts = None
        mid = None
        for layer in range(LAYERS):
            keys, values, out_here, gate_here, up_here = early if layer == 0 else stored
            if layer > 0:
                own, packed = call(
                    functools.partial(next_kernel, layer, n_tp),
                    (own_shape, packed_shape),
                    mid,
                    *parts,
                    *packed_weights,
                    name="next",
                )
            packed = call(
                functools.partial(attend_kernel, layer, width, heads, kv_heads),
                packed_shape,
                swap(packed),
                cosine,
                sine,
                length_table,
                keys,
                values,
                name="attend",
                )
            sent.append(swap(packed))
            part = call(
                functools.partial(combine_kernel, layer, heads),
                part_shape,
                sent[-1],
                out_here,
                name="combine",
            )
            mid, packed = call(
                functools.partial(widen_kernel, layer, n_tp),
                (own_shape, shape((n_seq, requests, 2 * ff_own + LANES), bf16)),
                own,
                *tp_parts(part),
                gate_here,
                up_here,
                name="widen",
            )
            hidden = call(
                functools.partial(silu_kernel, width),
                shape((n_seq, requests, ff_own), bf16),
                swap(packed),
                name="silu",
            )
            hidden = swap(hidden)
            if layer + 1 < LAYERS:
                part = call(
                    functools.partial(down_kernel, layer), part_shape, hidden, down_weight, name="down"
                )
                parts = tp_parts(part)
        half_shape = shape((requests, col_count // 2), f32)
        keep, give = call(
            functools.partial(down_last_kernel, LAYERS - 1),
            (half_shape, half_shape),
            hidden,
            down_weight,
            name="down_last",
        )
        give = lax.ppermute(give, "tp", [(i, i ^ 1) for i in range(n_tp)])
        cache_shape = jax.ShapeDtypeStruct(key_cache.shape, bf16)
        hbm = pl.BlockSpec(memory_space=pltpu.HBM)
        key_out, value_out, token = call(
            store_kernel,
            (cache_shape, cache_shape, shape((8, LANES), f32)),
            keep,
            length_table,
            key_cache,
            value_cache,
            *sent,
            name="store",
            out_specs=[hbm, hbm, pl.BlockSpec(memory_space=pltpu.VMEM)],
            scratch=[pltpu.VMEM(key_cache.shape, bf16)] * 2
            + [pltpu.SemaphoreType.DMA((2 * LAYERS,))],
        )
        stream = call(
            functools.partial(meet_kernel, n_tp),
            shape((n_seq * n_tp, requests, col_count // 2), bf16),
            mid,
            keep,
            give,
            token,
            name="meet",
        )
        stream = lax.all_to_all(stream, ("seq", "tp"), 0, 0)
        stream = call(
            functools.partial(last_kernel, n_tp),
            jax.ShapeDtypeStruct((requests, width), bf16),
            stream,
            name="last",
        )
        return (stream, key_out, value_out)

    return per_device


def solution(mesh):
    n_seq, n_tp = mesh.shape["seq"], mesh.shape["tp"]

    def per_device(*args):
        gate_weight, key_cache = args[7], args[10]
        aligned = (
            args[6].shape[2] % (2 * LANES) == 0
            and n_tp % 2 == 0
            and gate_weight.shape[2] // n_seq % LANES == 0
            and key_cache.shape[3] == LANES
            and args[0].shape[0] == 2 * n_seq
        )
        make = make_with_kernels if aligned else make_plain
        return make(n_seq, n_tp)(*args)

    return jax.shard_map(
        per_device,
        mesh=mesh,
        in_specs=(
            P(),
            P(),
            P(),
            P(None, "seq", "tp"),
            P(None, "seq", "tp"),
            P(None, "seq", "tp"),
            P(None, "tp", "seq"),
            P(None, "seq", "tp"),
            P(None, "seq", "tp"),
            P(None, "tp", "seq"),
            P(None, None, "seq", "tp"),
            P(None, None, "seq", "tp"),
        ),
        out_specs=(P(), P(None, None, "seq", "tp"), P(None, None, "seq", "tp")),
        check_vma=False,
    )
```

```python
import functools
import math

import jax
import jax.numpy as jnp
from jax import lax
from jax.experimental import pallas as pl
from jax.experimental.pallas import tpu as pltpu
from jax.sharding import PartitionSpec as P

HEAD_DIM = 64
LAYERS = 2
eps_norm = 1e-05
neg_fill = -1e30


def split_hi_lo(value, parts):
    out = []
    rest = value
    for _ in range(parts):
        head = lax.reduce_precision(rest, 8, 7)
        out.append(head.astype(jnp.bfloat16))
        rest = rest - head
    return out


def seq_swap(chunks):
    return lax.all_to_all(chunks, "seq", 0, 0)


def make_plain(n_seq, n_tp):
    def tp_sum(part):
        total = part
        for k in range(1, n_tp):
            total = total + lax.ppermute(part, "tp", [(i, (i + k) % n_tp) for i in range(n_tp)])
        return total

    def per_device(
        hidden_in,
        lengths,
        positions,
        query_weight,
        key_weight,
        value_weight,
        out_weight,
        gate_weight,
        up_weight,
        down_weight,
        key_cache,
        value_cache,
    ):
        seq_index = lax.axis_index("seq")
        requests, width = hidden_in.shape
        col_count = out_weight.shape[2]
        col_start = seq_index * col_count
        block_len = key_cache.shape[2]
        kv_width = key_cache.shape[3]
        query_width = query_weight.shape[2]
        heads = query_width // HEAD_DIM
        kv_heads = kv_width // HEAD_DIM
        repeat = heads // kv_heads
        ff_here = gate_weight.shape[2]
        ff_own = ff_here // n_seq
        scale = 1.0 / math.sqrt(HEAD_DIM)
        slots = seq_index * block_len + jnp.arange(block_len, dtype=jnp.int32)
        new_slot = (slots[None, :] == lengths[:, None])[:, :, None]
        live = (slots[None, :] <= lengths[:, None])[:, None, None, :]

        half = HEAD_DIM // 2
        inverse = 500000.0 ** (-(2.0 * jnp.arange(half, dtype=jnp.float32)) / HEAD_DIM)
        angles = positions.astype(jnp.float32)[:, None] * inverse[None, :]
        cosine = jnp.cos(angles)[:, None, :]
        sine = jnp.sin(angles)[:, None, :]

        def rotate(x):
            a, b = x[..., :half], x[..., half:]
            return jnp.concatenate([a * cosine - b * sine, b * cosine + a * sine], axis=-1)

        def stats_of(x):
            f = x.astype(jnp.float32)
            return jnp.sum(f * f, axis=-1, keepdims=True)

        def pad_lanes(cols):
            joined = jnp.concatenate(cols, axis=-1)
            return jnp.pad(joined, ((0, 0), (0, -joined.shape[-1] % 128)))

        own = lax.dynamic_slice_in_dim(hidden_in, col_start, col_count, 1)
        key_layers = []
        value_layers = []
        for layer in range(LAYERS):
            part = jnp.concatenate(
                [
                    jnp.dot(own, w[layer], preferred_element_type=jnp.float32)
                    for w in (query_weight, key_weight, value_weight)
                ],
                axis=1,
            ).astype(jnp.bfloat16)
            packed = jnp.concatenate([part, pad_lanes(split_hi_lo(stats_of(own), 2))], axis=1)
            got = seq_swap(jnp.broadcast_to(packed[None], (n_seq,) + packed.shape))
            got = jnp.sum(got.astype(jnp.float32), axis=0)
            qkv = query_width + 2 * kv_width
            spread = (got[:, qkv : qkv + 1] + got[:, qkv + 1 : qkv + 2]) / width
            got = got[:, :qkv] * lax.rsqrt(spread + eps_norm)
            query = rotate(got[:, :query_width].reshape(requests, heads, HEAD_DIM))
            query = query.astype(jnp.bfloat16).reshape(requests, kv_heads, repeat, HEAD_DIM)
            key_new = rotate(
                got[:, query_width : query_width + kv_width].reshape(requests, kv_heads, HEAD_DIM)
            )
            key_new = key_new.astype(jnp.bfloat16).reshape(requests, kv_width)
            value_new = got[:, query_width + kv_width :].astype(jnp.bfloat16)
            key_rows = jnp.where(new_slot, key_new[:, None, :], key_cache[layer])
            value_rows = jnp.where(new_slot, value_new[:, None, :], value_cache[layer])
            key_layers.append(key_rows)
            value_layers.append(value_rows)
            key_heads = key_rows.reshape(requests, block_len, kv_heads, HEAD_DIM)
            value_heads = value_rows.reshape(requests, block_len, kv_heads, HEAD_DIM)
            scores = (
                jnp.einsum("bkrd,bskd->bkrs", query, key_heads, preferred_element_type=jnp.float32)
                * scale
            )
            scores = jnp.where(live, scores, neg_fill)
            top = jnp.max(scores, axis=3)
            weights = jnp.where(live, jnp.exp(scores - top[..., None]), 0.0)
            sums = jnp.sum(weights, axis=3)
            acc = jnp.einsum(
                "bkrs,bskd->bkrd",
                weights.astype(jnp.bfloat16),
                value_heads,
                preferred_element_type=jnp.float32,
            )
            packed = jnp.concatenate(
                [
                    acc.reshape(requests, query_width).astype(jnp.bfloat16),
                    pad_lanes(
                        split_hi_lo(top.reshape(requests, heads), 3)
                        + split_hi_lo(sums.reshape(requests, heads), 2)
                    ),
                ],
                axis=1,
            )
            got = seq_swap(jnp.broadcast_to(packed[None], (n_seq,) + packed.shape))
            got = got.astype(jnp.float32)
            acc = got[:, :, :query_width].reshape(n_seq, requests, heads, HEAD_DIM)
            side = got[:, :, query_width : query_width + 5 * heads].reshape(
                n_seq, requests, 5, heads
            )
            tops = side[:, :, 0] + side[:, :, 1] + side[:, :, 2]
            factor = jnp.exp(tops - jnp.max(tops, axis=0, keepdims=True))
            total = jnp.sum(factor * (side[:, :, 3] + side[:, :, 4]), axis=0)
            attended = jnp.sum(acc * factor[..., None], axis=0) / total[..., None]
            attended = attended.astype(jnp.bfloat16).reshape(requests, query_width)

            part = jnp.dot(attended, out_weight[layer], preferred_element_type=jnp.float32)
            mid = (own.astype(jnp.float32) + tp_sum(part)).astype(jnp.bfloat16)

            gate = jnp.dot(mid, gate_weight[layer], preferred_element_type=jnp.float32)
            up = jnp.dot(mid, up_weight[layer], preferred_element_type=jnp.float32)
            side = pad_lanes(split_hi_lo(stats_of(mid), 2))
            packed = jnp.concatenate(
                [
                    gate.astype(jnp.bfloat16).reshape(requests, n_seq, ff_own),
                    up.astype(jnp.bfloat16).reshape(requests, n_seq, ff_own),
                    jnp.broadcast_to(side[:, None], (requests, n_seq, side.shape[1])),
                ],
                axis=2,
            )
            got = seq_swap(packed.transpose(1, 0, 2))
            got = jnp.sum(got.astype(jnp.float32), axis=0)
            spread = (got[:, 2 * ff_own : 2 * ff_own + 1] + got[:, 2 * ff_own + 1 : 2 * ff_own + 2]) / width
            inv = lax.rsqrt(spread + eps_norm)
            hidden = jax.nn.silu(got[:, :ff_own] * inv) * (got[:, ff_own : 2 * ff_own] * inv)
            hidden = hidden.astype(jnp.bfloat16)
            hidden = seq_swap(jnp.broadcast_to(hidden[None], (n_seq,) + hidden.shape))
            hidden = hidden.transpose(1, 0, 2).reshape(requests, ff_here)
            part = jnp.dot(hidden, down_weight[layer], preferred_element_type=jnp.float32)
            own = (mid.astype(jnp.float32) + tp_sum(part)).astype(jnp.bfloat16)

        stream = seq_swap(jnp.broadcast_to(own[None], (n_seq,) + own.shape))
        stream = stream.transpose(1, 0, 2).reshape(requests, width)
        return (stream, jnp.stack(key_layers), jnp.stack(value_layers))

    return per_device


LANES = 128
VMEM_ROOM = 8 << 20
QUARTER = LANES // 4
NEW_AT = 2 * QUARTER


def lane_ids(shape):
    return lax.broadcasted_iota(jnp.int32, shape, len(shape) - 1)


def as_hi_lo(value, lane):
    wide = jnp.broadcast_to(value, lane.shape)
    high = wide.astype(jnp.bfloat16).astype(jnp.float32)
    return jnp.where(lane == 0, high, jnp.where(lane == 1, wide - high, 0.0)).astype(jnp.bfloat16)


def member_order(n_seq, odd):
    if n_seq != 8:
        return list(range(n_seq))
    return [3, 2, 6, 7, 5, 4, 0, 1] if odd else [0, 1, 3, 2, 6, 7, 5, 4]


def whole_order(n_seq, n_tp):
    return [s * n_tp + (t ^ (t >> 1)) for s in member_order(n_seq, False) for t in range(n_tp)]


def position_of(member, n_seq):
    even, odd = (member_order(n_seq, side).index(member) for side in (False, True))
    return jnp.where(lax.axis_index("tp") % 2 == 0, even, odd)


def square_sum(own):
    wide = own.astype(jnp.float32)
    return jnp.sum(wide * wide, axis=1, keepdims=True)


def dot32(a, b):
    return jnp.dot(a, b, preferred_element_type=jnp.float32)


def call(body, out_shape, *args, name, held=None, scratch=(), out_specs=None):
    vmem, hbm = [pl.BlockSpec(memory_space=m) for m in (pltpu.VMEM, pltpu.HBM)]
    held = len(args) if held is None else held
    single = not isinstance(out_shape, (tuple, list))
    args = [
        pltpu.with_memory_space_constraint(a, pltpu.VMEM if i < held else pltpu.HBM)
        for i, a in enumerate(args)
    ]
    return pl.pallas_call(
        body,
        out_shape=out_shape,
        in_specs=[vmem if i < held else hbm for i in range(len(args))],
        out_specs=out_specs or (vmem if single else [vmem] * len(out_shape)),
        scratch_shapes=list(scratch),
        compiler_params=pltpu.CompilerParams(vmem_limit_bytes=VMEM_ROOM),
        name=name,
    )(*args)


def to_row(column):
    shape = (column.shape[0], LANES)
    row = lax.broadcasted_iota(jnp.int32, shape, 0)
    return jnp.sum(jnp.where(lane_ids(shape) == row, column, 0.0), axis=0, keepdims=True)


def to_column(line, requests):
    shape = (requests, LANES)
    row = lax.broadcasted_iota(jnp.int32, shape, 0)
    return jnp.sum(jnp.where(lane_ids(shape) == row, line, 0.0), axis=1, keepdims=True)


def project_body(own, weights, out_ref):
    requests = own.shape[0]
    members = out_ref.shape[0]
    per = requests // members
    query, key, value = [dot32(own, w) for w in weights]
    width = query.shape[1]
    query = query.astype(jnp.bfloat16)
    line = to_row(square_sum(own))
    high = line.astype(jnp.bfloat16).astype(jnp.float32)
    row = lax.broadcasted_iota(jnp.int32, (requests, LANES), 0)
    base = jnp.where(row == 2 * per, high, jnp.where(row == 2 * per + 1, line - high, 0.0))
    for member in range(members):
        block = base
        for r in range(per):
            at = member * per + r
            block = jnp.where(row == 2 * r, key[at : at + 1], block)
            block = jnp.where(row == 2 * r + 1, value[at : at + 1], block)
        place = position_of(member, members)
        out_ref[place, :, :width] = query
        out_ref[place, :, width:] = block.astype(jnp.bfloat16)


def first_kernel(n_more, *refs):
    hidden_ref, length_ref, position_ref, wq_ref, wk_ref, wv_ref = refs[:6]
    more = refs[6 : 6 + n_more]
    own_ref, cos_ref, sin_ref, table_ref, out_ref = refs[6 + n_more : 11 + n_more]
    more_here = refs[11 + n_more : 11 + 2 * n_more]
    wq_here, wk_here, wv_here, lengths, positions, sems = refs[11 + 2 * n_more :]
    span = own_ref.shape[1]
    start = pl.multiple_of(lax.axis_index("seq") * span, LANES)
    copies = [
        pltpu.make_async_copy(position_ref, positions, sems.at[0]),
        pltpu.make_async_copy(length_ref, lengths, sems.at[1]),
        pltpu.make_async_copy(hidden_ref.at[:, pl.ds(start, span)], own_ref, sems.at[2]),
        pltpu.make_async_copy(wq_ref.at[0], wq_here, sems.at[3]),
        pltpu.make_async_copy(wk_ref.at[0], wk_here, sems.at[4]),
        pltpu.make_async_copy(wv_ref.at[0], wv_here, sems.at[5]),
    ]
    copies += [
        pltpu.make_async_copy(ref.at[0], here.at[0], sems.at[6 + i])
        for i, (ref, here) in enumerate(zip(more, more_here))
    ]
    for copy in copies:
        copy.start()
    copies[0].wait()
    copies[1].wait()
    half = HEAD_DIM // 2
    lane = lane_ids(table_ref.shape)
    row = lax.broadcasted_iota(jnp.int32, table_ref.shape, 0)
    place = jnp.zeros(table_ref.shape, jnp.int32)
    length = jnp.zeros(table_ref.shape, jnp.int32)
    for b in range(table_ref.shape[0]):
        place = jnp.where(row == b, positions[b], place)
        length = jnp.where(row == b, lengths[b], length)
    inverse = jnp.zeros(table_ref.shape, jnp.float32)
    for i in range(half):
        inverse = jnp.where(lane % half == i, 500000.0 ** (-2.0 * i / HEAD_DIM), inverse)
    angles = place.astype(jnp.float32) * inverse
    sine = jnp.sin(angles)
    table_ref[...] = length
    cos_ref[...] = jnp.cos(angles)
    sin_ref[...] = jnp.where(lane % HEAD_DIM < half, -sine, sine)
    for copy in copies[2:6]:
        copy.wait()
    project_body(own_ref[...], [wq_here[...], wk_here[...], wv_here[...]], out_ref)
    for copy in copies[6:]:
        copy.wait()


def store_kernel(part_ref, length_ref, key_ref, value_ref, *refs):
    layers, requests, block, _ = key_ref.shape
    sent_refs = refs[:layers]
    key_out, value_out, token_ref, key_here, value_here, sems = refs[layers:]
    token_ref[...] = jnp.zeros_like(token_ref)
    fresh = length_ref[...] - lax.axis_index("seq") * block
    slot = lax.broadcasted_iota(jnp.int32, (block, LANES), 0)
    row = lax.broadcasted_iota(jnp.int32, (requests, LANES), 0)
    quarter_here = lane_ids((requests, LANES)) // QUARTER
    copies = []
    for layer in range(layers):
        members, _, span = sent_refs[layer].shape
        per = requests // members
        for member in range(members):
            sent = sent_refs[layer][position_of(member, members), :, span - LANES :]
            sent = sent.astype(jnp.float32)
            wide = jnp.zeros((requests, LANES), jnp.float32)
            for quarter in range(4):
                shifted = pltpu.roll(sent, (QUARTER * quarter - NEW_AT) % LANES, 1)
                wide = jnp.where((quarter_here == quarter) & (row % 4 == quarter), shifted, wide)
            for r in range(per):
                b = member * per + r
                here = slot == fresh[b : b + 1]
                for i, (old, new_here) in enumerate([(key_ref, key_here), (value_ref, value_here)]):
                    j = 4 * (2 * r + i)
                    new = jnp.sum(wide[j : j + 4], axis=0, keepdims=True)
                    kept = jnp.where(here, new, old[layer, b].astype(jnp.float32))
                    new_here[layer, b] = kept.astype(jnp.bfloat16)
        for i, (here, out) in enumerate([(key_here, key_out), (value_here, value_out)]):
            copies.append(
                pltpu.make_async_copy(here.at[layer], out.at[layer], sems.at[2 * layer + i])
            )
            copies[-1].start()
    for copy in copies:
        copy.wait()


def sum_parts(base_ref, part_refs):
    total = part_refs[0][...]
    for ref in part_refs[1:]:
        total = total + ref[...]
    return (base_ref[...].astype(jnp.float32) + total).astype(jnp.bfloat16)


def next_kernel(layer, n_parts, *refs):
    base_ref, parts = refs[0], refs[1 : 1 + n_parts]
    wq_ref, wk_ref, wv_ref, own_ref, out_ref = refs[1 + n_parts :]
    own = sum_parts(base_ref, parts)
    own_ref[...] = own
    project_body(own, [w[layer] for w in (wq_ref, wk_ref, wv_ref)], out_ref)


def half_of(value, core):
    middle = value.shape[1] // 2
    return jnp.where(core == 0, value[:, :middle], value[:, middle:])


def meet_kernel(n_tp, mid_ref, keep_ref, got_ref, out_ref):
    place = lax.axis_index("tp")
    total = keep_ref[...] + got_ref[...]
    base = half_of(mid_ref[...].astype(jnp.float32), place % 2)
    total = (total + jnp.where(place < 2, base, 0.0)).astype(jnp.bfloat16)
    for member in range(out_ref.shape[0]):
        out_ref[member] = total


def last_kernel(n_tp, got_ref, out_ref):
    span = got_ref.shape[2]
    order = whole_order(got_ref.shape[0] // n_tp, n_tp)
    for block in range(got_ref.shape[0] // n_tp):
        for core in range(2):
            total = got_ref[order.index(block * n_tp + core)].astype(jnp.float32)
            for pair in range(1, n_tp // 2):
                total = total + got_ref[order.index(block * n_tp + 2 * pair + core)].astype(jnp.float32)
            at = (2 * block + core) * span
            out_ref[:, at : at + span] = total.astype(jnp.bfloat16)


def attend_kernel(
    layer, width, heads, kv_heads, got_ref, cos_ref, sin_ref, length_ref,
    key_ref, value_ref, out_ref,
):
    members, requests, _ = got_ref.shape
    query_width = heads * HEAD_DIM
    repeat = heads // kv_heads
    block = key_ref.shape[2]
    per = requests // members
    place = lax.axis_index("seq")

    def summed(at):
        total = got_ref[0, :, at : at + LANES].astype(jnp.float32)
        for member in range(1, members):
            total = total + got_ref[member, :, at : at + LANES].astype(jnp.float32)
        return total

    lane = lane_ids((requests, LANES))
    low = lane < HEAD_DIM
    fresh_sums = summed(query_width)
    spread = (fresh_sums[2 * per : 2 * per + 1] + fresh_sums[2 * per + 1 : 2 * per + 2]) * (
        1.0 / width
    )
    inv_line = lax.rsqrt(spread + eps_norm)
    inv = to_column(inv_line, requests)
    half = HEAD_DIM // 2

    def rotated(x, cosine, sine):
        first = lane_ids(x.shape) % HEAD_DIM < half
        other = jnp.where(first, pltpu.roll(x, LANES - half, 1), pltpu.roll(x, half, 1))
        return x * cosine + other * sine

    stacked = []
    for pair in range(heads // 2):
        x = rotated(summed(pair * LANES) * inv, cos_ref[...], sin_ref[...])
        turned = pltpu.roll(x, HEAD_DIM, 1)
        if 2 * pair // repeat == 0:
            stacked += [jnp.where(low, x, 0.0), jnp.where(low, turned, 0.0)]
        else:
            stacked += [jnp.where(low, 0.0, turned), jnp.where(low, 0.0, x)]
    query = jnp.concatenate(stacked, axis=0).astype(jnp.bfloat16).astype(jnp.float32)
    query = query * (1.0 / math.sqrt(HEAD_DIM))

    request = lax.broadcasted_iota(jnp.int32, (requests, LANES), 0)
    key_new = jnp.zeros((requests, LANES), jnp.float32)
    value_new = jnp.zeros((requests, LANES), jnp.float32)
    rows = []
    for r in range(per):
        at = place * per + r
        scale = jnp.sum(
            jnp.where(lane_ids((1, LANES)) == at, inv_line, 0.0), axis=1, keepdims=True
        )
        key = rotated(
            fresh_sums[2 * r : 2 * r + 1] * scale, cos_ref[pl.ds(at, 1)], sin_ref[pl.ds(at, 1)]
        )
        key = key.astype(jnp.bfloat16).astype(jnp.float32)
        value = (fresh_sums[2 * r + 1 : 2 * r + 2] * scale).astype(jnp.bfloat16).astype(jnp.float32)
        key_new = jnp.where(request == at, key, key_new)
        value_new = jnp.where(request == at, value, value_new)
        rows += [key, value]
    owned = jnp.concatenate([request // per == place] * heads, axis=0)

    def per_head(x):
        return jnp.concatenate([x] * heads, axis=0)

    fresh_scores = jnp.sum(query * per_head(key_new), axis=1, keepdims=True)
    owned_row = owned[:, 0:1]
    fresh_scores = jnp.where(owned_row, fresh_scores, neg_fill)

    keys = key_ref[layer].reshape(requests * block, LANES)
    values = value_ref[layer].reshape(requests * block, LANES)
    scores = lax.dot_general(
        query.astype(jnp.bfloat16),
        keys,
        (((1,), (1,)), ((), ())),
        preferred_element_type=jnp.float32,
    )
    begin = request * block
    end = begin + jnp.clip(length_ref[...] - place * block, 0, block)
    copies = scores.shape[1] // LANES
    begin = jnp.concatenate([per_head(begin)] * copies, axis=1)
    end = jnp.concatenate([per_head(end)] * copies, axis=1)
    column = lane_ids(scores.shape)
    live = (column >= begin) & (column < end)
    scores = jnp.where(live, scores, neg_fill)
    top = jnp.maximum(jnp.max(scores, axis=1, keepdims=True), fresh_scores)
    top = jnp.maximum(top, 0.5 * neg_fill)
    weights = jnp.exp(scores - top)
    fresh_weights = jnp.exp(fresh_scores - top)
    sums = jnp.sum(weights, axis=1, keepdims=True) + fresh_weights
    acc = dot32(weights.astype(jnp.bfloat16), values)
    acc = acc + fresh_weights.astype(jnp.bfloat16).astype(jnp.float32) * per_head(value_new)
    turned = pltpu.roll(acc, HEAD_DIM, 1)

    side = jnp.zeros((requests, LANES), jnp.float32)
    for h in range(heads):
        part = slice(h * requests, (h + 1) * requests)
        for group in range(5):
            side = jnp.where(lane == group * heads + h, (top if group < 3 else sums)[part], side)
    spare = jnp.zeros((requests, LANES), jnp.float32)
    for j, line in enumerate(rows):
        spare = jnp.where(request // 4 == j, line, spare)
    for quarter in range(4):
        shifted = pltpu.roll(spare, (NEW_AT - QUARTER * quarter) % LANES, 1)
        side = jnp.where(
            (lane >= NEW_AT) & (lane < NEW_AT + QUARTER) & (request % 4 == quarter), shifted, side
        )
    one = side.astype(jnp.bfloat16).astype(jnp.float32)
    two = (side - one).astype(jnp.bfloat16).astype(jnp.float32)
    three = side - one - two
    second = ((lane >= heads) & (lane < 2 * heads)) | ((lane >= 4 * heads) & (lane < 5 * heads))
    third = (lane >= 2 * heads) & (lane < 3 * heads)
    side = jnp.where(third, three, jnp.where(second, two, one)).astype(jnp.bfloat16)
    pieces = []
    for pair in range(heads // 2):
        even = slice(2 * pair * requests, (2 * pair + 1) * requests)
        odd = slice((2 * pair + 1) * requests, (2 * pair + 2) * requests)
        if 2 * pair // repeat == 0:
            pieces.append(jnp.where(low, acc[even], turned[odd]).astype(jnp.bfloat16))
        else:
            pieces.append(jnp.where(low, turned[even], acc[odd]).astype(jnp.bfloat16))
    pieces.append(side)
    for member in range(members):
        for i, piece in enumerate(pieces):
            out_ref[member, :, i * LANES : (i + 1) * LANES] = piece


def combine_kernel(layer, heads, got_ref, w_ref, out_ref):
    members, requests, _ = got_ref.shape
    query_width = heads * HEAD_DIM
    low = lane_ids((requests, LANES)) < HEAD_DIM
    sides = [
        got_ref[m, :, query_width : query_width + LANES].astype(jnp.float32) for m in range(members)
    ]
    tops = [
        s[:, :heads] + s[:, heads : 2 * heads] + s[:, 2 * heads : 3 * heads] for s in sides
    ]
    sums = [s[:, 3 * heads : 4 * heads] + s[:, 4 * heads : 5 * heads] for s in sides]
    top = tops[0]
    for t in tops[1:]:
        top = jnp.maximum(top, t)
    factors = [jnp.exp(t - top) for t in tops]
    total = factors[0] * sums[0]
    for f, s in zip(factors[1:], sums[1:]):
        total = total + f * s

    def spread(column, pair):
        return jnp.where(low, column[:, 2 * pair : 2 * pair + 1], column[:, 2 * pair + 1 : 2 * pair + 2])

    attended = []
    for pair in range(heads // 2):
        acc = jnp.zeros((requests, LANES), jnp.float32)
        for m in range(members):
            piece = got_ref[m, :, pair * LANES : (pair + 1) * LANES].astype(jnp.float32)
            acc = acc + piece * spread(factors[m], pair)
        attended.append((acc / spread(total, pair)).astype(jnp.bfloat16))
    out_ref[...] = dot32(jnp.concatenate(attended, axis=1), w_ref[layer])


def widen_kernel(layer, n_parts, *refs):
    base_ref, parts = refs[0], refs[1 : 1 + n_parts]
    gate_ref, up_ref = refs[1 + n_parts : 3 + n_parts]
    mid_ref, out_ref = refs[-2:]
    mid = sum_parts(base_ref, parts)
    mid_ref[...] = mid
    side = as_hi_lo(square_sum(mid), lane_ids((mid.shape[0], LANES)))
    members = out_ref.shape[0]
    own = gate_ref.shape[2] // members
    for member in range(members):
        cols = slice(member * own, (member + 1) * own)
        place = position_of(member, members)
        out_ref[place, :, :own] = dot32(mid, gate_ref[layer, :, cols]).astype(jnp.bfloat16)
        out_ref[place, :, own : 2 * own] = dot32(mid, up_ref[layer, :, cols]).astype(jnp.bfloat16)
        out_ref[place, :, 2 * own :] = side


def silu_kernel(width, got_ref, out_ref):
    members, _, span = got_ref.shape
    own = (span - LANES) // 2
    total = got_ref[0].astype(jnp.float32)
    for member in range(1, members):
        total = total + got_ref[member].astype(jnp.float32)
    spread = (total[:, 2 * own : 2 * own + 1] + total[:, 2 * own + 1 : 2 * own + 2]) * (1.0 / width)
    inv = lax.rsqrt(spread + eps_norm)
    gate = total[:, :own] * inv
    hidden = (gate / (1.0 + jnp.exp(-gate)) * (total[:, own : 2 * own] * inv)).astype(jnp.bfloat16)
    for member in range(members):
        out_ref[member] = hidden


def in_order(got_ref):
    members = got_ref.shape[0]
    return jnp.concatenate([got_ref[position_of(m, members)] for m in range(members)], axis=1)


def down_kernel(layer, got_ref, w_ref, out_ref):
    hidden = in_order(got_ref)
    out_ref[...] = dot32(hidden, w_ref[layer])


def down_last_kernel(layer, got_ref, w_ref, keep_ref, give_ref):
    hidden = in_order(got_ref)
    part = dot32(hidden, w_ref[layer])
    core = lax.axis_index("tp") % 2
    keep_ref[...] = half_of(part, core)
    give_ref[...] = half_of(part, 1 - core)


def make_with_kernels(n_seq, n_tp):
    groups = [[s * n_tp + t for s in member_order(n_seq, t % 2 == 1)] for t in range(n_tp)]

    def swap(chunks):
        return lax.all_to_all(chunks, ("seq", "tp"), 0, 0, axis_index_groups=groups)

    def tp_parts(part):
        got = [
            lax.ppermute(part, "tp", [(i, (i + k) % n_tp) for i in range(n_tp)])
            for k in range(1, n_tp)
        ]
        return [part] + got

    def per_device(
        hidden_in,
        lengths,
        positions,
        query_weight,
        key_weight,
        value_weight,
        out_weight,
        gate_weight,
        up_weight,
        down_weight,
        key_cache,
        value_cache,
    ):
        requests, width = hidden_in.shape
        col_count = out_weight.shape[2]
        kv_width = key_cache.shape[3]
        query_width = query_weight.shape[2]
        heads = query_width // HEAD_DIM
        kv_heads = kv_width // HEAD_DIM
        ff_own = gate_weight.shape[2] // n_seq
        bf16, f32 = jnp.bfloat16, jnp.float32

        def shape(dims, kind):
            return pltpu.VMEM(dims, kind)

        packed_shape = shape((n_seq, requests, query_width + LANES), bf16)
        part_shape = shape((requests, col_count), f32)
        own_shape = shape((requests, col_count), bf16)
        sent = []
        packed_weights = (query_weight, key_weight, value_weight)
        table_shape = (requests, LANES)
        stored = (key_cache, value_cache, out_weight, gate_weight, up_weight)
        own, cosine, sine, length_table, packed, *early = call(
            functools.partial(first_kernel, len(stored)),
            (
                own_shape,
                shape(table_shape, f32),
                shape(table_shape, f32),
                shape(table_shape, jnp.int32),
                packed_shape,
            )
            + tuple(shape((1,) + a.shape[1:], bf16) for a in stored),
            hidden_in,
            lengths,
            positions,
            *packed_weights,
            *stored,
            name="first",
            held=0,
            scratch=[pltpu.VMEM(w.shape[1:], bf16) for w in packed_weights]
            + [pltpu.SMEM((requests,), jnp.int32)] * 2
            + [pltpu.SemaphoreType.DMA((6 + len(stored),))],
        )
        parts = None
        mid = None
        for layer in range(LAYERS):
            if layer > 0:
                own, packed = call(
                    functools.partial(next_kernel, layer, n_tp),
                    (own_shape, packed_shape),
                    mid,
                    *parts,
                    *packed_weights,
                    name="next",
                )
            keys, values, out_here, gate_here, up_here = early if layer == 0 else stored
            packed = call(
                functools.partial(attend_kernel, layer, width, heads, kv_heads),
                packed_shape,
                swap(packed),
                cosine,
                sine,
                length_table,
                keys,
                values,
                name="attend",
            )
            sent.append(swap(packed))
            part = call(
                functools.partial(combine_kernel, layer, heads),
                part_shape,
                sent[-1],
                out_here,
                name="combine",
            )
            parts = tp_parts(part)
            tokens = []
            if layer + 1 == LAYERS:
                cache_shape = jax.ShapeDtypeStruct(key_cache.shape, bf16)
                hbm = pl.BlockSpec(memory_space=pltpu.HBM)
                key_out, value_out, token = call(
                    store_kernel,
                    (cache_shape, cache_shape, shape((8, LANES), f32)),
                    part,
                    length_table,
                    key_cache,
                    value_cache,
                    *sent,
                    name="store",
                    out_specs=[hbm, hbm, pl.BlockSpec(memory_space=pltpu.VMEM)],
                    scratch=[pltpu.VMEM(key_cache.shape, bf16)] * 2
                    + [pltpu.SemaphoreType.DMA((2 * LAYERS,))],
                )
                tokens = [token]
            mid, packed = call(
                functools.partial(widen_kernel, layer, n_tp),
                (own_shape, shape((n_seq, requests, 2 * ff_own + LANES), bf16)),
                own,
                *parts,
                gate_here,
                up_here,
                *tokens,
                name="widen",
            )
            hidden = call(
                functools.partial(silu_kernel, width),
                shape((n_seq, requests, ff_own), bf16),
                swap(packed),
                name="silu",
            )
            hidden = swap(hidden)
            if layer + 1 < LAYERS:
                part = call(
                    functools.partial(down_kernel, layer), part_shape, hidden, down_weight, name="down"
                )
                parts = tp_parts(part)
        half_shape = shape((requests, col_count // 2), f32)
        keep, give = call(
            functools.partial(down_last_kernel, LAYERS - 1),
            (half_shape, half_shape),
            hidden,
            down_weight,
            name="down_last",
        )
        give = lax.ppermute(give, "tp", [(i, i ^ 1) for i in range(n_tp)])
        stream = call(
            functools.partial(meet_kernel, n_tp),
            shape((n_seq * n_tp, requests, col_count // 2), bf16),
            mid,
            keep,
            give,
            name="meet",
        )
        everyone = [whole_order(n_seq, n_tp)]
        stream = lax.all_to_all(stream, ("seq", "tp"), 0, 0, axis_index_groups=everyone)
        stream = call(
            functools.partial(last_kernel, n_tp),
            jax.ShapeDtypeStruct((requests, width), bf16),
            stream,
            name="last",
        )
        return (stream, key_out, value_out)

    return per_device


def solution(mesh):
    n_seq, n_tp = mesh.shape["seq"], mesh.shape["tp"]

    def per_device(*args):
        gate_weight, key_cache = args[7], args[10]
        aligned = (
            args[6].shape[2] % (2 * LANES) == 0
            and n_tp % 2 == 0
            and gate_weight.shape[2] // n_seq % LANES == 0
            and key_cache.shape[3] == LANES
            and args[0].shape[0] == 2 * n_seq
        )
        make = make_with_kernels if aligned else make_plain
        return make(n_seq, n_tp)(*args)

    return jax.shard_map(
        per_device,
        mesh=mesh,
        in_specs=(
            P(),
            P(),
            P(),
            P(None, "seq", "tp"),
            P(None, "seq", "tp"),
            P(None, "seq", "tp"),
            P(None, "tp", "seq"),
            P(None, "seq", "tp"),
            P(None, "seq", "tp"),
            P(None, "tp", "seq"),
            P(None, None, "seq", "tp"),
            P(None, None, "seq", "tp"),
        ),
        out_specs=(P(), P(None, None, "seq", "tp"), P(None, None, "seq", "tp")),
        check_vma=False,
    )
```

```python
import functools
import math

import jax
import jax.numpy as jnp
from jax import lax
from jax.experimental import pallas as pl
from jax.experimental.pallas import tpu as pltpu
from jax.sharding import PartitionSpec as P

HEAD_DIM = 64
LAYERS = 2
eps_norm = 1e-05
neg_fill = -1e30


def split_hi_lo(value, parts):
    out = []
    rest = value
    for _ in range(parts):
        head = lax.reduce_precision(rest, 8, 7)
        out.append(head.astype(jnp.bfloat16))
        rest = rest - head
    return out


def seq_swap(chunks):
    return lax.all_to_all(chunks, "seq", 0, 0)


def make_plain(n_seq, n_tp):
    def tp_sum(part):
        total = part
        for k in range(1, n_tp):
            total = total + lax.ppermute(part, "tp", [(i, (i + k) % n_tp) for i in range(n_tp)])
        return total

    def per_device(
        hidden_in,
        lengths,
        positions,
        query_weight,
        key_weight,
        value_weight,
        out_weight,
        gate_weight,
        up_weight,
        down_weight,
        key_cache,
        value_cache,
    ):
        seq_index = lax.axis_index("seq")
        requests, width = hidden_in.shape
        col_count = out_weight.shape[2]
        col_start = seq_index * col_count
        block_len = key_cache.shape[2]
        kv_width = key_cache.shape[3]
        query_width = query_weight.shape[2]
        heads = query_width // HEAD_DIM
        kv_heads = kv_width // HEAD_DIM
        repeat = heads // kv_heads
        ff_here = gate_weight.shape[2]
        ff_own = ff_here // n_seq
        scale = 1.0 / math.sqrt(HEAD_DIM)
        slots = seq_index * block_len + jnp.arange(block_len, dtype=jnp.int32)
        new_slot = (slots[None, :] == lengths[:, None])[:, :, None]
        live = (slots[None, :] <= lengths[:, None])[:, None, None, :]

        half = HEAD_DIM // 2
        inverse = 500000.0 ** (-(2.0 * jnp.arange(half, dtype=jnp.float32)) / HEAD_DIM)
        angles = positions.astype(jnp.float32)[:, None] * inverse[None, :]
        cosine = jnp.cos(angles)[:, None, :]
        sine = jnp.sin(angles)[:, None, :]

        def rotate(x):
            a, b = x[..., :half], x[..., half:]
            return jnp.concatenate([a * cosine - b * sine, b * cosine + a * sine], axis=-1)

        def stats_of(x):
            f = x.astype(jnp.float32)
            return jnp.sum(f * f, axis=-1, keepdims=True)

        def pad_lanes(cols):
            joined = jnp.concatenate(cols, axis=-1)
            return jnp.pad(joined, ((0, 0), (0, -joined.shape[-1] % 128)))

        own = lax.dynamic_slice_in_dim(hidden_in, col_start, col_count, 1)
        key_layers = []
        value_layers = []
        for layer in range(LAYERS):
            part = jnp.concatenate(
                [
                    jnp.dot(own, w[layer], preferred_element_type=jnp.float32)
                    for w in (query_weight, key_weight, value_weight)
                ],
                axis=1,
            ).astype(jnp.bfloat16)
            packed = jnp.concatenate([part, pad_lanes(split_hi_lo(stats_of(own), 2))], axis=1)
            got = seq_swap(jnp.broadcast_to(packed[None], (n_seq,) + packed.shape))
            got = jnp.sum(got.astype(jnp.float32), axis=0)
            qkv = query_width + 2 * kv_width
            spread = (got[:, qkv : qkv + 1] + got[:, qkv + 1 : qkv + 2]) / width
            got = got[:, :qkv] * lax.rsqrt(spread + eps_norm)
            query = rotate(got[:, :query_width].reshape(requests, heads, HEAD_DIM))
            query = query.astype(jnp.bfloat16).reshape(requests, kv_heads, repeat, HEAD_DIM)
            key_new = rotate(
                got[:, query_width : query_width + kv_width].reshape(requests, kv_heads, HEAD_DIM)
            )
            key_new = key_new.astype(jnp.bfloat16).reshape(requests, kv_width)
            value_new = got[:, query_width + kv_width :].astype(jnp.bfloat16)
            key_rows = jnp.where(new_slot, key_new[:, None, :], key_cache[layer])
            value_rows = jnp.where(new_slot, value_new[:, None, :], value_cache[layer])
            key_layers.append(key_rows)
            value_layers.append(value_rows)
            key_heads = key_rows.reshape(requests, block_len, kv_heads, HEAD_DIM)
            value_heads = value_rows.reshape(requests, block_len, kv_heads, HEAD_DIM)
            scores = (
                jnp.einsum("bkrd,bskd->bkrs", query, key_heads, preferred_element_type=jnp.float32)
                * scale
            )
            scores = jnp.where(live, scores, neg_fill)
            top = jnp.max(scores, axis=3)
            weights = jnp.where(live, jnp.exp(scores - top[..., None]), 0.0)
            sums = jnp.sum(weights, axis=3)
            acc = jnp.einsum(
                "bkrs,bskd->bkrd",
                weights.astype(jnp.bfloat16),
                value_heads,
                preferred_element_type=jnp.float32,
            )
            packed = jnp.concatenate(
                [
                    acc.reshape(requests, query_width).astype(jnp.bfloat16),
                    pad_lanes(
                        split_hi_lo(top.reshape(requests, heads), 3)
                        + split_hi_lo(sums.reshape(requests, heads), 2)
                    ),
                ],
                axis=1,
            )
            got = seq_swap(jnp.broadcast_to(packed[None], (n_seq,) + packed.shape))
            got = got.astype(jnp.float32)
            acc = got[:, :, :query_width].reshape(n_seq, requests, heads, HEAD_DIM)
            side = got[:, :, query_width : query_width + 5 * heads].reshape(
                n_seq, requests, 5, heads
            )
            tops = side[:, :, 0] + side[:, :, 1] + side[:, :, 2]
            factor = jnp.exp(tops - jnp.max(tops, axis=0, keepdims=True))
            total = jnp.sum(factor * (side[:, :, 3] + side[:, :, 4]), axis=0)
            attended = jnp.sum(acc * factor[..., None], axis=0) / total[..., None]
            attended = attended.astype(jnp.bfloat16).reshape(requests, query_width)

            part = jnp.dot(attended, out_weight[layer], preferred_element_type=jnp.float32)
            mid = (own.astype(jnp.float32) + tp_sum(part)).astype(jnp.bfloat16)

            gate = jnp.dot(mid, gate_weight[layer], preferred_element_type=jnp.float32)
            up = jnp.dot(mid, up_weight[layer], preferred_element_type=jnp.float32)
            side = pad_lanes(split_hi_lo(stats_of(mid), 2))
            packed = jnp.concatenate(
                [
                    gate.astype(jnp.bfloat16).reshape(requests, n_seq, ff_own),
                    up.astype(jnp.bfloat16).reshape(requests, n_seq, ff_own),
                    jnp.broadcast_to(side[:, None], (requests, n_seq, side.shape[1])),
                ],
                axis=2,
            )
            got = seq_swap(packed.transpose(1, 0, 2))
            got = jnp.sum(got.astype(jnp.float32), axis=0)
            spread = (got[:, 2 * ff_own : 2 * ff_own + 1] + got[:, 2 * ff_own + 1 : 2 * ff_own + 2]) / width
            inv = lax.rsqrt(spread + eps_norm)
            hidden = jax.nn.silu(got[:, :ff_own] * inv) * (got[:, ff_own : 2 * ff_own] * inv)
            hidden = hidden.astype(jnp.bfloat16)
            hidden = seq_swap(jnp.broadcast_to(hidden[None], (n_seq,) + hidden.shape))
            hidden = hidden.transpose(1, 0, 2).reshape(requests, ff_here)
            part = jnp.dot(hidden, down_weight[layer], preferred_element_type=jnp.float32)
            own = (mid.astype(jnp.float32) + tp_sum(part)).astype(jnp.bfloat16)

        stream = seq_swap(jnp.broadcast_to(own[None], (n_seq,) + own.shape))
        stream = stream.transpose(1, 0, 2).reshape(requests, width)
        return (stream, jnp.stack(key_layers), jnp.stack(value_layers))

    return per_device


LANES = 128
VMEM_ROOM = 8 << 20
QUARTER = LANES // 4
NEW_AT = 2 * QUARTER


def lane_ids(shape):
    return lax.broadcasted_iota(jnp.int32, shape, len(shape) - 1)


def as_hi_lo(value, lane):
    wide = jnp.broadcast_to(value, lane.shape)
    high = wide.astype(jnp.bfloat16).astype(jnp.float32)
    return jnp.where(lane == 0, high, jnp.where(lane == 1, wide - high, 0.0)).astype(jnp.bfloat16)


def member_order(n_seq, odd):
    if n_seq != 8:
        return list(range(n_seq))
    return [3, 2, 6, 7, 5, 4, 0, 1] if odd else [0, 1, 3, 2, 6, 7, 5, 4]


def whole_order(n_seq, n_tp):
    return [s * n_tp + (t ^ (t >> 1)) for s in member_order(n_seq, False) for t in range(n_tp)]


def position_of(member, n_seq):
    even, odd = (member_order(n_seq, side).index(member) for side in (False, True))
    return jnp.where(lax.axis_index("tp") % 2 == 0, even, odd)


def square_sum(own):
    wide = own.astype(jnp.float32)
    return jnp.sum(wide * wide, axis=1, keepdims=True)


def dot32(a, b):
    return jnp.dot(a, b, preferred_element_type=jnp.float32)


def call(body, out_shape, *args, name, held=None, scratch=(), out_specs=None):
    vmem, hbm = [pl.BlockSpec(memory_space=m) for m in (pltpu.VMEM, pltpu.HBM)]
    held = len(args) if held is None else held
    single = not isinstance(out_shape, (tuple, list))
    args = [
        pltpu.with_memory_space_constraint(a, pltpu.VMEM if i < held else pltpu.HBM)
        for i, a in enumerate(args)
    ]
    return pl.pallas_call(
        body,
        out_shape=out_shape,
        in_specs=[vmem if i < held else hbm for i in range(len(args))],
        out_specs=out_specs or (vmem if single else [vmem] * len(out_shape)),
        scratch_shapes=list(scratch),
        compiler_params=pltpu.CompilerParams(vmem_limit_bytes=VMEM_ROOM),
        name=name,
    )(*args)


def to_row(column):
    shape = (column.shape[0], LANES)
    row = lax.broadcasted_iota(jnp.int32, shape, 0)
    return jnp.sum(jnp.where(lane_ids(shape) == row, column, 0.0), axis=0, keepdims=True)


def to_column(line, requests):
    shape = (requests, LANES)
    row = lax.broadcasted_iota(jnp.int32, shape, 0)
    return jnp.sum(jnp.where(lane_ids(shape) == row, line, 0.0), axis=1, keepdims=True)


def project_body(own, weights, out_ref):
    requests = own.shape[0]
    members = out_ref.shape[0]
    per = requests // members
    query, key, value = [dot32(own, w) for w in weights]
    width = query.shape[1]
    query = query.astype(jnp.bfloat16)
    line = to_row(square_sum(own))
    high = line.astype(jnp.bfloat16).astype(jnp.float32)
    row = lax.broadcasted_iota(jnp.int32, (requests, LANES), 0)
    base = jnp.where(row == 2 * per, high, jnp.where(row == 2 * per + 1, line - high, 0.0))
    for member in range(members):
        block = base
        for r in range(per):
            at = member * per + r
            block = jnp.where(row == 2 * r, key[at : at + 1], block)
            block = jnp.where(row == 2 * r + 1, value[at : at + 1], block)
        place = position_of(member, members)
        out_ref[place, :, :width] = query
        out_ref[place, :, width:] = block.astype(jnp.bfloat16)


def first_kernel(n_more, *refs):
    hidden_ref, length_ref, position_ref, wq_ref, wk_ref, wv_ref = refs[:6]
    more = refs[6 : 6 + n_more]
    own_ref, cos_ref, sin_ref, table_ref, out_ref = refs[6 + n_more : 11 + n_more]
    more_here = refs[11 + n_more : 11 + 2 * n_more]
    wq_here, wk_here, wv_here, lengths, positions, sems = refs[11 + 2 * n_more :]
    span = own_ref.shape[1]
    start = pl.multiple_of(lax.axis_index("seq") * span, LANES)
    copies = [
        pltpu.make_async_copy(position_ref, positions, sems.at[0]),
        pltpu.make_async_copy(length_ref, lengths, sems.at[1]),
        pltpu.make_async_copy(hidden_ref.at[:, pl.ds(start, span)], own_ref, sems.at[2]),
        pltpu.make_async_copy(wq_ref.at[0], wq_here, sems.at[3]),
        pltpu.make_async_copy(wk_ref.at[0], wk_here, sems.at[4]),
        pltpu.make_async_copy(wv_ref.at[0], wv_here, sems.at[5]),
    ]
    copies += [
        pltpu.make_async_copy(ref.at[0], here.at[0], sems.at[6 + i])
        for i, (ref, here) in enumerate(zip(more, more_here))
    ]
    for copy in copies:
        copy.start()
    copies[0].wait()
    copies[1].wait()
    half = HEAD_DIM // 2
    lane = lane_ids(table_ref.shape)
    row = lax.broadcasted_iota(jnp.int32, table_ref.shape, 0)
    place = jnp.zeros(table_ref.shape, jnp.int32)
    length = jnp.zeros(table_ref.shape, jnp.int32)
    for b in range(table_ref.shape[0]):
        place = jnp.where(row == b, positions[b], place)
        length = jnp.where(row == b, lengths[b], length)
    inverse = jnp.zeros(table_ref.shape, jnp.float32)
    for i in range(half):
        inverse = jnp.where(lane % half == i, 500000.0 ** (-2.0 * i / HEAD_DIM), inverse)
    angles = place.astype(jnp.float32) * inverse
    sine = jnp.sin(angles)
    table_ref[...] = length
    cos_ref[...] = jnp.cos(angles)
    sin_ref[...] = jnp.where(lane % HEAD_DIM < half, -sine, sine)
    for copy in copies[2:6]:
        copy.wait()
    project_body(own_ref[...], [wq_here[...], wk_here[...], wv_here[...]], out_ref)
    for copy in copies[6:]:
        copy.wait()


def load_kernel(n_more, *refs):
    more, more_here, sems = refs[1 : 1 + n_more], refs[1 + n_more : 1 + 2 * n_more], refs[-1]
    copies = [
        pltpu.make_async_copy(ref.at[0], here.at[0], sems.at[i])
        for i, (ref, here) in enumerate(zip(more, more_here))
    ]
    for copy in copies:
        copy.start()
    for copy in copies:
        copy.wait()


def store_kernel(part_ref, length_ref, key_ref, value_ref, *refs):
    layers, requests, block, _ = key_ref.shape
    sent_refs = refs[:layers]
    key_out, value_out, token_ref, key_here, value_here, sems = refs[layers:]
    token_ref[...] = jnp.zeros_like(token_ref)
    fresh = length_ref[...] - lax.axis_index("seq") * block
    slot = lax.broadcasted_iota(jnp.int32, (block, LANES), 0)
    row = lax.broadcasted_iota(jnp.int32, (requests, LANES), 0)
    quarter_here = lane_ids((requests, LANES)) // QUARTER
    copies = []
    for layer in range(layers):
        members, _, span = sent_refs[layer].shape
        per = requests // members
        for member in range(members):
            sent = sent_refs[layer][position_of(member, members), :, span - LANES :]
            sent = sent.astype(jnp.float32)
            wide = jnp.zeros((requests, LANES), jnp.float32)
            for quarter in range(4):
                shifted = pltpu.roll(sent, (QUARTER * quarter - NEW_AT) % LANES, 1)
                wide = jnp.where((quarter_here == quarter) & (row % 4 == quarter), shifted, wide)
            for r in range(per):
                b = member * per + r
                here = slot == fresh[b : b + 1]
                for i, (old, new_here) in enumerate([(key_ref, key_here), (value_ref, value_here)]):
                    j = 4 * (2 * r + i)
                    new = jnp.sum(wide[j : j + 4], axis=0, keepdims=True)
                    kept = jnp.where(here, new, old[layer, b].astype(jnp.float32))
                    new_here[layer, b] = kept.astype(jnp.bfloat16)
        for i, (here, out) in enumerate([(key_here, key_out), (value_here, value_out)]):
            copies.append(
                pltpu.make_async_copy(here.at[layer], out.at[layer], sems.at[2 * layer + i])
            )
            copies[-1].start()
    for copy in copies:
        copy.wait()


def sum_parts(base_ref, part_refs):
    total = part_refs[0][...]
    for ref in part_refs[1:]:
        total = total + ref[...]
    return (base_ref[...].astype(jnp.float32) + total).astype(jnp.bfloat16)


def next_kernel(layer, n_parts, *refs):
    base_ref, parts = refs[0], refs[1 : 1 + n_parts]
    wq_ref, wk_ref, wv_ref, own_ref, out_ref = refs[1 + n_parts :]
    own = sum_parts(base_ref, parts)
    own_ref[...] = own
    project_body(own, [w[layer] for w in (wq_ref, wk_ref, wv_ref)], out_ref)


def half_of(value, core):
    middle = value.shape[1] // 2
    return jnp.where(core == 0, value[:, :middle], value[:, middle:])


def meet_kernel(n_tp, mid_ref, keep_ref, got_ref, out_ref):
    place = lax.axis_index("tp")
    total = keep_ref[...] + got_ref[...]
    base = half_of(mid_ref[...].astype(jnp.float32), place % 2)
    total = (total + jnp.where(place < 2, base, 0.0)).astype(jnp.bfloat16)
    for member in range(out_ref.shape[0]):
        out_ref[member] = total


def last_kernel(n_tp, got_ref, out_ref):
    span = got_ref.shape[2]
    order = whole_order(got_ref.shape[0] // n_tp, n_tp)
    for block in range(got_ref.shape[0] // n_tp):
        for core in range(2):
            total = got_ref[order.index(block * n_tp + core)].astype(jnp.float32)
            for pair in range(1, n_tp // 2):
                total = total + got_ref[order.index(block * n_tp + 2 * pair + core)].astype(jnp.float32)
            at = (2 * block + core) * span
            out_ref[:, at : at + span] = total.astype(jnp.bfloat16)


def attend_kernel(
    layer, width, heads, kv_heads, got_ref, cos_ref, sin_ref, length_ref,
    key_ref, value_ref, out_ref,
):
    members, requests, _ = got_ref.shape
    query_width = heads * HEAD_DIM
    repeat = heads // kv_heads
    block = key_ref.shape[2]
    per = requests // members
    place = lax.axis_index("seq")

    def summed(at):
        total = got_ref[0, :, at : at + LANES].astype(jnp.float32)
        for member in range(1, members):
            total = total + got_ref[member, :, at : at + LANES].astype(jnp.float32)
        return total

    lane = lane_ids((requests, LANES))
    low = lane < HEAD_DIM
    fresh_sums = summed(query_width)
    spread = (fresh_sums[2 * per : 2 * per + 1] + fresh_sums[2 * per + 1 : 2 * per + 2]) * (
        1.0 / width
    )
    inv_line = lax.rsqrt(spread + eps_norm)
    inv = to_column(inv_line, requests)
    half = HEAD_DIM // 2

    def rotated(x, cosine, sine):
        first = lane_ids(x.shape) % HEAD_DIM < half
        other = jnp.where(first, pltpu.roll(x, LANES - half, 1), pltpu.roll(x, half, 1))
        return x * cosine + other * sine

    stacked = []
    for pair in range(heads // 2):
        x = rotated(summed(pair * LANES) * inv, cos_ref[...], sin_ref[...])
        turned = pltpu.roll(x, HEAD_DIM, 1)
        if 2 * pair // repeat == 0:
            stacked += [jnp.where(low, x, 0.0), jnp.where(low, turned, 0.0)]
        else:
            stacked += [jnp.where(low, 0.0, turned), jnp.where(low, 0.0, x)]
    query = jnp.concatenate(stacked, axis=0).astype(jnp.bfloat16).astype(jnp.float32)
    query = query * (1.0 / math.sqrt(HEAD_DIM))

    request = lax.broadcasted_iota(jnp.int32, (requests, LANES), 0)
    key_new = jnp.zeros((requests, LANES), jnp.float32)
    value_new = jnp.zeros((requests, LANES), jnp.float32)
    rows = []
    for r in range(per):
        at = place * per + r
        scale = jnp.sum(
            jnp.where(lane_ids((1, LANES)) == at, inv_line, 0.0), axis=1, keepdims=True
        )
        key = rotated(
            fresh_sums[2 * r : 2 * r + 1] * scale, cos_ref[pl.ds(at, 1)], sin_ref[pl.ds(at, 1)]
        )
        key = key.astype(jnp.bfloat16).astype(jnp.float32)
        value = (fresh_sums[2 * r + 1 : 2 * r + 2] * scale).astype(jnp.bfloat16).astype(jnp.float32)
        key_new = jnp.where(request == at, key, key_new)
        value_new = jnp.where(request == at, value, value_new)
        rows += [key, value]
    owned = jnp.concatenate([request // per == place] * heads, axis=0)

    def per_head(x):
        return jnp.concatenate([x] * heads, axis=0)

    fresh_scores = jnp.sum(query * per_head(key_new), axis=1, keepdims=True)
    owned_row = owned[:, 0:1]
    fresh_scores = jnp.where(owned_row, fresh_scores, neg_fill)

    keys = key_ref[layer].reshape(requests * block, LANES)
    values = value_ref[layer].reshape(requests * block, LANES)
    scores = lax.dot_general(
        query.astype(jnp.bfloat16),
        keys,
        (((1,), (1,)), ((), ())),
        preferred_element_type=jnp.float32,
    )
    begin = request * block
    end = begin + jnp.clip(length_ref[...] - place * block, 0, block)
    copies = scores.shape[1] // LANES
    begin = jnp.concatenate([per_head(begin)] * copies, axis=1)
    end = jnp.concatenate([per_head(end)] * copies, axis=1)
    column = lane_ids(scores.shape)
    live = (column >= begin) & (column < end)
    scores = jnp.where(live, scores, neg_fill)
    top = jnp.maximum(jnp.max(scores, axis=1, keepdims=True), fresh_scores)
    top = jnp.maximum(top, 0.5 * neg_fill)
    weights = jnp.exp(scores - top)
    fresh_weights = jnp.exp(fresh_scores - top)
    sums = jnp.sum(weights, axis=1, keepdims=True) + fresh_weights
    acc = dot32(weights.astype(jnp.bfloat16), values)
    acc = acc + fresh_weights.astype(jnp.bfloat16).astype(jnp.float32) * per_head(value_new)
    turned = pltpu.roll(acc, HEAD_DIM, 1)

    side = jnp.zeros((requests, LANES), jnp.float32)
    for h in range(heads):
        part = slice(h * requests, (h + 1) * requests)
        for group in range(5):
            side = jnp.where(lane == group * heads + h, (top if group < 3 else sums)[part], side)
    spare = jnp.zeros((requests, LANES), jnp.float32)
    for j, line in enumerate(rows):
        spare = jnp.where(request // 4 == j, line, spare)
    for quarter in range(4):
        shifted = pltpu.roll(spare, (NEW_AT - QUARTER * quarter) % LANES, 1)
        side = jnp.where(
            (lane >= NEW_AT) & (lane < NEW_AT + QUARTER) & (request % 4 == quarter), shifted, side
        )
    one = side.astype(jnp.bfloat16).astype(jnp.float32)
    two = (side - one).astype(jnp.bfloat16).astype(jnp.float32)
    three = side - one - two
    second = ((lane >= heads) & (lane < 2 * heads)) | ((lane >= 4 * heads) & (lane < 5 * heads))
    third = (lane >= 2 * heads) & (lane < 3 * heads)
    side = jnp.where(third, three, jnp.where(second, two, one)).astype(jnp.bfloat16)
    pieces = []
    for pair in range(heads // 2):
        even = slice(2 * pair * requests, (2 * pair + 1) * requests)
        odd = slice((2 * pair + 1) * requests, (2 * pair + 2) * requests)
        if 2 * pair // repeat == 0:
            pieces.append(jnp.where(low, acc[even], turned[odd]).astype(jnp.bfloat16))
        else:
            pieces.append(jnp.where(low, turned[even], acc[odd]).astype(jnp.bfloat16))
    pieces.append(side)
    for member in range(members):
        for i, piece in enumerate(pieces):
            out_ref[member, :, i * LANES : (i + 1) * LANES] = piece


def combine_kernel(layer, heads, got_ref, w_ref, out_ref):
    members, requests, _ = got_ref.shape
    query_width = heads * HEAD_DIM
    low = lane_ids((requests, LANES)) < HEAD_DIM
    sides = [
        got_ref[m, :, query_width : query_width + LANES].astype(jnp.float32) for m in range(members)
    ]
    tops = [
        s[:, :heads] + s[:, heads : 2 * heads] + s[:, 2 * heads : 3 * heads] for s in sides
    ]
    sums = [s[:, 3 * heads : 4 * heads] + s[:, 4 * heads : 5 * heads] for s in sides]
    top = tops[0]
    for t in tops[1:]:
        top = jnp.maximum(top, t)
    factors = [jnp.exp(t - top) for t in tops]
    total = factors[0] * sums[0]
    for f, s in zip(factors[1:], sums[1:]):
        total = total + f * s

    def spread(column, pair):
        return jnp.where(low, column[:, 2 * pair : 2 * pair + 1], column[:, 2 * pair + 1 : 2 * pair + 2])

    attended = []
    for pair in range(heads // 2):
        acc = jnp.zeros((requests, LANES), jnp.float32)
        for m in range(members):
            piece = got_ref[m, :, pair * LANES : (pair + 1) * LANES].astype(jnp.float32)
            acc = acc + piece * spread(factors[m], pair)
        attended.append((acc / spread(total, pair)).astype(jnp.bfloat16))
    out_ref[...] = dot32(jnp.concatenate(attended, axis=1), w_ref[layer])


def widen_kernel(layer, n_parts, *refs):
    base_ref, parts = refs[0], refs[1 : 1 + n_parts]
    gate_ref, up_ref = refs[1 + n_parts : 3 + n_parts]
    mid_ref, out_ref = refs[-2:]
    mid = sum_parts(base_ref, parts)
    mid_ref[...] = mid
    side = as_hi_lo(square_sum(mid), lane_ids((mid.shape[0], LANES)))
    members = out_ref.shape[0]
    own = gate_ref.shape[2] // members
    for member in range(members):
        cols = slice(member * own, (member + 1) * own)
        place = position_of(member, members)
        out_ref[place, :, :own] = dot32(mid, gate_ref[layer, :, cols]).astype(jnp.bfloat16)
        out_ref[place, :, own : 2 * own] = dot32(mid, up_ref[layer, :, cols]).astype(jnp.bfloat16)
        out_ref[place, :, 2 * own :] = side


def silu_kernel(width, got_ref, out_ref):
    members, _, span = got_ref.shape
    own = (span - LANES) // 2
    total = got_ref[0].astype(jnp.float32)
    for member in range(1, members):
        total = total + got_ref[member].astype(jnp.float32)
    spread = (total[:, 2 * own : 2 * own + 1] + total[:, 2 * own + 1 : 2 * own + 2]) * (1.0 / width)
    inv = lax.rsqrt(spread + eps_norm)
    gate = total[:, :own] * inv
    hidden = (gate / (1.0 + jnp.exp(-gate)) * (total[:, own : 2 * own] * inv)).astype(jnp.bfloat16)
    for member in range(members):
        out_ref[member] = hidden


def in_order(got_ref):
    members = got_ref.shape[0]
    return jnp.concatenate([got_ref[position_of(m, members)] for m in range(members)], axis=1)


def down_kernel(layer, got_ref, w_ref, out_ref):
    hidden = in_order(got_ref)
    out_ref[...] = dot32(hidden, w_ref[layer])


def down_last_kernel(layer, got_ref, w_ref, keep_ref, give_ref):
    hidden = in_order(got_ref)
    part = dot32(hidden, w_ref[layer])
    core = lax.axis_index("tp") % 2
    keep_ref[...] = half_of(part, core)
    give_ref[...] = half_of(part, 1 - core)


def make_with_kernels(n_seq, n_tp):
    groups = [[s * n_tp + t for s in member_order(n_seq, t % 2 == 1)] for t in range(n_tp)]

    def swap(chunks):
        return lax.all_to_all(chunks, ("seq", "tp"), 0, 0, axis_index_groups=groups)

    def tp_parts(part):
        got = [
            lax.ppermute(part, "tp", [(i, (i + k) % n_tp) for i in range(n_tp)])
            for k in range(1, n_tp)
        ]
        return [part] + got

    def per_device(
        hidden_in,
        lengths,
        positions,
        query_weight,
        key_weight,
        value_weight,
        out_weight,
        gate_weight,
        up_weight,
        down_weight,
        key_cache,
        value_cache,
    ):
        requests, width = hidden_in.shape
        col_count = out_weight.shape[2]
        kv_width = key_cache.shape[3]
        query_width = query_weight.shape[2]
        heads = query_width // HEAD_DIM
        kv_heads = kv_width // HEAD_DIM
        ff_own = gate_weight.shape[2] // n_seq
        bf16, f32 = jnp.bfloat16, jnp.float32

        def shape(dims, kind):
            return pltpu.VMEM(dims, kind)

        packed_shape = shape((n_seq, requests, query_width + LANES), bf16)
        part_shape = shape((requests, col_count), f32)
        own_shape = shape((requests, col_count), bf16)
        sent = []
        packed_weights = (query_weight, key_weight, value_weight)
        table_shape = (requests, LANES)
        stored = (key_cache, value_cache, out_weight)
        wide = (gate_weight, up_weight)
        own, cosine, sine, length_table, packed, *early = call(
            functools.partial(first_kernel, len(stored)),
            (
                own_shape,
                shape(table_shape, f32),
                shape(table_shape, f32),
                shape(table_shape, jnp.int32),
                packed_shape,
            )
            + tuple(shape((1,) + a.shape[1:], bf16) for a in stored),
            hidden_in,
            lengths,
            positions,
            *packed_weights,
            *stored,
            name="first",
            held=0,
            scratch=[pltpu.VMEM(w.shape[1:], bf16) for w in packed_weights]
            + [pltpu.SMEM((requests,), jnp.int32)] * 2
            + [pltpu.SemaphoreType.DMA((6 + len(stored),))],
        )
        parts = None
        mid = None
        for layer in range(LAYERS):
            if layer > 0:
                own, packed = call(
                    functools.partial(next_kernel, layer, n_tp),
                    (own_shape, packed_shape),
                    mid,
                    *parts,
                    *packed_weights,
                    name="next",
                )
            keys, values, out_here = early if layer == 0 else stored
            packed = call(
                functools.partial(attend_kernel, layer, width, heads, kv_heads),
                packed_shape,
                swap(packed),
                cosine,
                sine,
                length_table,
                keys,
                values,
                name="attend",
            )
            sent.append(swap(packed))
            part = call(
                functools.partial(combine_kernel, layer, heads),
                part_shape,
                sent[-1],
                out_here,
                name="combine",
            )
            parts = tp_parts(part)
            gate_here, up_here = wide
            if layer == 0:
                gate_here, up_here = call(
                    functools.partial(load_kernel, len(wide)),
                    tuple(shape((1,) + a.shape[1:], bf16) for a in wide),
                    part,
                    *wide,
                    name="load",
                    held=1,
                    scratch=[pltpu.SemaphoreType.DMA((len(wide),))],
                )
            tokens = []
            if layer + 1 == LAYERS:
                cache_shape = jax.ShapeDtypeStruct(key_cache.shape, bf16)
                hbm = pl.BlockSpec(memory_space=pltpu.HBM)
                key_out, value_out, token = call(
                    store_kernel,
                    (cache_shape, cache_shape, shape((8, LANES), f32)),
                    part,
                    length_table,
                    key_cache,
                    value_cache,
                    *sent,
                    name="store",
                    out_specs=[hbm, hbm, pl.BlockSpec(memory_space=pltpu.VMEM)],
                    scratch=[pltpu.VMEM(key_cache.shape, bf16)] * 2
                    + [pltpu.SemaphoreType.DMA((2 * LAYERS,))],
                )
                tokens = [token]
            mid, packed = call(
                functools.partial(widen_kernel, layer, n_tp),
                (own_shape, shape((n_seq, requests, 2 * ff_own + LANES), bf16)),
                own,
                *parts,
                gate_here,
                up_here,
                *tokens,
                name="widen",
            )
            hidden = call(
                functools.partial(silu_kernel, width),
                shape((n_seq, requests, ff_own), bf16),
                swap(packed),
                name="silu",
            )
            hidden = swap(hidden)
            if layer + 1 < LAYERS:
                part = call(
                    functools.partial(down_kernel, layer), part_shape, hidden, down_weight, name="down"
                )
                parts = tp_parts(part)
        half_shape = shape((requests, col_count // 2), f32)
        keep, give = call(
            functools.partial(down_last_kernel, LAYERS - 1),
            (half_shape, half_shape),
            hidden,
            down_weight,
            name="down_last",
        )
        give = lax.ppermute(give, "tp", [(i, i ^ 1) for i in range(n_tp)])
        stream = call(
            functools.partial(meet_kernel, n_tp),
            shape((n_seq * n_tp, requests, col_count // 2), bf16),
            mid,
            keep,
            give,
            name="meet",
        )
        everyone = [whole_order(n_seq, n_tp)]
        stream = lax.all_to_all(stream, ("seq", "tp"), 0, 0, axis_index_groups=everyone)
        stream = call(
            functools.partial(last_kernel, n_tp),
            jax.ShapeDtypeStruct((requests, width), bf16),
            stream,
            name="last",
        )
        return (stream, key_out, value_out)

    return per_device


def solution(mesh):
    n_seq, n_tp = mesh.shape["seq"], mesh.shape["tp"]

    def per_device(*args):
        gate_weight, key_cache = args[7], args[10]
        aligned = (
            args[6].shape[2] % (2 * LANES) == 0
            and n_tp % 2 == 0
            and gate_weight.shape[2] // n_seq % LANES == 0
            and key_cache.shape[3] == LANES
            and args[0].shape[0] == 2 * n_seq
        )
        make = make_with_kernels if aligned else make_plain
        return make(n_seq, n_tp)(*args)

    return jax.shard_map(
        per_device,
        mesh=mesh,
        in_specs=(
            P(),
            P(),
            P(),
            P(None, "seq", "tp"),
            P(None, "seq", "tp"),
            P(None, "seq", "tp"),
            P(None, "tp", "seq"),
            P(None, "seq", "tp"),
            P(None, "seq", "tp"),
            P(None, "tp", "seq"),
            P(None, None, "seq", "tp"),
            P(None, None, "seq", "tp"),
        ),
        out_specs=(P(), P(None, None, "seq", "tp"), P(None, None, "seq", "tp")),
        check_vma=False,
    )
```

```python
import functools
import math

import jax
import jax.numpy as jnp
from jax import lax
from jax.experimental import pallas as pl
from jax.experimental.pallas import tpu as pltpu
from jax.sharding import PartitionSpec as P

HEAD_DIM = 64
LAYERS = 2
eps_norm = 1e-05
neg_fill = -1e30


def split_hi_lo(value, parts):
    out = []
    rest = value
    for _ in range(parts):
        head = lax.reduce_precision(rest, 8, 7)
        out.append(head.astype(jnp.bfloat16))
        rest = rest - head
    return out


def seq_swap(chunks):
    return lax.all_to_all(chunks, "seq", 0, 0)


def make_plain(n_seq, n_tp):
    def tp_sum(part):
        total = part
        for k in range(1, n_tp):
            total = total + lax.ppermute(part, "tp", [(i, (i + k) % n_tp) for i in range(n_tp)])
        return total

    def per_device(
        hidden_in,
        lengths,
        positions,
        query_weight,
        key_weight,
        value_weight,
        out_weight,
        gate_weight,
        up_weight,
        down_weight,
        key_cache,
        value_cache,
    ):
        seq_index = lax.axis_index("seq")
        requests, width = hidden_in.shape
        col_count = out_weight.shape[2]
        col_start = seq_index * col_count
        block_len = key_cache.shape[2]
        kv_width = key_cache.shape[3]
        query_width = query_weight.shape[2]
        heads = query_width // HEAD_DIM
        kv_heads = kv_width // HEAD_DIM
        repeat = heads // kv_heads
        ff_here = gate_weight.shape[2]
        ff_own = ff_here // n_seq
        scale = 1.0 / math.sqrt(HEAD_DIM)
        slots = seq_index * block_len + jnp.arange(block_len, dtype=jnp.int32)
        new_slot = (slots[None, :] == lengths[:, None])[:, :, None]
        live = (slots[None, :] <= lengths[:, None])[:, None, None, :]

        half = HEAD_DIM // 2
        inverse = 500000.0 ** (-(2.0 * jnp.arange(half, dtype=jnp.float32)) / HEAD_DIM)
        angles = positions.astype(jnp.float32)[:, None] * inverse[None, :]
        cosine = jnp.cos(angles)[:, None, :]
        sine = jnp.sin(angles)[:, None, :]

        def rotate(x):
            a, b = x[..., :half], x[..., half:]
            return jnp.concatenate([a * cosine - b * sine, b * cosine + a * sine], axis=-1)

        def stats_of(x):
            f = x.astype(jnp.float32)
            return jnp.sum(f * f, axis=-1, keepdims=True)

        def pad_lanes(cols):
            joined = jnp.concatenate(cols, axis=-1)
            return jnp.pad(joined, ((0, 0), (0, -joined.shape[-1] % 128)))

        own = lax.dynamic_slice_in_dim(hidden_in, col_start, col_count, 1)
        key_layers = []
        value_layers = []
        for layer in range(LAYERS):
            part = jnp.concatenate(
                [
                    jnp.dot(own, w[layer], preferred_element_type=jnp.float32)
                    for w in (query_weight, key_weight, value_weight)
                ],
                axis=1,
            ).astype(jnp.bfloat16)
            packed = jnp.concatenate([part, pad_lanes(split_hi_lo(stats_of(own), 2))], axis=1)
            got = seq_swap(jnp.broadcast_to(packed[None], (n_seq,) + packed.shape))
            got = jnp.sum(got.astype(jnp.float32), axis=0)
            qkv = query_width + 2 * kv_width
            spread = (got[:, qkv : qkv + 1] + got[:, qkv + 1 : qkv + 2]) / width
            got = got[:, :qkv] * lax.rsqrt(spread + eps_norm)
            query = rotate(got[:, :query_width].reshape(requests, heads, HEAD_DIM))
            query = query.astype(jnp.bfloat16).reshape(requests, kv_heads, repeat, HEAD_DIM)
            key_new = rotate(
                got[:, query_width : query_width + kv_width].reshape(requests, kv_heads, HEAD_DIM)
            )
            key_new = key_new.astype(jnp.bfloat16).reshape(requests, kv_width)
            value_new = got[:, query_width + kv_width :].astype(jnp.bfloat16)
            key_rows = jnp.where(new_slot, key_new[:, None, :], key_cache[layer])
            value_rows = jnp.where(new_slot, value_new[:, None, :], value_cache[layer])
            key_layers.append(key_rows)
            value_layers.append(value_rows)
            key_heads = key_rows.reshape(requests, block_len, kv_heads, HEAD_DIM)
            value_heads = value_rows.reshape(requests, block_len, kv_heads, HEAD_DIM)
            scores = (
                jnp.einsum("bkrd,bskd->bkrs", query, key_heads, preferred_element_type=jnp.float32)
                * scale
            )
            scores = jnp.where(live, scores, neg_fill)
            top = jnp.max(scores, axis=3)
            weights = jnp.where(live, jnp.exp(scores - top[..., None]), 0.0)
            sums = jnp.sum(weights, axis=3)
            acc = jnp.einsum(
                "bkrs,bskd->bkrd",
                weights.astype(jnp.bfloat16),
                value_heads,
                preferred_element_type=jnp.float32,
            )
            packed = jnp.concatenate(
                [
                    acc.reshape(requests, query_width).astype(jnp.bfloat16),
                    pad_lanes(
                        split_hi_lo(top.reshape(requests, heads), 3)
                        + split_hi_lo(sums.reshape(requests, heads), 2)
                    ),
                ],
                axis=1,
            )
            got = seq_swap(jnp.broadcast_to(packed[None], (n_seq,) + packed.shape))
            got = got.astype(jnp.float32)
            acc = got[:, :, :query_width].reshape(n_seq, requests, heads, HEAD_DIM)
            side = got[:, :, query_width : query_width + 5 * heads].reshape(
                n_seq, requests, 5, heads
            )
            tops = side[:, :, 0] + side[:, :, 1] + side[:, :, 2]
            factor = jnp.exp(tops - jnp.max(tops, axis=0, keepdims=True))
            total = jnp.sum(factor * (side[:, :, 3] + side[:, :, 4]), axis=0)
            attended = jnp.sum(acc * factor[..., None], axis=0) / total[..., None]
            attended = attended.astype(jnp.bfloat16).reshape(requests, query_width)

            part = jnp.dot(attended, out_weight[layer], preferred_element_type=jnp.float32)
            mid = (own.astype(jnp.float32) + tp_sum(part)).astype(jnp.bfloat16)

            gate = jnp.dot(mid, gate_weight[layer], preferred_element_type=jnp.float32)
            up = jnp.dot(mid, up_weight[layer], preferred_element_type=jnp.float32)
            side = pad_lanes(split_hi_lo(stats_of(mid), 2))
            packed = jnp.concatenate(
                [
                    gate.astype(jnp.bfloat16).reshape(requests, n_seq, ff_own),
                    up.astype(jnp.bfloat16).reshape(requests, n_seq, ff_own),
                    jnp.broadcast_to(side[:, None], (requests, n_seq, side.shape[1])),
                ],
                axis=2,
            )
            got = seq_swap(packed.transpose(1, 0, 2))
            got = jnp.sum(got.astype(jnp.float32), axis=0)
            spread = (got[:, 2 * ff_own : 2 * ff_own + 1] + got[:, 2 * ff_own + 1 : 2 * ff_own + 2]) / width
            inv = lax.rsqrt(spread + eps_norm)
            hidden = jax.nn.silu(got[:, :ff_own] * inv) * (got[:, ff_own : 2 * ff_own] * inv)
            hidden = hidden.astype(jnp.bfloat16)
            hidden = seq_swap(jnp.broadcast_to(hidden[None], (n_seq,) + hidden.shape))
            hidden = hidden.transpose(1, 0, 2).reshape(requests, ff_here)
            part = jnp.dot(hidden, down_weight[layer], preferred_element_type=jnp.float32)
            own = (mid.astype(jnp.float32) + tp_sum(part)).astype(jnp.bfloat16)

        stream = seq_swap(jnp.broadcast_to(own[None], (n_seq,) + own.shape))
        stream = stream.transpose(1, 0, 2).reshape(requests, width)
        return (stream, jnp.stack(key_layers), jnp.stack(value_layers))

    return per_device


LANES = 128
VMEM_ROOM = 8 << 20
QUARTER = LANES // 4
NEW_AT = 2 * QUARTER


def lane_ids(shape):
    return lax.broadcasted_iota(jnp.int32, shape, len(shape) - 1)


def as_hi_lo(value, lane):
    wide = jnp.broadcast_to(value, lane.shape)
    high = wide.astype(jnp.bfloat16).astype(jnp.float32)
    return jnp.where(lane == 0, high, jnp.where(lane == 1, wide - high, 0.0)).astype(jnp.bfloat16)


def member_order(n_seq, odd):
    if n_seq != 8:
        return list(range(n_seq))
    return [3, 2, 6, 7, 5, 4, 0, 1] if odd else [0, 1, 3, 2, 6, 7, 5, 4]


def whole_order(n_seq, n_tp):
    return [s * n_tp + (t ^ (t >> 1)) for s in member_order(n_seq, False) for t in range(n_tp)]


def position_of(member, n_seq):
    even, odd = (member_order(n_seq, side).index(member) for side in (False, True))
    return jnp.where(lax.axis_index("tp") % 2 == 0, even, odd)


def square_sum(own):
    wide = own.astype(jnp.float32)
    return jnp.sum(wide * wide, axis=1, keepdims=True)


def dot32(a, b):
    return jnp.dot(a, b, preferred_element_type=jnp.float32)


def call(body, out_shape, *args, name, held=None, scratch=(), out_specs=None):
    vmem, hbm = [pl.BlockSpec(memory_space=m) for m in (pltpu.VMEM, pltpu.HBM)]
    held = len(args) if held is None else held
    single = not isinstance(out_shape, (tuple, list))
    args = [
        pltpu.with_memory_space_constraint(a, pltpu.VMEM if i < held else pltpu.HBM)
        for i, a in enumerate(args)
    ]
    return pl.pallas_call(
        body,
        out_shape=out_shape,
        in_specs=[vmem if i < held else hbm for i in range(len(args))],
        out_specs=out_specs or (vmem if single else [vmem] * len(out_shape)),
        scratch_shapes=list(scratch),
        compiler_params=pltpu.CompilerParams(vmem_limit_bytes=VMEM_ROOM),
        name=name,
    )(*args)


def to_row(column):
    shape = (column.shape[0], LANES)
    row = lax.broadcasted_iota(jnp.int32, shape, 0)
    return jnp.sum(jnp.where(lane_ids(shape) == row, column, 0.0), axis=0, keepdims=True)


def to_column(line, requests):
    shape = (requests, LANES)
    row = lax.broadcasted_iota(jnp.int32, shape, 0)
    return jnp.sum(jnp.where(lane_ids(shape) == row, line, 0.0), axis=1, keepdims=True)


def project_body(own, weights, out_ref):
    requests = own.shape[0]
    members = out_ref.shape[0]
    per = requests // members
    query, key, value = [dot32(own, w) for w in weights]
    width = query.shape[1]
    query = query.astype(jnp.bfloat16)
    line = to_row(square_sum(own))
    high = line.astype(jnp.bfloat16).astype(jnp.float32)
    row = lax.broadcasted_iota(jnp.int32, (requests, LANES), 0)
    base = jnp.where(row == 2 * per, high, jnp.where(row == 2 * per + 1, line - high, 0.0))
    for member in range(members):
        block = base
        for r in range(per):
            at = member * per + r
            block = jnp.where(row == 2 * r, key[at : at + 1], block)
            block = jnp.where(row == 2 * r + 1, value[at : at + 1], block)
        place = position_of(member, members)
        out_ref[place, :, :width] = query
        out_ref[place, :, width:] = block.astype(jnp.bfloat16)


def first_kernel(n_more, *refs):
    hidden_ref, length_ref, position_ref, wq_ref, wk_ref, wv_ref = refs[:6]
    more = refs[6 : 6 + n_more]
    own_ref, cos_ref, sin_ref, table_ref, out_ref = refs[6 + n_more : 11 + n_more]
    more_here = refs[11 + n_more : 11 + 2 * n_more]
    wq_here, wk_here, wv_here, lengths, positions, sems = refs[11 + 2 * n_more :]
    span = own_ref.shape[1]
    start = pl.multiple_of(lax.axis_index("seq") * span, LANES)
    copies = [
        pltpu.make_async_copy(position_ref, positions, sems.at[0]),
        pltpu.make_async_copy(length_ref, lengths, sems.at[1]),
        pltpu.make_async_copy(hidden_ref.at[:, pl.ds(start, span)], own_ref, sems.at[2]),
        pltpu.make_async_copy(wq_ref.at[0], wq_here, sems.at[3]),
        pltpu.make_async_copy(wk_ref.at[0], wk_here, sems.at[4]),
        pltpu.make_async_copy(wv_ref.at[0], wv_here, sems.at[5]),
    ]
    copies += [
        pltpu.make_async_copy(ref.at[0], here.at[0], sems.at[6 + i])
        for i, (ref, here) in enumerate(zip(more, more_here))
    ]
    for copy in copies:
        copy.start()
    copies[0].wait()
    copies[1].wait()
    half = HEAD_DIM // 2
    lane = lane_ids(table_ref.shape)
    row = lax.broadcasted_iota(jnp.int32, table_ref.shape, 0)
    place = jnp.zeros(table_ref.shape, jnp.int32)
    length = jnp.zeros(table_ref.shape, jnp.int32)
    for b in range(table_ref.shape[0]):
        place = jnp.where(row == b, positions[b], place)
        length = jnp.where(row == b, lengths[b], length)
    inverse = jnp.zeros(table_ref.shape, jnp.float32)
    for i in range(half):
        inverse = jnp.where(lane % half == i, 500000.0 ** (-2.0 * i / HEAD_DIM), inverse)
    angles = place.astype(jnp.float32) * inverse
    sine = jnp.sin(angles)
    table_ref[...] = length
    cos_ref[...] = jnp.cos(angles)
    sin_ref[...] = jnp.where(lane % HEAD_DIM < half, -sine, sine)
    for copy in copies[2:6]:
        copy.wait()
    project_body(own_ref[...], [wq_here[...], wk_here[...], wv_here[...]], out_ref)
    for copy in copies[6:]:
        copy.wait()


def load_kernel(n_more, *refs):
    more, more_here, sems = refs[1 : 1 + n_more], refs[1 + n_more : 1 + 2 * n_more], refs[-1]
    copies = [
        pltpu.make_async_copy(ref.at[0], here.at[0], sems.at[i])
        for i, (ref, here) in enumerate(zip(more, more_here))
    ]
    for copy in copies:
        copy.start()
    for copy in copies:
        copy.wait()


def store_kernel(part_ref, length_ref, key_ref, value_ref, *refs):
    layers, requests, block, _ = key_ref.shape
    sent_refs = refs[:layers]
    key_out, value_out, token_ref, key_here, value_here, sems = refs[layers:]
    token_ref[...] = jnp.zeros_like(token_ref)
    fresh = length_ref[...] - lax.axis_index("seq") * block
    slot = lax.broadcasted_iota(jnp.int32, (block, LANES), 0)
    row = lax.broadcasted_iota(jnp.int32, (requests, LANES), 0)
    quarter_here = lane_ids((requests, LANES)) // QUARTER
    copies = []
    for layer in range(layers):
        members, _, span = sent_refs[layer].shape
        per = requests // members
        for member in range(members):
            sent = sent_refs[layer][position_of(member, members), :, span - LANES :]
            sent = sent.astype(jnp.float32)
            wide = jnp.zeros((requests, LANES), jnp.float32)
            for quarter in range(4):
                shifted = pltpu.roll(sent, (QUARTER * quarter - NEW_AT) % LANES, 1)
                wide = jnp.where((quarter_here == quarter) & (row % 4 == quarter), shifted, wide)
            for r in range(per):
                b = member * per + r
                here = slot == fresh[b : b + 1]
                for i, (old, new_here) in enumerate([(key_ref, key_here), (value_ref, value_here)]):
                    j = 4 * (2 * r + i)
                    new = jnp.sum(wide[j : j + 4], axis=0, keepdims=True)
                    kept = jnp.where(here, new, old[layer, b].astype(jnp.float32))
                    new_here[layer, b] = kept.astype(jnp.bfloat16)
        for i, (here, out) in enumerate([(key_here, key_out), (value_here, value_out)]):
            copies.append(
                pltpu.make_async_copy(here.at[layer], out.at[layer], sems.at[2 * layer + i])
            )
            copies[-1].start()
    for copy in copies:
        copy.wait()


def sum_parts(base_ref, part_refs):
    total = part_refs[0][...].astype(jnp.float32)
    for ref in part_refs[1:]:
        total = total + ref[...].astype(jnp.float32)
    return (base_ref[...].astype(jnp.float32) + total).astype(jnp.bfloat16)


def next_kernel(layer, n_parts, *refs):
    base_ref, parts = refs[0], refs[1 : 1 + n_parts]
    wq_ref, wk_ref, wv_ref, own_ref, out_ref = refs[1 + n_parts :]
    own = sum_parts(base_ref, parts)
    own_ref[...] = own
    project_body(own, [w[layer] for w in (wq_ref, wk_ref, wv_ref)], out_ref)


def half_of(value, core):
    middle = value.shape[1] // 2
    return jnp.where(core == 0, value[:, :middle], value[:, middle:])


def meet_kernel(n_tp, mid_ref, keep_ref, got_ref, out_ref):
    place = lax.axis_index("tp")
    total = keep_ref[...] + got_ref[...]
    base = half_of(mid_ref[...].astype(jnp.float32), place % 2)
    total = (total + jnp.where(place < 2, base, 0.0)).astype(jnp.bfloat16)
    for member in range(out_ref.shape[0]):
        out_ref[member] = total


def last_kernel(n_tp, got_ref, out_ref):
    span = got_ref.shape[2]
    order = whole_order(got_ref.shape[0] // n_tp, n_tp)
    for block in range(got_ref.shape[0] // n_tp):
        for core in range(2):
            total = got_ref[order.index(block * n_tp + core)].astype(jnp.float32)
            for pair in range(1, n_tp // 2):
                total = total + got_ref[order.index(block * n_tp + 2 * pair + core)].astype(jnp.float32)
            at = (2 * block + core) * span
            out_ref[:, at : at + span] = total.astype(jnp.bfloat16)


def attend_kernel(
    layer, width, heads, kv_heads, got_ref, cos_ref, sin_ref, length_ref,
    key_ref, value_ref, out_ref,
):
    members, requests, _ = got_ref.shape
    query_width = heads * HEAD_DIM
    repeat = heads // kv_heads
    block = key_ref.shape[2]
    per = requests // members
    place = lax.axis_index("seq")

    def summed(at):
        total = got_ref[0, :, at : at + LANES].astype(jnp.float32)
        for member in range(1, members):
            total = total + got_ref[member, :, at : at + LANES].astype(jnp.float32)
        return total

    lane = lane_ids((requests, LANES))
    low = lane < HEAD_DIM
    fresh_sums = summed(query_width)
    spread = (fresh_sums[2 * per : 2 * per + 1] + fresh_sums[2 * per + 1 : 2 * per + 2]) * (
        1.0 / width
    )
    inv_line = lax.rsqrt(spread + eps_norm)
    inv = to_column(inv_line, requests)
    half = HEAD_DIM // 2

    def rotated(x, cosine, sine):
        first = lane_ids(x.shape) % HEAD_DIM < half
        other = jnp.where(first, pltpu.roll(x, LANES - half, 1), pltpu.roll(x, half, 1))
        return x * cosine + other * sine

    stacked = []
    for pair in range(heads // 2):
        x = rotated(summed(pair * LANES) * inv, cos_ref[...], sin_ref[...])
        turned = pltpu.roll(x, HEAD_DIM, 1)
        if 2 * pair // repeat == 0:
            stacked += [jnp.where(low, x, 0.0), jnp.where(low, turned, 0.0)]
        else:
            stacked += [jnp.where(low, 0.0, turned), jnp.where(low, 0.0, x)]
    query = jnp.concatenate(stacked, axis=0).astype(jnp.bfloat16).astype(jnp.float32)
    query = query * (1.0 / math.sqrt(HEAD_DIM))

    request = lax.broadcasted_iota(jnp.int32, (requests, LANES), 0)
    key_new = jnp.zeros((requests, LANES), jnp.float32)
    value_new = jnp.zeros((requests, LANES), jnp.float32)
    rows = []
    for r in range(per):
        at = place * per + r
        scale = jnp.sum(
            jnp.where(lane_ids((1, LANES)) == at, inv_line, 0.0), axis=1, keepdims=True
        )
        key = rotated(
            fresh_sums[2 * r : 2 * r + 1] * scale, cos_ref[pl.ds(at, 1)], sin_ref[pl.ds(at, 1)]
        )
        key = key.astype(jnp.bfloat16).astype(jnp.float32)
        value = (fresh_sums[2 * r + 1 : 2 * r + 2] * scale).astype(jnp.bfloat16).astype(jnp.float32)
        key_new = jnp.where(request == at, key, key_new)
        value_new = jnp.where(request == at, value, value_new)
        rows += [key, value]
    owned = jnp.concatenate([request // per == place] * heads, axis=0)

    def per_head(x):
        return jnp.concatenate([x] * heads, axis=0)

    fresh_scores = jnp.sum(query * per_head(key_new), axis=1, keepdims=True)
    owned_row = owned[:, 0:1]
    fresh_scores = jnp.where(owned_row, fresh_scores, neg_fill)

    keys = key_ref[layer].reshape(requests * block, LANES)
    values = value_ref[layer].reshape(requests * block, LANES)
    scores = lax.dot_general(
        query.astype(jnp.bfloat16),
        keys,
        (((1,), (1,)), ((), ())),
        preferred_element_type=jnp.float32,
    )
    begin = request * block
    end = begin + jnp.clip(length_ref[...] - place * block, 0, block)
    copies = scores.shape[1] // LANES
    begin = jnp.concatenate([per_head(begin)] * copies, axis=1)
    end = jnp.concatenate([per_head(end)] * copies, axis=1)
    column = lane_ids(scores.shape)
    live = (column >= begin) & (column < end)
    scores = jnp.where(live, scores, neg_fill)
    top = jnp.maximum(jnp.max(scores, axis=1, keepdims=True), fresh_scores)
    top = jnp.maximum(top, 0.5 * neg_fill)
    weights = jnp.exp(scores - top)
    fresh_weights = jnp.exp(fresh_scores - top)
    sums = jnp.sum(weights, axis=1, keepdims=True) + fresh_weights
    acc = dot32(weights.astype(jnp.bfloat16), values)
    acc = acc + fresh_weights.astype(jnp.bfloat16).astype(jnp.float32) * per_head(value_new)
    turned = pltpu.roll(acc, HEAD_DIM, 1)

    side = jnp.zeros((requests, LANES), jnp.float32)
    for h in range(heads):
        part = slice(h * requests, (h + 1) * requests)
        for group in range(5):
            side = jnp.where(lane == group * heads + h, (top if group < 3 else sums)[part], side)
    spare = jnp.zeros((requests, LANES), jnp.float32)
    for j, line in enumerate(rows):
        spare = jnp.where(request // 4 == j, line, spare)
    for quarter in range(4):
        shifted = pltpu.roll(spare, (NEW_AT - QUARTER * quarter) % LANES, 1)
        side = jnp.where(
            (lane >= NEW_AT) & (lane < NEW_AT + QUARTER) & (request % 4 == quarter), shifted, side
        )
    one = side.astype(jnp.bfloat16).astype(jnp.float32)
    two = (side - one).astype(jnp.bfloat16).astype(jnp.float32)
    three = side - one - two
    second = ((lane >= heads) & (lane < 2 * heads)) | ((lane >= 4 * heads) & (lane < 5 * heads))
    third = (lane >= 2 * heads) & (lane < 3 * heads)
    side = jnp.where(third, three, jnp.where(second, two, one)).astype(jnp.bfloat16)
    pieces = []
    for pair in range(heads // 2):
        even = slice(2 * pair * requests, (2 * pair + 1) * requests)
        odd = slice((2 * pair + 1) * requests, (2 * pair + 2) * requests)
        if 2 * pair // repeat == 0:
            pieces.append(jnp.where(low, acc[even], turned[odd]).astype(jnp.bfloat16))
        else:
            pieces.append(jnp.where(low, turned[even], acc[odd]).astype(jnp.bfloat16))
    pieces.append(side)
    for member in range(members):
        for i, piece in enumerate(pieces):
            out_ref[member, :, i * LANES : (i + 1) * LANES] = piece


def combine_kernel(layer, heads, got_ref, w_ref, out_ref):
    members, requests, _ = got_ref.shape
    query_width = heads * HEAD_DIM
    low = lane_ids((requests, LANES)) < HEAD_DIM
    sides = [
        got_ref[m, :, query_width : query_width + LANES].astype(jnp.float32) for m in range(members)
    ]
    tops = [
        s[:, :heads] + s[:, heads : 2 * heads] + s[:, 2 * heads : 3 * heads] for s in sides
    ]
    sums = [s[:, 3 * heads : 4 * heads] + s[:, 4 * heads : 5 * heads] for s in sides]
    top = tops[0]
    for t in tops[1:]:
        top = jnp.maximum(top, t)
    factors = [jnp.exp(t - top) for t in tops]
    total = factors[0] * sums[0]
    for f, s in zip(factors[1:], sums[1:]):
        total = total + f * s

    def spread(column, pair):
        return jnp.where(low, column[:, 2 * pair : 2 * pair + 1], column[:, 2 * pair + 1 : 2 * pair + 2])

    attended = []
    for pair in range(heads // 2):
        acc = jnp.zeros((requests, LANES), jnp.float32)
        for m in range(members):
            piece = got_ref[m, :, pair * LANES : (pair + 1) * LANES].astype(jnp.float32)
            acc = acc + piece * spread(factors[m], pair)
        attended.append((acc / spread(total, pair)).astype(jnp.bfloat16))
    out_ref[...] = dot32(jnp.concatenate(attended, axis=1), w_ref[layer]).astype(jnp.bfloat16)


def widen_kernel(layer, n_parts, *refs):
    base_ref, parts = refs[0], refs[1 : 1 + n_parts]
    gate_ref, up_ref = refs[1 + n_parts : 3 + n_parts]
    mid_ref, out_ref = refs[-2:]
    mid = sum_parts(base_ref, parts)
    mid_ref[...] = mid
    side = as_hi_lo(square_sum(mid), lane_ids((mid.shape[0], LANES)))
    members = out_ref.shape[0]
    own = gate_ref.shape[2] // members
    for member in range(members):
        cols = slice(member * own, (member + 1) * own)
        place = position_of(member, members)
        out_ref[place, :, :own] = dot32(mid, gate_ref[layer, :, cols]).astype(jnp.bfloat16)
        out_ref[place, :, own : 2 * own] = dot32(mid, up_ref[layer, :, cols]).astype(jnp.bfloat16)
        out_ref[place, :, 2 * own :] = side


def silu_kernel(width, got_ref, out_ref):
    members, _, span = got_ref.shape
    own = (span - LANES) // 2
    total = got_ref[0].astype(jnp.float32)
    for member in range(1, members):
        total = total + got_ref[member].astype(jnp.float32)
    spread = (total[:, 2 * own : 2 * own + 1] + total[:, 2 * own + 1 : 2 * own + 2]) * (1.0 / width)
    inv = lax.rsqrt(spread + eps_norm)
    gate = total[:, :own] * inv
    hidden = (gate / (1.0 + jnp.exp(-gate)) * (total[:, own : 2 * own] * inv)).astype(jnp.bfloat16)
    for member in range(members):
        out_ref[member] = hidden


def in_order(got_ref):
    members = got_ref.shape[0]
    return jnp.concatenate([got_ref[position_of(m, members)] for m in range(members)], axis=1)


def down_kernel(layer, got_ref, w_ref, out_ref):
    hidden = in_order(got_ref)
    out_ref[...] = dot32(hidden, w_ref[layer]).astype(jnp.bfloat16)


def down_last_kernel(layer, got_ref, w_ref, keep_ref, give_ref):
    hidden = in_order(got_ref)
    part = dot32(hidden, w_ref[layer])
    core = lax.axis_index("tp") % 2
    keep_ref[...] = half_of(part, core)
    give_ref[...] = half_of(part, 1 - core)


def make_with_kernels(n_seq, n_tp):
    groups = [[s * n_tp + t for s in member_order(n_seq, t % 2 == 1)] for t in range(n_tp)]

    def swap(chunks):
        return lax.all_to_all(chunks, ("seq", "tp"), 0, 0, axis_index_groups=groups)

    def tp_parts(part):
        got = [
            lax.ppermute(part, "tp", [(i, (i + k) % n_tp) for i in range(n_tp)])
            for k in range(1, n_tp)
        ]
        return [part] + got

    def per_device(
        hidden_in,
        lengths,
        positions,
        query_weight,
        key_weight,
        value_weight,
        out_weight,
        gate_weight,
        up_weight,
        down_weight,
        key_cache,
        value_cache,
    ):
        requests, width = hidden_in.shape
        col_count = out_weight.shape[2]
        kv_width = key_cache.shape[3]
        query_width = query_weight.shape[2]
        heads = query_width // HEAD_DIM
        kv_heads = kv_width // HEAD_DIM
        ff_own = gate_weight.shape[2] // n_seq
        bf16, f32 = jnp.bfloat16, jnp.float32

        def shape(dims, kind):
            return pltpu.VMEM(dims, kind)

        packed_shape = shape((n_seq, requests, query_width + LANES), bf16)
        part_shape = shape((requests, col_count), bf16)
        own_shape = shape((requests, col_count), bf16)
        sent = []
        packed_weights = (query_weight, key_weight, value_weight)
        table_shape = (requests, LANES)
        stored = (key_cache, value_cache, out_weight)
        wide = (gate_weight, up_weight)
        own, cosine, sine, length_table, packed, *early = call(
            functools.partial(first_kernel, len(stored)),
            (
                own_shape,
                shape(table_shape, f32),
                shape(table_shape, f32),
                shape(table_shape, jnp.int32),
                packed_shape,
            )
            + tuple(shape((1,) + a.shape[1:], bf16) for a in stored),
            hidden_in,
            lengths,
            positions,
            *packed_weights,
            *stored,
            name="first",
            held=0,
            scratch=[pltpu.VMEM(w.shape[1:], bf16) for w in packed_weights]
            + [pltpu.SMEM((requests,), jnp.int32)] * 2
            + [pltpu.SemaphoreType.DMA((6 + len(stored),))],
        )
        parts = None
        mid = None
        for layer in range(LAYERS):
            if layer > 0:
                own, packed = call(
                    functools.partial(next_kernel, layer, n_tp),
                    (own_shape, packed_shape),
                    mid,
                    *parts,
                    *packed_weights,
                    name="next",
                )
            keys, values, out_here = early if layer == 0 else stored
            packed = call(
                functools.partial(attend_kernel, layer, width, heads, kv_heads),
                packed_shape,
                swap(packed),
                cosine,
                sine,
                length_table,
                keys,
                values,
                name="attend",
            )
            sent.append(swap(packed))
            part = call(
                functools.partial(combine_kernel, layer, heads),
                part_shape,
                sent[-1],
                out_here,
                name="combine",
            )
            parts = tp_parts(part)
            gate_here, up_here = wide
            if layer == 0:
                gate_here, up_here = call(
                    functools.partial(load_kernel, len(wide)),
                    tuple(shape((1,) + a.shape[1:], bf16) for a in wide),
                    part,
                    *wide,
                    name="load",
                    held=1,
                    scratch=[pltpu.SemaphoreType.DMA((len(wide),))],
                )
            tokens = []
            if layer + 1 == LAYERS:
                cache_shape = jax.ShapeDtypeStruct(key_cache.shape, bf16)
                hbm = pl.BlockSpec(memory_space=pltpu.HBM)
                key_out, value_out, token = call(
                    store_kernel,
                    (cache_shape, cache_shape, shape((8, LANES), f32)),
                    part,
                    length_table,
                    key_cache,
                    value_cache,
                    *sent,
                    name="store",
                    out_specs=[hbm, hbm, pl.BlockSpec(memory_space=pltpu.VMEM)],
                    scratch=[pltpu.VMEM(key_cache.shape, bf16)] * 2
                    + [pltpu.SemaphoreType.DMA((2 * LAYERS,))],
                )
                tokens = [token]
            mid, packed = call(
                functools.partial(widen_kernel, layer, n_tp),
                (own_shape, shape((n_seq, requests, 2 * ff_own + LANES), bf16)),
                own,
                *parts,
                gate_here,
                up_here,
                *tokens,
                name="widen",
            )
            hidden = call(
                functools.partial(silu_kernel, width),
                shape((n_seq, requests, ff_own), bf16),
                swap(packed),
                name="silu",
            )
            hidden = swap(hidden)
            if layer + 1 < LAYERS:
                part = call(
                    functools.partial(down_kernel, layer), part_shape, hidden, down_weight, name="down"
                )
                parts = tp_parts(part)
        half_shape = shape((requests, col_count // 2), f32)
        keep, give = call(
            functools.partial(down_last_kernel, LAYERS - 1),
            (half_shape, half_shape),
            hidden,
            down_weight,
            name="down_last",
        )
        give = lax.ppermute(give, "tp", [(i, i ^ 1) for i in range(n_tp)])
        stream = call(
            functools.partial(meet_kernel, n_tp),
            shape((n_seq * n_tp, requests, col_count // 2), bf16),
            mid,
            keep,
            give,
            name="meet",
        )
        everyone = [whole_order(n_seq, n_tp)]
        stream = lax.all_to_all(stream, ("seq", "tp"), 0, 0, axis_index_groups=everyone)
        stream = call(
            functools.partial(last_kernel, n_tp),
            jax.ShapeDtypeStruct((requests, width), bf16),
            stream,
            name="last",
        )
        return (stream, key_out, value_out)

    return per_device


def solution(mesh):
    n_seq, n_tp = mesh.shape["seq"], mesh.shape["tp"]

    def per_device(*args):
        gate_weight, key_cache = args[7], args[10]
        aligned = (
            args[6].shape[2] % (2 * LANES) == 0
            and n_tp % 2 == 0
            and gate_weight.shape[2] // n_seq % LANES == 0
            and key_cache.shape[3] == LANES
            and args[0].shape[0] == 2 * n_seq
        )
        make = make_with_kernels if aligned else make_plain
        return make(n_seq, n_tp)(*args)

    return jax.shard_map(
        per_device,
        mesh=mesh,
        in_specs=(
            P(),
            P(),
            P(),
            P(None, "seq", "tp"),
            P(None, "seq", "tp"),
            P(None, "seq", "tp"),
            P(None, "tp", "seq"),
            P(None, "seq", "tp"),
            P(None, "seq", "tp"),
            P(None, "tp", "seq"),
            P(None, None, "seq", "tp"),
            P(None, None, "seq", "tp"),
        ),
        out_specs=(P(), P(None, None, "seq", "tp"), P(None, None, "seq", "tp")),
        check_vma=False,
    )
```

```python
import functools
import math

import jax
import jax.numpy as jnp
from jax import lax
from jax.experimental import pallas as pl
from jax.experimental.pallas import tpu as pltpu
from jax.sharding import PartitionSpec as P

HEAD_DIM = 64
LAYERS = 2
eps_norm = 1e-05
neg_fill = -1e30


def split_hi_lo(value, parts):
    out = []
    rest = value
    for _ in range(parts):
        head = lax.reduce_precision(rest, 8, 7)
        out.append(head.astype(jnp.bfloat16))
        rest = rest - head
    return out


def seq_swap(chunks):
    return lax.all_to_all(chunks, "seq", 0, 0)


def make_plain(n_seq, n_tp):
    def tp_sum(part):
        total = part
        for k in range(1, n_tp):
            total = total + lax.ppermute(part, "tp", [(i, (i + k) % n_tp) for i in range(n_tp)])
        return total

    def per_device(
        hidden_in,
        lengths,
        positions,
        query_weight,
        key_weight,
        value_weight,
        out_weight,
        gate_weight,
        up_weight,
        down_weight,
        key_cache,
        value_cache,
    ):
        seq_index = lax.axis_index("seq")
        requests, width = hidden_in.shape
        col_count = out_weight.shape[2]
        col_start = seq_index * col_count
        block_len = key_cache.shape[2]
        kv_width = key_cache.shape[3]
        query_width = query_weight.shape[2]
        heads = query_width // HEAD_DIM
        kv_heads = kv_width // HEAD_DIM
        repeat = heads // kv_heads
        ff_here = gate_weight.shape[2]
        ff_own = ff_here // n_seq
        scale = 1.0 / math.sqrt(HEAD_DIM)
        slots = seq_index * block_len + jnp.arange(block_len, dtype=jnp.int32)
        new_slot = (slots[None, :] == lengths[:, None])[:, :, None]
        live = (slots[None, :] <= lengths[:, None])[:, None, None, :]

        half = HEAD_DIM // 2
        inverse = 500000.0 ** (-(2.0 * jnp.arange(half, dtype=jnp.float32)) / HEAD_DIM)
        angles = positions.astype(jnp.float32)[:, None] * inverse[None, :]
        cosine = jnp.cos(angles)[:, None, :]
        sine = jnp.sin(angles)[:, None, :]

        def rotate(x):
            a, b = x[..., :half], x[..., half:]
            return jnp.concatenate([a * cosine - b * sine, b * cosine + a * sine], axis=-1)

        def stats_of(x):
            f = x.astype(jnp.float32)
            return jnp.sum(f * f, axis=-1, keepdims=True)

        def pad_lanes(cols):
            joined = jnp.concatenate(cols, axis=-1)
            return jnp.pad(joined, ((0, 0), (0, -joined.shape[-1] % 128)))

        own = lax.dynamic_slice_in_dim(hidden_in, col_start, col_count, 1)
        key_layers = []
        value_layers = []
        for layer in range(LAYERS):
            part = jnp.concatenate(
                [
                    jnp.dot(own, w[layer], preferred_element_type=jnp.float32)
                    for w in (query_weight, key_weight, value_weight)
                ],
                axis=1,
            ).astype(jnp.bfloat16)
            packed = jnp.concatenate([part, pad_lanes(split_hi_lo(stats_of(own), 2))], axis=1)
            got = seq_swap(jnp.broadcast_to(packed[None], (n_seq,) + packed.shape))
            got = jnp.sum(got.astype(jnp.float32), axis=0)
            qkv = query_width + 2 * kv_width
            spread = (got[:, qkv : qkv + 1] + got[:, qkv + 1 : qkv + 2]) / width
            got = got[:, :qkv] * lax.rsqrt(spread + eps_norm)
            query = rotate(got[:, :query_width].reshape(requests, heads, HEAD_DIM))
            query = query.astype(jnp.bfloat16).reshape(requests, kv_heads, repeat, HEAD_DIM)
            key_new = rotate(
                got[:, query_width : query_width + kv_width].reshape(requests, kv_heads, HEAD_DIM)
            )
            key_new = key_new.astype(jnp.bfloat16).reshape(requests, kv_width)
            value_new = got[:, query_width + kv_width :].astype(jnp.bfloat16)
            key_rows = jnp.where(new_slot, key_new[:, None, :], key_cache[layer])
            value_rows = jnp.where(new_slot, value_new[:, None, :], value_cache[layer])
            key_layers.append(key_rows)
            value_layers.append(value_rows)
            key_heads = key_rows.reshape(requests, block_len, kv_heads, HEAD_DIM)
            value_heads = value_rows.reshape(requests, block_len, kv_heads, HEAD_DIM)
            scores = (
                jnp.einsum("bkrd,bskd->bkrs", query, key_heads, preferred_element_type=jnp.float32)
                * scale
            )
            scores = jnp.where(live, scores, neg_fill)
            top = jnp.max(scores, axis=3)
            weights = jnp.where(live, jnp.exp(scores - top[..., None]), 0.0)
            sums = jnp.sum(weights, axis=3)
            acc = jnp.einsum(
                "bkrs,bskd->bkrd",
                weights.astype(jnp.bfloat16),
                value_heads,
                preferred_element_type=jnp.float32,
            )
            packed = jnp.concatenate(
                [
                    acc.reshape(requests, query_width).astype(jnp.bfloat16),
                    pad_lanes(
                        split_hi_lo(top.reshape(requests, heads), 3)
                        + split_hi_lo(sums.reshape(requests, heads), 2)
                    ),
                ],
                axis=1,
            )
            got = seq_swap(jnp.broadcast_to(packed[None], (n_seq,) + packed.shape))
            got = got.astype(jnp.float32)
            acc = got[:, :, :query_width].reshape(n_seq, requests, heads, HEAD_DIM)
            side = got[:, :, query_width : query_width + 5 * heads].reshape(
                n_seq, requests, 5, heads
            )
            tops = side[:, :, 0] + side[:, :, 1] + side[:, :, 2]
            factor = jnp.exp(tops - jnp.max(tops, axis=0, keepdims=True))
            total = jnp.sum(factor * (side[:, :, 3] + side[:, :, 4]), axis=0)
            attended = jnp.sum(acc * factor[..., None], axis=0) / total[..., None]
            attended = attended.astype(jnp.bfloat16).reshape(requests, query_width)

            part = jnp.dot(attended, out_weight[layer], preferred_element_type=jnp.float32)
            mid = (own.astype(jnp.float32) + tp_sum(part)).astype(jnp.bfloat16)

            gate = jnp.dot(mid, gate_weight[layer], preferred_element_type=jnp.float32)
            up = jnp.dot(mid, up_weight[layer], preferred_element_type=jnp.float32)
            side = pad_lanes(split_hi_lo(stats_of(mid), 2))
            packed = jnp.concatenate(
                [
                    gate.astype(jnp.bfloat16).reshape(requests, n_seq, ff_own),
                    up.astype(jnp.bfloat16).reshape(requests, n_seq, ff_own),
                    jnp.broadcast_to(side[:, None], (requests, n_seq, side.shape[1])),
                ],
                axis=2,
            )
            got = seq_swap(packed.transpose(1, 0, 2))
            got = jnp.sum(got.astype(jnp.float32), axis=0)
            spread = (got[:, 2 * ff_own : 2 * ff_own + 1] + got[:, 2 * ff_own + 1 : 2 * ff_own + 2]) / width
            inv = lax.rsqrt(spread + eps_norm)
            hidden = jax.nn.silu(got[:, :ff_own] * inv) * (got[:, ff_own : 2 * ff_own] * inv)
            hidden = hidden.astype(jnp.bfloat16)
            hidden = seq_swap(jnp.broadcast_to(hidden[None], (n_seq,) + hidden.shape))
            hidden = hidden.transpose(1, 0, 2).reshape(requests, ff_here)
            part = jnp.dot(hidden, down_weight[layer], preferred_element_type=jnp.float32)
            own = (mid.astype(jnp.float32) + tp_sum(part)).astype(jnp.bfloat16)

        stream = seq_swap(jnp.broadcast_to(own[None], (n_seq,) + own.shape))
        stream = stream.transpose(1, 0, 2).reshape(requests, width)
        return (stream, jnp.stack(key_layers), jnp.stack(value_layers))

    return per_device


LANES = 128
VMEM_ROOM = 8 << 20
QUARTER = LANES // 4
NEW_AT = 2 * QUARTER


def lane_ids(shape):
    return lax.broadcasted_iota(jnp.int32, shape, len(shape) - 1)


def as_hi_lo(value, lane):
    wide = jnp.broadcast_to(value, lane.shape)
    high = wide.astype(jnp.bfloat16).astype(jnp.float32)
    return jnp.where(lane == 0, high, jnp.where(lane == 1, wide - high, 0.0)).astype(jnp.bfloat16)


def member_order(n_seq, odd):
    if n_seq != 8:
        return list(range(n_seq))
    return [3, 2, 6, 7, 5, 4, 0, 1] if odd else [0, 1, 3, 2, 6, 7, 5, 4]


def whole_order(n_seq, n_tp):
    return [s * n_tp + (t ^ (t >> 1)) for s in member_order(n_seq, False) for t in range(n_tp)]


def position_of(member, n_seq):
    even, odd = (member_order(n_seq, side).index(member) for side in (False, True))
    return jnp.where(lax.axis_index("tp") % 2 == 0, even, odd)


def square_sum(own):
    wide = own.astype(jnp.float32)
    return jnp.sum(wide * wide, axis=1, keepdims=True)


def dot32(a, b):
    return jnp.dot(a, b, preferred_element_type=jnp.float32)


def call(body, out_shape, *args, name, held=None, scratch=(), out_specs=None):
    vmem, hbm = [pl.BlockSpec(memory_space=m) for m in (pltpu.VMEM, pltpu.HBM)]
    held = len(args) if held is None else held
    single = not isinstance(out_shape, (tuple, list))
    args = [
        pltpu.with_memory_space_constraint(a, pltpu.VMEM if i < held else pltpu.HBM)
        for i, a in enumerate(args)
    ]
    return pl.pallas_call(
        body,
        out_shape=out_shape,
        in_specs=[vmem if i < held else hbm for i in range(len(args))],
        out_specs=out_specs or (vmem if single else [vmem] * len(out_shape)),
        scratch_shapes=list(scratch),
        compiler_params=pltpu.CompilerParams(vmem_limit_bytes=VMEM_ROOM),
        name=name,
    )(*args)


def to_row(column):
    shape = (column.shape[0], LANES)
    row = lax.broadcasted_iota(jnp.int32, shape, 0)
    return jnp.sum(jnp.where(lane_ids(shape) == row, column, 0.0), axis=0, keepdims=True)


def to_column(line, requests):
    shape = (requests, LANES)
    row = lax.broadcasted_iota(jnp.int32, shape, 0)
    return jnp.sum(jnp.where(lane_ids(shape) == row, line, 0.0), axis=1, keepdims=True)


def project_body(own, weights, out_ref):
    requests = own.shape[0]
    members = out_ref.shape[0]
    per = requests // members
    query, key, value = [dot32(own, w) for w in weights]
    width = query.shape[1]
    query = query.astype(jnp.bfloat16)
    line = to_row(square_sum(own))
    high = line.astype(jnp.bfloat16).astype(jnp.float32)
    row = lax.broadcasted_iota(jnp.int32, (requests, LANES), 0)
    base = jnp.where(row == 2 * per, high, jnp.where(row == 2 * per + 1, line - high, 0.0))
    for member in range(members):
        block = base
        for r in range(per):
            at = member * per + r
            block = jnp.where(row == 2 * r, key[at : at + 1], block)
            block = jnp.where(row == 2 * r + 1, value[at : at + 1], block)
        place = position_of(member, members)
        out_ref[place, :, :width] = query
        out_ref[place, :, width:] = block.astype(jnp.bfloat16)


def first_kernel(n_more, *refs):
    hidden_ref, length_ref, position_ref, wq_ref, wk_ref, wv_ref = refs[:6]
    more = refs[6 : 6 + n_more]
    own_ref, cos_ref, sin_ref, table_ref, out_ref = refs[6 + n_more : 11 + n_more]
    more_here = refs[11 + n_more : 11 + 2 * n_more]
    wq_here, wk_here, wv_here, lengths, positions, sems = refs[11 + 2 * n_more :]
    span = own_ref.shape[1]
    start = pl.multiple_of(lax.axis_index("seq") * span, LANES)
    copies = [
        pltpu.make_async_copy(position_ref, positions, sems.at[0]),
        pltpu.make_async_copy(length_ref, lengths, sems.at[1]),
        pltpu.make_async_copy(hidden_ref.at[:, pl.ds(start, span)], own_ref, sems.at[2]),
        pltpu.make_async_copy(wq_ref.at[0], wq_here, sems.at[3]),
        pltpu.make_async_copy(wk_ref.at[0], wk_here, sems.at[4]),
        pltpu.make_async_copy(wv_ref.at[0], wv_here, sems.at[5]),
    ]
    copies += [
        pltpu.make_async_copy(ref.at[0], here.at[0], sems.at[6 + i])
        for i, (ref, here) in enumerate(zip(more, more_here))
    ]
    for copy in copies:
        copy.start()
    copies[0].wait()
    copies[1].wait()
    half = HEAD_DIM // 2
    lane = lane_ids(table_ref.shape)
    row = lax.broadcasted_iota(jnp.int32, table_ref.shape, 0)
    place = jnp.zeros(table_ref.shape, jnp.int32)
    length = jnp.zeros(table_ref.shape, jnp.int32)
    for b in range(table_ref.shape[0]):
        place = jnp.where(row == b, positions[b], place)
        length = jnp.where(row == b, lengths[b], length)
    inverse = jnp.zeros(table_ref.shape, jnp.float32)
    for i in range(half):
        inverse = jnp.where(lane % half == i, 500000.0 ** (-2.0 * i / HEAD_DIM), inverse)
    angles = place.astype(jnp.float32) * inverse
    sine = jnp.sin(angles)
    table_ref[...] = length
    cos_ref[...] = jnp.cos(angles)
    sin_ref[...] = jnp.where(lane % HEAD_DIM < half, -sine, sine)
    for copy in copies[2:6]:
        copy.wait()
    project_body(own_ref[...], [wq_here[...], wk_here[...], wv_here[...]], out_ref)
    for copy in copies[6:]:
        copy.wait()


def load_kernel(n_more, *refs):
    more, more_here, sems = refs[1 : 1 + n_more], refs[1 + n_more : 1 + 2 * n_more], refs[-1]
    copies = [
        pltpu.make_async_copy(ref.at[0], here.at[0], sems.at[i])
        for i, (ref, here) in enumerate(zip(more, more_here))
    ]
    for copy in copies:
        copy.start()
    for copy in copies:
        copy.wait()


def store_kernel(part_ref, length_ref, key_ref, value_ref, *refs):
    layers, requests, block, _ = key_ref.shape
    sent_refs = refs[:layers]
    key_out, value_out, token_ref, key_here, value_here, sems = refs[layers:]
    token_ref[...] = jnp.zeros_like(token_ref)
    fresh = length_ref[...] - lax.axis_index("seq") * block
    slot = lax.broadcasted_iota(jnp.int32, (block, LANES), 0)
    row = lax.broadcasted_iota(jnp.int32, (requests, LANES), 0)
    quarter_here = lane_ids((requests, LANES)) // QUARTER
    copies = []
    for layer in range(layers):
        members, _, span = sent_refs[layer].shape
        per = requests // members
        for member in range(members):
            sent = sent_refs[layer][position_of(member, members), :, span - LANES :]
            sent = sent.astype(jnp.float32)
            wide = jnp.zeros((requests, LANES), jnp.float32)
            for quarter in range(4):
                shifted = pltpu.roll(sent, (QUARTER * quarter - NEW_AT) % LANES, 1)
                wide = jnp.where((quarter_here == quarter) & (row % 4 == quarter), shifted, wide)
            for r in range(per):
                b = member * per + r
                here = slot == fresh[b : b + 1]
                for i, (old, new_here) in enumerate([(key_ref, key_here), (value_ref, value_here)]):
                    j = 4 * (2 * r + i)
                    new = jnp.sum(wide[j : j + 4], axis=0, keepdims=True)
                    kept = jnp.where(here, new, old[layer, b].astype(jnp.float32))
                    new_here[layer, b] = kept.astype(jnp.bfloat16)
        for i, (here, out) in enumerate([(key_here, key_out), (value_here, value_out)]):
            copies.append(
                pltpu.make_async_copy(here.at[layer], out.at[layer], sems.at[2 * layer + i])
            )
            copies[-1].start()
    for copy in copies:
        copy.wait()


def sum_parts(base_ref, part_refs):
    total = part_refs[0][...].astype(jnp.float32)
    for ref in part_refs[1:]:
        total = total + ref[...].astype(jnp.float32)
    return (base_ref[...].astype(jnp.float32) + total).astype(jnp.bfloat16)


def next_kernel(layer, n_parts, *refs):
    base_ref, parts = refs[0], refs[1 : 1 + n_parts]
    wq_ref, wk_ref, wv_ref, own_ref, out_ref = refs[1 + n_parts :]
    own = sum_parts(base_ref, parts)
    own_ref[...] = own
    project_body(own, [w[layer] for w in (wq_ref, wk_ref, wv_ref)], out_ref)


def half_of(value, core):
    middle = value.shape[1] // 2
    return jnp.where(core == 0, value[:, :middle], value[:, middle:])


def meet_kernel(n_tp, mid_ref, keep_ref, got_ref, out_ref):
    place = lax.axis_index("tp")
    total = keep_ref[...] + got_ref[...]
    base = half_of(mid_ref[...].astype(jnp.float32), place % 2)
    total = (total + jnp.where(place < 2, base, 0.0)).astype(jnp.bfloat16)
    for member in range(out_ref.shape[0]):
        out_ref[member] = total


def last_kernel(n_tp, got_ref, out_ref):
    span = got_ref.shape[2]
    order = whole_order(got_ref.shape[0] // n_tp, n_tp)
    for block in range(got_ref.shape[0] // n_tp):
        for core in range(2):
            total = got_ref[order.index(block * n_tp + core)].astype(jnp.float32)
            for pair in range(1, n_tp // 2):
                total = total + got_ref[order.index(block * n_tp + 2 * pair + core)].astype(jnp.float32)
            at = (2 * block + core) * span
            out_ref[:, at : at + span] = total.astype(jnp.bfloat16)


def attend_kernel(
    layer, width, heads, kv_heads, got_ref, cos_ref, sin_ref, length_ref,
    key_ref, value_ref, out_ref,
):
    members, requests, _ = got_ref.shape
    query_width = heads * HEAD_DIM
    repeat = heads // kv_heads
    block = key_ref.shape[2]
    per = requests // members
    place = lax.axis_index("seq")

    def summed(at):
        total = got_ref[0, :, at : at + LANES].astype(jnp.float32)
        for member in range(1, members):
            total = total + got_ref[member, :, at : at + LANES].astype(jnp.float32)
        return total

    lane = lane_ids((requests, LANES))
    low = lane < HEAD_DIM
    fresh_sums = summed(query_width)
    spread = (fresh_sums[2 * per : 2 * per + 1] + fresh_sums[2 * per + 1 : 2 * per + 2]) * (
        1.0 / width
    )
    inv_line = lax.rsqrt(spread + eps_norm)
    inv = to_column(inv_line, requests)
    half = HEAD_DIM // 2

    def rotated(x, cosine, sine):
        first = lane_ids(x.shape) % HEAD_DIM < half
        other = jnp.where(first, pltpu.roll(x, LANES - half, 1), pltpu.roll(x, half, 1))
        return x * cosine + other * sine

    stacked = []
    for pair in range(heads // 2):
        x = rotated(summed(pair * LANES) * inv, cos_ref[...], sin_ref[...])
        turned = pltpu.roll(x, HEAD_DIM, 1)
        if 2 * pair // repeat == 0:
            stacked += [jnp.where(low, x, 0.0), jnp.where(low, turned, 0.0)]
        else:
            stacked += [jnp.where(low, 0.0, turned), jnp.where(low, 0.0, x)]
    query = jnp.concatenate(stacked, axis=0).astype(jnp.bfloat16).astype(jnp.float32)
    query = query * (1.0 / math.sqrt(HEAD_DIM))

    request = lax.broadcasted_iota(jnp.int32, (requests, LANES), 0)
    key_new = jnp.zeros((requests, LANES), jnp.float32)
    value_new = jnp.zeros((requests, LANES), jnp.float32)
    rows = []
    for r in range(per):
        at = place * per + r
        scale = jnp.sum(
            jnp.where(lane_ids((1, LANES)) == at, inv_line, 0.0), axis=1, keepdims=True
        )
        key = rotated(
            fresh_sums[2 * r : 2 * r + 1] * scale, cos_ref[pl.ds(at, 1)], sin_ref[pl.ds(at, 1)]
        )
        key = key.astype(jnp.bfloat16).astype(jnp.float32)
        value = (fresh_sums[2 * r + 1 : 2 * r + 2] * scale).astype(jnp.bfloat16).astype(jnp.float32)
        key_new = jnp.where(request == at, key, key_new)
        value_new = jnp.where(request == at, value, value_new)
        rows += [key, value]
    owned = jnp.concatenate([request // per == place] * heads, axis=0)

    def per_head(x):
        return jnp.concatenate([x] * heads, axis=0)

    fresh_scores = jnp.sum(query * per_head(key_new), axis=1, keepdims=True)
    owned_row = owned[:, 0:1]
    fresh_scores = jnp.where(owned_row, fresh_scores, neg_fill)

    keys = key_ref[layer].reshape(requests * block, LANES)
    values = value_ref[layer].reshape(requests * block, LANES)
    scores = lax.dot_general(
        query.astype(jnp.bfloat16),
        keys,
        (((1,), (1,)), ((), ())),
        preferred_element_type=jnp.float32,
    )
    begin = request * block
    end = begin + jnp.clip(length_ref[...] - place * block, 0, block)
    copies = scores.shape[1] // LANES
    begin = jnp.concatenate([per_head(begin)] * copies, axis=1)
    end = jnp.concatenate([per_head(end)] * copies, axis=1)
    column = lane_ids(scores.shape)
    live = (column >= begin) & (column < end)
    scores = jnp.where(live, scores, neg_fill)
    top = jnp.maximum(jnp.max(scores, axis=1, keepdims=True), fresh_scores)
    top = jnp.maximum(top, 0.5 * neg_fill)
    weights = jnp.exp(scores - top)
    fresh_weights = jnp.exp(fresh_scores - top)
    sums = jnp.sum(weights, axis=1, keepdims=True) + fresh_weights
    acc = dot32(weights.astype(jnp.bfloat16), values)
    acc = acc + fresh_weights.astype(jnp.bfloat16).astype(jnp.float32) * per_head(value_new)
    turned = pltpu.roll(acc, HEAD_DIM, 1)

    side = jnp.zeros((requests, LANES), jnp.float32)
    for h in range(heads):
        part = slice(h * requests, (h + 1) * requests)
        both = jnp.where(lane < 3 * heads, top[part], sums[part])
        side = jnp.where((lane % heads == h) & (lane < 5 * heads), both, side)
    spare = jnp.zeros((requests, LANES), jnp.float32)
    for j, line in enumerate(rows):
        spare = jnp.where(request // 4 == j, line, spare)
    for quarter in range(4):
        shifted = pltpu.roll(spare, (NEW_AT - QUARTER * quarter) % LANES, 1)
        side = jnp.where(
            (lane >= NEW_AT) & (lane < NEW_AT + QUARTER) & (request % 4 == quarter), shifted, side
        )
    one = side.astype(jnp.bfloat16).astype(jnp.float32)
    two = (side - one).astype(jnp.bfloat16).astype(jnp.float32)
    three = side - one - two
    second = ((lane >= heads) & (lane < 2 * heads)) | ((lane >= 4 * heads) & (lane < 5 * heads))
    third = (lane >= 2 * heads) & (lane < 3 * heads)
    side = jnp.where(third, three, jnp.where(second, two, one)).astype(jnp.bfloat16)
    pieces = []
    for pair in range(heads // 2):
        even = slice(2 * pair * requests, (2 * pair + 1) * requests)
        odd = slice((2 * pair + 1) * requests, (2 * pair + 2) * requests)
        if 2 * pair // repeat == 0:
            pieces.append(jnp.where(low, acc[even], turned[odd]).astype(jnp.bfloat16))
        else:
            pieces.append(jnp.where(low, turned[even], acc[odd]).astype(jnp.bfloat16))
    pieces.append(side)
    for member in range(members):
        for i, piece in enumerate(pieces):
            out_ref[member, :, i * LANES : (i + 1) * LANES] = piece


def combine_kernel(layer, heads, got_ref, w_ref, out_ref):
    members, requests, _ = got_ref.shape
    query_width = heads * HEAD_DIM
    low = lane_ids((requests, LANES)) < HEAD_DIM
    sides = [
        got_ref[m, :, query_width : query_width + LANES].astype(jnp.float32) for m in range(members)
    ]
    tops = [
        s[:, :heads] + s[:, heads : 2 * heads] + s[:, 2 * heads : 3 * heads] for s in sides
    ]
    sums = [s[:, 3 * heads : 4 * heads] + s[:, 4 * heads : 5 * heads] for s in sides]
    top = tops[0]
    for t in tops[1:]:
        top = jnp.maximum(top, t)
    factors = [jnp.exp(t - top) for t in tops]
    total = factors[0] * sums[0]
    for f, s in zip(factors[1:], sums[1:]):
        total = total + f * s

    scale = 1.0 / total
    factors = [f * scale for f in factors]

    def spread(column, pair):
        return jnp.where(low, column[:, 2 * pair : 2 * pair + 1], column[:, 2 * pair + 1 : 2 * pair + 2])

    attended = []
    for pair in range(heads // 2):
        acc = jnp.zeros((requests, LANES), jnp.float32)
        for m in range(members):
            piece = got_ref[m, :, pair * LANES : (pair + 1) * LANES].astype(jnp.float32)
            acc = acc + piece * spread(factors[m], pair)
        attended.append(acc.astype(jnp.bfloat16))
    out_ref[...] = dot32(jnp.concatenate(attended, axis=1), w_ref[layer]).astype(jnp.bfloat16)


def widen_kernel(layer, n_parts, *refs):
    base_ref, parts = refs[0], refs[1 : 1 + n_parts]
    gate_ref, up_ref = refs[1 + n_parts : 3 + n_parts]
    mid_ref, out_ref = refs[-2:]
    mid = sum_parts(base_ref, parts)
    mid_ref[...] = mid
    side = as_hi_lo(square_sum(mid), lane_ids((mid.shape[0], LANES)))
    members = out_ref.shape[0]
    own = gate_ref.shape[2] // members
    for member in range(members):
        cols = slice(member * own, (member + 1) * own)
        place = position_of(member, members)
        out_ref[place, :, :own] = dot32(mid, gate_ref[layer, :, cols]).astype(jnp.bfloat16)
        out_ref[place, :, own : 2 * own] = dot32(mid, up_ref[layer, :, cols]).astype(jnp.bfloat16)
        out_ref[place, :, 2 * own :] = side


def silu_kernel(width, got_ref, out_ref):
    members, _, span = got_ref.shape
    own = (span - LANES) // 2
    total = got_ref[0].astype(jnp.float32)
    for member in range(1, members):
        total = total + got_ref[member].astype(jnp.float32)
    spread = (total[:, 2 * own : 2 * own + 1] + total[:, 2 * own + 1 : 2 * own + 2]) * (1.0 / width)
    inv = lax.rsqrt(spread + eps_norm)
    gate = total[:, :own] * inv
    hidden = (gate / (1.0 + jnp.exp(-gate)) * (total[:, own : 2 * own] * inv)).astype(jnp.bfloat16)
    for member in range(members):
        out_ref[member] = hidden


def in_order(got_ref):
    members = got_ref.shape[0]
    return jnp.concatenate([got_ref[position_of(m, members)] for m in range(members)], axis=1)


def down_kernel(layer, got_ref, w_ref, out_ref):
    hidden = in_order(got_ref)
    out_ref[...] = dot32(hidden, w_ref[layer]).astype(jnp.bfloat16)


def down_last_kernel(layer, got_ref, w_ref, keep_ref, give_ref):
    hidden = in_order(got_ref)
    part = dot32(hidden, w_ref[layer])
    core = lax.axis_index("tp") % 2
    keep_ref[...] = half_of(part, core)
    give_ref[...] = half_of(part, 1 - core)


def make_with_kernels(n_seq, n_tp):
    groups = [[s * n_tp + t for s in member_order(n_seq, t % 2 == 1)] for t in range(n_tp)]

    def swap(chunks):
        return lax.all_to_all(chunks, ("seq", "tp"), 0, 0, axis_index_groups=groups)

    def tp_parts(part):
        got = [
            lax.ppermute(part, "tp", [(i, (i + k) % n_tp) for i in range(n_tp)])
            for k in range(1, n_tp)
        ]
        return [part] + got

    def per_device(
        hidden_in,
        lengths,
        positions,
        query_weight,
        key_weight,
        value_weight,
        out_weight,
        gate_weight,
        up_weight,
        down_weight,
        key_cache,
        value_cache,
    ):
        requests, width = hidden_in.shape
        col_count = out_weight.shape[2]
        kv_width = key_cache.shape[3]
        query_width = query_weight.shape[2]
        heads = query_width // HEAD_DIM
        kv_heads = kv_width // HEAD_DIM
        ff_own = gate_weight.shape[2] // n_seq
        bf16, f32 = jnp.bfloat16, jnp.float32

        def shape(dims, kind):
            return pltpu.VMEM(dims, kind)

        packed_shape = shape((n_seq, requests, query_width + LANES), bf16)
        part_shape = shape((requests, col_count), bf16)
        own_shape = shape((requests, col_count), bf16)
        sent = []
        packed_weights = (query_weight, key_weight, value_weight)
        table_shape = (requests, LANES)
        stored = (key_cache, value_cache, out_weight)
        wide = (gate_weight, up_weight)
        own, cosine, sine, length_table, packed, *early = call(
            functools.partial(first_kernel, len(stored)),
            (
                own_shape,
                shape(table_shape, f32),
                shape(table_shape, f32),
                shape(table_shape, jnp.int32),
                packed_shape,
            )
            + tuple(shape((1,) + a.shape[1:], bf16) for a in stored),
            hidden_in,
            lengths,
            positions,
            *packed_weights,
            *stored,
            name="first",
            held=0,
            scratch=[pltpu.VMEM(w.shape[1:], bf16) for w in packed_weights]
            + [pltpu.SMEM((requests,), jnp.int32)] * 2
            + [pltpu.SemaphoreType.DMA((6 + len(stored),))],
        )
        parts = None
        mid = None
        for layer in range(LAYERS):
            if layer > 0:
                own, packed = call(
                    functools.partial(next_kernel, layer, n_tp),
                    (own_shape, packed_shape),
                    mid,
                    *parts,
                    *packed_weights,
                    name="next",
                )
            keys, values, out_here = early if layer == 0 else stored
            packed = call(
                functools.partial(attend_kernel, layer, width, heads, kv_heads),
                packed_shape,
                swap(packed),
                cosine,
                sine,
                length_table,
                keys,
                values,
                name="attend",
            )
            sent.append(swap(packed))
            part = call(
                functools.partial(combine_kernel, layer, heads),
                part_shape,
                sent[-1],
                out_here,
                name="combine",
            )
            parts = tp_parts(part)
            gate_here, up_here = wide
            if layer == 0:
                gate_here, up_here = call(
                    functools.partial(load_kernel, len(wide)),
                    tuple(shape((1,) + a.shape[1:], bf16) for a in wide),
                    part,
                    *wide,
                    name="load",
                    held=1,
                    scratch=[pltpu.SemaphoreType.DMA((len(wide),))],
                )
            tokens = []
            if layer + 1 == LAYERS:
                cache_shape = jax.ShapeDtypeStruct(key_cache.shape, bf16)
                hbm = pl.BlockSpec(memory_space=pltpu.HBM)
                key_out, value_out, token = call(
                    store_kernel,
                    (cache_shape, cache_shape, shape((8, LANES), f32)),
                    part,
                    length_table,
                    key_cache,
                    value_cache,
                    *sent,
                    name="store",
                    out_specs=[hbm, hbm, pl.BlockSpec(memory_space=pltpu.VMEM)],
                    scratch=[pltpu.VMEM(key_cache.shape, bf16)] * 2
                    + [pltpu.SemaphoreType.DMA((2 * LAYERS,))],
                )
                tokens = [token]
            mid, packed = call(
                functools.partial(widen_kernel, layer, n_tp),
                (own_shape, shape((n_seq, requests, 2 * ff_own + LANES), bf16)),
                own,
                *parts,
                gate_here,
                up_here,
                *tokens,
                name="widen",
            )
            hidden = call(
                functools.partial(silu_kernel, width),
                shape((n_seq, requests, ff_own), bf16),
                swap(packed),
                name="silu",
            )
            hidden = swap(hidden)
            if layer + 1 < LAYERS:
                part = call(
                    functools.partial(down_kernel, layer), part_shape, hidden, down_weight, name="down"
                )
                parts = tp_parts(part)
        half_shape = shape((requests, col_count // 2), f32)
        keep, give = call(
            functools.partial(down_last_kernel, LAYERS - 1),
            (half_shape, half_shape),
            hidden,
            down_weight,
            name="down_last",
        )
        give = lax.ppermute(give, "tp", [(i, i ^ 1) for i in range(n_tp)])
        stream = call(
            functools.partial(meet_kernel, n_tp),
            shape((n_seq * n_tp, requests, col_count // 2), bf16),
            mid,
            keep,
            give,
            name="meet",
        )
        everyone = [whole_order(n_seq, n_tp)]
        stream = lax.all_to_all(stream, ("seq", "tp"), 0, 0, axis_index_groups=everyone)
        stream = call(
            functools.partial(last_kernel, n_tp),
            jax.ShapeDtypeStruct((requests, width), bf16),
            stream,
            name="last",
        )
        return (stream, key_out, value_out)

    return per_device


def solution(mesh):
    n_seq, n_tp = mesh.shape["seq"], mesh.shape["tp"]

    def per_device(*args):
        gate_weight, key_cache = args[7], args[10]
        aligned = (
            args[6].shape[2] % (2 * LANES) == 0
            and n_tp % 2 == 0
            and gate_weight.shape[2] // n_seq % LANES == 0
            and key_cache.shape[3] == LANES
            and args[0].shape[0] == 2 * n_seq
        )
        make = make_with_kernels if aligned else make_plain
        return make(n_seq, n_tp)(*args)

    return jax.shard_map(
        per_device,
        mesh=mesh,
        in_specs=(
            P(),
            P(),
            P(),
            P(None, "seq", "tp"),
            P(None, "seq", "tp"),
            P(None, "seq", "tp"),
            P(None, "tp", "seq"),
            P(None, "seq", "tp"),
            P(None, "seq", "tp"),
            P(None, "tp", "seq"),
            P(None, None, "seq", "tp"),
            P(None, None, "seq", "tp"),
        ),
        out_specs=(P(), P(None, None, "seq", "tp"), P(None, None, "seq", "tp")),
        check_vma=False,
    )
```
